32 devices in a mesh: head: 4 (over x, core), blk: 8 (over z, y).
Axes of the slice: x: 2, y: 2, z: 4, core: 2. Of those that a mesh axis runs over, the one named last changes fastest.
Arguments:
- inputs: bfloat16 [4096, 1024], P(('blk', 'head')), may hold values from -60 to 60
- cotangent: bfloat16 [4096, 1024], P(('blk', 'head')), may hold values from -6 to 6
- attn_gain: float32 [1024], replicated, may hold values from 0.5 to 1.5
- ffn_gain: float32 [1024], replicated, may hold values from 0.5 to 1.5
- query_gain: float32 [64], replicated, may hold values from 0.25 to 1.75
- key_gain: float32 [64], replicated, may hold values from 0.25 to 1.75
- variate_bias: float32 [2, 16], replicated, may hold values from -4 to 4
- qkv_weight: bfloat16 [1024, 3072], P(('blk', 'head')), may hold values from -0.1875 to 0.1875
- out_weight: bfloat16 [1024, 1024], P(('blk', 'head')), may hold values from -1 to 1
- expand_weight: bfloat16 [1024, 8192], P(('blk', 'head')), may hold values from -0.1875 to 0.1875
- down_weight: bfloat16 [4096, 1024], P(('blk', 'head')), may hold values from -0.09375 to 0.09375
- seq_lengths: int32 [8], replicated, may hold values from 1 to 2048, 3584 in all
- variate_ids: int32 [4096], replicated, may hold values from 0 to 3
- block_order: int32 [32], replicated, may hold values from 0 to 31, each once
Outputs:
- outputs: bfloat16 [4096, 1024], P(('blk', 'head'))
- grad_inputs: float32 [4096, 1024], P(('blk', 'head'))
- grad_qkv: float32 [1024, 3072], P(('blk', 'head'))
- grad_out: float32 [1024, 1024], P(('blk', 'head'))
- grad_expand: float32 [1024, 8192], P(('blk', 'head'))
- grad_down: float32 [4096, 1024], P(('blk', 'head'))
- grad_attn: float32 [1024], replicated
- grad_ffn: float32 [1024], replicated
- grad_query: float32 [64], replicated
- grad_key: float32 [64], replicated
- grad_bias: float32 [2, 16], replicated
- root_means: float32 [3], replicated
The draws below stay inside these ranges and needn't reach their ends.
Inputs may be any that keep to these rules, and one draw needn't show every extreme that they name: `seq_lengths`: the lengths sum to 3584; the last 512 packed positions are padding, which is one more segment. `block_order`: each block number once.
All inputs are finite; a program needn't handle non-finite values.
Results may differ from the reference program's by a relative error of at most 0.02.
Values may be sent and summed in bfloat16 or wider, within the bound.
No kernel may reach another device: no remote copies, remote signals or barrier semaphores. Data moves between devices by JAX's collectives and lax.ppermute only.
A program may use at most 192 MiB of HBM per device.

```python
import math
from functools import partial
import jax
import jax.numpy as jnp
import numpy as np
from jax import lax

D = 1024
H = 16
HD = 64
FF = 4096
BLOCK = 128
NSEQ = 8
NVAR = 4
TOKENS = 4096
PAD = 512
LONGEST = 2048
NBLK = 32


def draw_inputs(key, part):
    rows = jnp.arange(TOKENS, dtype=jnp.float32)[:, None] / TOKENS
    values = jax.random.normal(key, (TOKENS, D), jnp.float32)
    rising = 1.0 + 2.0 * rows
    return (values * rising).astype(jnp.bfloat16)


def set_ends(entries, own_key, low, high):
    longest = entries.shape.index(max(entries.shape))
    spots = []
    for shift in (0, 1):
        where = [jax.random.randint(jax.random.fold_in(own_key, axis), (), 0, length) for axis, length in enumerate(entries.shape)]
        where[longest] = (where[longest] + shift) % entries.shape[longest]
        spots.append(tuple(where))
    return entries.at[spots[0]].set(low).at[spots[1]].set(high)


def block_scale(key, extent, split, low, largest):
    factor_of = 1.0
    for axis_at, shards_of in split:
        draws = jax.random.uniform(jax.random.fold_in(jax.random.fold_in(key, 6), axis_at), (shards_of,), jnp.float32, low / len(split), largest / len(split))
        factor_of = factor_of * jnp.repeat(jnp.exp(draws), extent[axis_at] // shards_of).reshape((-1,) + (1,) * (len(extent) - 1 - axis_at))
    return factor_of


def profile(count, total, bound, lean):
    weights = [(1 << 20) // math.isqrt(rank ** lean) + 1 for rank in range(2, count + 1)]
    spare, holding = total - bound - (count - 1), [1] * (count - 1)
    while spare > 0:
        candidates = [i for i in range(count - 1) if holding[i] < bound]
        pool, remaining = sum([weights[i] for i in candidates]), spare
        for i in candidates:
            addition = min(bound - holding[i], max(1, remaining * weights[i] // pool), spare)
            holding[i] = holding[i] + addition
            spare = spare - addition
    return np.array([bound] + holding)


def ragged_sizes(rng, amount, total, most, lean):
    if amount == 2:
        one = jax.random.randint(rng, (), max(1, total - most), min(most, total - 1) + 1)
        return jnp.stack([one, total - one])
    tallies = jnp.asarray(profile(amount, total, most, lean), jnp.int32)
    couples = (amount - 1) // 2
    giver, taker = tallies[1:1 + 2 * couples:2], tallies[2:2 + 2 * couples:2]
    room = jnp.minimum(giver - 1, most - taker)
    moved = jax.random.randint(jax.random.fold_in(rng, 1), (couples,), 0, 1 << 20) % (room + 1)
    tallies = tallies.at[1:1 + 2 * couples:2].set(giver - moved).at[2:2 + 2 * couples:2].set(taker + moved)
    return tallies[jax.random.permutation(jax.random.fold_in(rng, 2), amount)]


def gaussian(key, dims, width, limit, split=(), held_as=jnp.bfloat16):
    values = jax.random.normal(key, dims, jnp.float32) * width
    if len(split) > 0:
        values = block_scale(key, dims, split, -0.22, 0.18) * values
    return jnp.clip(values, min=-limit, max=limit).astype(held_as)


def setup_inputs(seed: int = 0) -> dict:
    key_of = jax.random.split(jax.random.key(seed), 15)
    inputs = draw_inputs(jax.random.fold_in(key_of[14], 71), 0)
    cotangent = gaussian(key_of[1], (TOKENS, D), 1.0, 6.0, ((0, 32),))
    attn_gain = jnp.clip(1.0 + 0.1 * jax.random.normal(key_of[2], (D,), jnp.float32), 0.5, 1.5)
    ffn_gain = jnp.clip(1.0 + 0.1 * jax.random.normal(key_of[3], (D,), jnp.float32), 0.5, 1.5)
    query_gain = jnp.clip(1.0 + 0.15 * jax.random.normal(key_of[4], (HD,), jnp.float32), 0.25, 1.75)
    key_gain = jnp.clip(1.0 + 0.15 * jax.random.normal(key_of[5], (HD,), jnp.float32), 0.25, 1.75)
    variate_bias = gaussian(key_of[6], (2, H), 1.0, 4.0, (), jnp.float32)
    qkv_weight = gaussian(key_of[7], (D, 3 * D), D ** -0.5, 0.1875, ((0, 32),))
    out_weight = gaussian(key_of[8], (D, D), (D // 32) ** -0.5, 1.0, ((0, 32),))
    expand_weight = gaussian(key_of[9], (D, 2 * FF), D ** -0.5, 0.1875, ((0, 32),))
    down_weight = gaussian(key_of[10], (FF, D), FF ** -0.5, 0.09375, ((0, 32),))
    seq_lengths = ragged_sizes(key_of[11], NSEQ, TOKENS - PAD, LONGEST, 2).astype(jnp.int32)
    variate_ids = set_ends(jax.random.randint(key_of[12], (TOKENS,), 0, NVAR), jax.random.fold_in(key_of[12], 1), 0, NVAR - 1).astype(jnp.int32)
    block_order = jax.random.permutation(key_of[13], NBLK).astype(jnp.int32)
    return {"inputs": inputs, "cotangent": cotangent, "attn_gain": attn_gain, "ffn_gain": ffn_gain, "query_gain": query_gain, "key_gain": key_gain, "variate_bias": variate_bias, "qkv_weight": qkv_weight, "out_weight": out_weight, "expand_weight": expand_weight, "down_weight": down_weight, "seq_lengths": seq_lengths, "variate_ids": variate_ids, "block_order": block_order}


EPSILON = 1e-05
THETA = 10000.0
HIGHEST = lax.Precision.HIGHEST

@jax.custom_vjp
def low(v):
    return lax.optimization_barrier(v.astype(jnp.bfloat16)).astype(jnp.float32)

@jax.custom_vjp
def low_back(v):
    return v

def low_keep(v):
    return (low(v), None)

def low_pass(kept, grad):
    return (grad,)

def back_keep(v):
    return (v, None)

def back_low(kept, grad):
    return (low(grad),)
low.defvjp(low_keep, low_pass)
low_back.defvjp(back_keep, back_low)

def norm_rows(values, gain):
    factor = lax.rsqrt(lax.optimization_barrier(jnp.mean(values * values, axis=-1, keepdims=True)) + EPSILON)
    return values * factor * gain

def rotate(values, position):
    halfway = values.shape[-1] // 2
    freqs = THETA ** (-jnp.arange(halfway, dtype=jnp.float32) / halfway)
    angles = position.astype(jnp.float32)[:, None] * freqs[None, :]
    cosine = jnp.cos(angles)[:, None, :]
    sine = jnp.sin(angles)[:, None, :]
    first = values[..., :halfway]
    latter = values[..., halfway:]
    return jnp.concatenate([first * cosine - latter * sine, latter * cosine + first * sine], axis=-1)

def token_meta(seq_lengths, block_order):
    blocks = block_order.shape[0]
    packed_at = (jnp.repeat(block_order, BLOCK) * BLOCK + jnp.tile(jnp.arange(BLOCK, dtype=jnp.int32), blocks)).astype(jnp.int32)
    ends = jnp.cumsum(seq_lengths).astype(jnp.int32)
    after = packed_at[:, None] >= ends[None, :]
    segment = lax.optimization_barrier(jnp.sum(after.astype(jnp.int32), axis=1)).astype(jnp.int32)
    begin = lax.optimization_barrier(jnp.max(jnp.where(after, ends[None, :], jnp.zeros_like(ends)[None, :]), axis=1))
    return (segment, (packed_at - begin).astype(jnp.int32))

def attention(queries, keys, values, variate_bias, segment, variate_ids):
    rows = queries.shape[0]
    block_size = min(128, rows)

    def one_block(block_index):
        first_row = block_index * block_size
        block_rows = lax.dynamic_slice_in_dim(queries, first_row, block_size)
        block_segment = lax.dynamic_slice_in_dim(segment, first_row, block_size)
        block_variate = lax.dynamic_slice_in_dim(variate_ids, first_row, block_size)
        dots = low_back(jnp.einsum('qhd,khd->hqk', block_rows, keys, precision=HIGHEST))
        same_variate = (block_variate[:, None] == variate_ids[None, :])[None]
        scores = dots * HD ** (-0.5) + jnp.where(same_variate, variate_bias[1][:, None, None], variate_bias[0][:, None, None])
        same_segment = (block_segment[:, None] == segment[None, :])[None]
        expo = jnp.where(same_segment, jnp.exp(scores), 0.0)
        totals = lax.optimization_barrier(jnp.sum(expo, axis=2))
        accum = low_back(jnp.einsum('hqk,khd->qhd', low(expo), values, precision=HIGHEST))
        return accum / totals.T[:, :, None]
    blocks = lax.map(jax.checkpoint(one_block), jnp.arange(rows // block_size, dtype=jnp.int32))
    return blocks.reshape(rows, H, HD)

def layer(floats, segment, position, variate_ids):
    inputs, attn_gain, ffn_gain, query_gain, key_gain, variate_bias, qkv_weight, out_weight, expand_weight, down_weight = floats
    rows = inputs.shape[0]
    normed = low(norm_rows(inputs, attn_gain))
    project = low_back(jnp.dot(normed, qkv_weight, precision=HIGHEST))
    queries = rotate(norm_rows(project[:, :D].reshape(rows, H, HD), query_gain), position)
    keys = rotate(norm_rows(project[:, D:2 * D].reshape(rows, H, HD), key_gain), position)
    queries = low_back(low(queries))
    keys = low_back(low(keys))
    values = low_back(low(project[:, 2 * D:].reshape(rows, H, HD)))
    attended = attention(queries, keys, values, variate_bias, segment, variate_ids)
    attended = low_back(low(attended.reshape(rows, D)))
    attn_branch = low_back(jnp.dot(attended, out_weight, precision=HIGHEST))
    middle = inputs + attn_branch
    second = low(norm_rows(middle, ffn_gain))
    expand = low_back(jnp.dot(second, expand_weight, precision=HIGHEST))
    hidden = low(jax.nn.silu(expand[:, :FF]) * expand[:, FF:])
    ffn_branch = low_back(jnp.dot(hidden, down_weight, precision=HIGHEST))
    return (middle + ffn_branch, (attn_branch, ffn_branch))

def reference(inputs, cotangent, attn_gain, ffn_gain, query_gain, key_gain, variate_bias, qkv_weight, out_weight, expand_weight, down_weight, seq_lengths, variate_ids, block_order):
    segment, position = token_meta(seq_lengths, block_order)
    floats = (inputs.astype(jnp.float32), attn_gain, ffn_gain, query_gain, key_gain, variate_bias, qkv_weight.astype(jnp.float32), out_weight.astype(jnp.float32), expand_weight.astype(jnp.float32), down_weight.astype(jnp.float32))
    result, pullback, branches = jax.vjp(partial(layer, segment=segment, position=position, variate_ids=variate_ids), floats, has_aux=True)
    grads = pullback(cotangent.astype(jnp.float32))[0]
    squares = jnp.stack([jnp.mean(floats[0] * floats[0]), jnp.mean(branches[0] * branches[0]), jnp.mean(branches[1] * branches[1])])
    return (result.astype(jnp.bfloat16), grads[0], grads[6], grads[7], grads[8], grads[9], grads[1], grads[2], grads[3], grads[4], grads[5], jnp.sqrt(squares))
```

```python
from functools import partial

import jax
import jax.numpy as jnp
from jax import lax
from jax.experimental import pallas as pl
from jax.experimental.pallas import tpu as pltpu
from jax.sharding import Mesh
from jax.sharding import PartitionSpec as P

D = 1024
H = 16
HD = 64
BLOCK = 128
NVAR = 4
EPSILON = 1e-05
THETA = 10000.0

DEVICES = ("bz", "by", "hx", "core")
CHIPS = ("bz", "by", "hx")
PLANE = ("by", "hx", "core")

SEGMENT_LANE = 64
VARIATE_LANE = 76
MASK = -512.0
QUERY_TILE = 256
KEY_TILE = 256

bf16 = jnp.bfloat16
f32 = jnp.float32


def dot(left, right, dims):
    return lax.dot_general(left, right, (dims, ((), ())), preferred_element_type=f32)


def norm_rows(values, gain):
    factor = lax.rsqrt(jnp.mean(values * values, axis=-1, keepdims=True) + EPSILON)
    return values * factor * gain


def norm_back(values, gain, grad):
    factor = lax.rsqrt(jnp.mean(values * values, axis=-1, keepdims=True) + EPSILON)
    scaled = grad * gain
    inner = jnp.mean(scaled * values, axis=-1, keepdims=True)
    grad_values = factor * (scaled - values * (factor * factor) * inner)
    return grad_values, grad * values * factor


def swiglu(expand):
    half = expand.shape[1] // 2
    return jax.nn.silu(expand[:, :half]) * expand[:, half:]


def swap(shard, axis):
    return lax.ppermute(shard, axis, [(0, 1), (1, 0)])


def plane_gather(shard):
    half = shard.shape[0] // 2
    across_x = swap(shard, "hx")
    across_y = swap(shard, "by")
    corner_a = swap(across_y[:half], "hx")
    corner_b = swap(across_x[half:], "by")
    mine = jnp.concatenate([shard, across_x, across_y, corner_a, corner_b], axis=0)
    return jnp.concatenate([mine, swap(mine, "core")], axis=0)


def plane_scatter(partial_low):
    rows = partial_low.shape[0] // 8
    half = rows // 2
    other = swap(partial_low[4 * rows :], "core")
    mine = partial_low[: 4 * rows].astype(f32) + other.astype(f32)
    corner = mine[3 * rows :].astype(bf16)
    for_y = swap(corner[:half], "hx").astype(f32)
    for_x = swap(corner[half:], "by").astype(f32)
    to_x = mine[rows : 2 * rows]
    to_y = mine[2 * rows : 3 * rows]
    to_x = jnp.concatenate([to_x[:half], to_x[half:] + for_x], axis=0).astype(bf16)
    to_y = jnp.concatenate([to_y[:half] + for_y, to_y[half:]], axis=0).astype(bf16)
    from_x = swap(to_x, "hx")
    from_y = swap(to_y, "by")
    return mine[:rows] + from_x.astype(f32) + from_y.astype(f32)


def plane_members():
    by, hx, core = lax.axis_index("by"), lax.axis_index("hx"), lax.axis_index("core")
    members = []
    for core_flip in (0, 1):
        for x_flip, y_flip in ((0, 0), (1, 0), (0, 1), (1, 1)):
            members.append((by ^ y_flip) * 4 + (hx ^ x_flip) * 2 + (core ^ core_flip))
    return members


def lanes(shape):
    return lax.broadcasted_iota(jnp.int32, shape, len(shape) - 1)


def half_mean(values, lane):
    low = jnp.sum(jnp.where(lane < HD, values, 0.0), axis=-1, keepdims=True)
    high = jnp.sum(jnp.where(lane < HD, 0.0, values), axis=-1, keepdims=True)
    return jnp.where(lane < HD, low, high) * (1.0 / HD)


def swap_halves(values, lane):
    return jnp.where(
        (lane & (HD - 1)) < HD // 2, pltpu.roll(values, 96, 1), pltpu.roll(values, 32, 1)
    )


def project_kernel(
    core_ref,
    x_ref,
    gain_ref,
    weight_ref,
    cosine_ref,
    sine_ref,
    gains_ref,
    hot_ref,
    normed_ref,
    raw_ref,
    query_ref,
    kv_ref,
):
    x = x_ref[0, 0].astype(f32)
    normed = norm_rows(x, gain_ref[...]).astype(bf16)
    normed_ref[...] = normed
    project = dot(normed, weight_ref[...], ((1,), (0,)))
    both = project[:, : 2 * HD]
    value = project[:, 2 * HD :]
    raw_ref[...] = both
    lane = lanes(both.shape)
    scaled = both * lax.rsqrt(half_mean(both * both, lane) + EPSILON) * gains_ref[...]
    turned = scaled * cosine_ref[...] + swap_halves(scaled, lane) * sine_ref[...]
    turned = turned.astype(bf16).astype(f32)
    query_ref[...] = jnp.where(lane < HD, turned, hot_ref[...].astype(f32)).astype(bf16)
    kv_ref[...] = jnp.where(lane < HD, value, turned * HD ** (-0.5)).astype(bf16)


def project(core, gathered, gain, weight, cosine, sine, gains, hot):
    blocks = gathered.shape[0]
    rows = blocks * BLOCK
    row_spec = lambda width: pl.BlockSpec((BLOCK, width), lambda j, core: (j, 0))
    whole = lambda array: pl.BlockSpec(array.shape, lambda j, core: (0, 0))
    return pl.pallas_call(
        project_kernel,
        grid_spec=pltpu.PrefetchScalarGridSpec(
            num_scalar_prefetch=1,
            grid=(blocks,),
            in_specs=[
                pl.BlockSpec((1, 1, BLOCK, D), lambda j, core: (j, core[0], 0, 0)),
                whole(gain),
                whole(weight),
                row_spec(128),
                row_spec(128),
                whole(gains),
                row_spec(128),
            ],
            out_specs=[row_spec(D), row_spec(128), row_spec(128), row_spec(128)],
        ),
        out_shape=[
            jax.ShapeDtypeStruct((rows, D), bf16),
            jax.ShapeDtypeStruct((rows, 128), f32),
            jax.ShapeDtypeStruct((rows, 128), bf16),
            jax.ShapeDtypeStruct((rows, 128), bf16),
        ],
        name="project",
    )(core, gathered, gain, weight, cosine, sine, gains, hot)


def sort_keys(place_ref, own_ref, other_ref, mask_ref, key_ref, value_ref):
    blocks = own_ref.shape[0] // BLOCK
    lane = lanes((BLOCK, 128))
    ones = jnp.where((lane >= HD) & (lane < HD + 3), 1.0, 0.0)
    for half, source_ref in ((0, own_ref), (1, other_ref)):

        def put(j, unused, half=half, source_ref=source_ref):
            source = pl.multiple_of(j * BLOCK, BLOCK)
            tail = pl.multiple_of((half * blocks + j) * BLOCK, BLOCK)
            target = pl.multiple_of(place_ref[half * blocks + j] * BLOCK, BLOCK)
            both = source_ref[pl.ds(source, BLOCK), :].astype(f32)
            mask = mask_ref[pl.ds(tail, BLOCK), :].astype(f32)
            key_ref[pl.ds(target, BLOCK), :] = jnp.where(
                lane < HD, pltpu.roll(both, HD, 1), mask
            ).astype(bf16)
            value_ref[pl.ds(target, BLOCK), :] = jnp.where(lane < HD, both, ones).astype(bf16)
            return unused

        lax.fori_loop(0, blocks, put, 0)


def tile_rows(order_ref, tile):
    count = QUERY_TILE // BLOCK
    return [pl.multiple_of(order_ref[tile * count + i] * BLOCK, BLOCK) for i in range(count)]


def load_rows(ref, starts):
    return jnp.concatenate([ref[pl.ds(start, BLOCK), :] for start in starts], axis=0)


def attend_kernel(
    order_ref,
    place_ref,
    low_ref,
    high_ref,
    query_ref,
    own_ref,
    other_ref,
    mask_ref,
    kept_ref,
    attended_ref,
    key_ref,
    value_ref,
):
    tile = pl.program_id(0)

    @pl.when(tile == 0)
    def _():
        sort_keys(place_ref, own_ref, other_ref, mask_ref, key_ref, value_ref)
        kept_ref[...] = jnp.zeros_like(kept_ref)
        attended_ref[...] = jnp.zeros_like(attended_ref)

    starts = tile_rows(order_ref, tile)
    query = load_rows(query_ref, starts)

    def chunk(index, accumulated):
        first = pl.multiple_of(index * KEY_TILE, KEY_TILE)
        key = key_ref[pl.ds(first, KEY_TILE), :]
        value = value_ref[pl.ds(first, KEY_TILE), :]
        expo = jnp.exp(dot(query, key, ((1,), (1,))))
        return accumulated + dot(expo.astype(bf16), value, ((1,), (0,)))

    accumulated = lax.fori_loop(
        low_ref[tile], high_ref[tile], chunk, jnp.zeros((QUERY_TILE, 128), f32)
    )
    totals = accumulated[:, HD : HD + 1]
    lane = lanes(accumulated.shape)
    kept = jnp.where(lane < HD, accumulated / totals, totals)
    for i, start in enumerate(starts):
        piece = kept[i * BLOCK : (i + 1) * BLOCK]
        kept_ref[pl.ds(start, BLOCK), :] = piece
        attended_ref[pl.ds(start, BLOCK), :] = piece[:, :HD].astype(bf16)


def fixed(array, prefetched):
    return pl.BlockSpec(
        array.shape, lambda *unused: (0,) * len(array.shape), pipeline_mode=pl.Buffered(1)
    )


def attend(order, place, low, high, query, own, other, mask):
    rows = query.shape[0]
    operands = (query, own, other, mask)
    outs = (jax.ShapeDtypeStruct((rows, 128), f32), jax.ShapeDtypeStruct((rows, HD), bf16))
    return pl.pallas_call(
        attend_kernel,
        grid_spec=pltpu.PrefetchScalarGridSpec(
            num_scalar_prefetch=4,
            grid=(low.shape[0],),
            in_specs=[fixed(array, 4) for array in operands],
            out_specs=[fixed(array, 4) for array in outs],
            scratch_shapes=[pltpu.VMEM((2 * rows, 128), bf16), pltpu.VMEM((2 * rows, 128), bf16)],
        ),
        out_shape=list(outs),
        name="attend",
    )(order, place, low, high, *operands)


def attend_back_kernel(
    order_ref,
    place_ref,
    low_ref,
    high_ref,
    query_ref,
    own_ref,
    other_ref,
    mask_ref,
    hot_ref,
    kept_ref,
    grad_ref,
    query_grad_ref,
    own_grad_ref,
    other_grad_ref,
    bias_ref,
    key_ref,
    value_ref,
    key_grad_ref,
    value_grad_ref,
):
    tile = pl.program_id(0)

    @pl.when(tile == 0)
    def _():
        sort_keys(place_ref, own_ref, other_ref, mask_ref, key_ref, value_ref)
        query_grad_ref[...] = jnp.zeros_like(query_grad_ref)
        key_grad_ref[...] = jnp.zeros_like(key_grad_ref)
        value_grad_ref[...] = jnp.zeros_like(value_grad_ref)

    starts = tile_rows(order_ref, tile)
    query = load_rows(query_ref, starts)
    kept = load_rows(kept_ref, starts)
    grad = load_rows(grad_ref, starts).astype(f32)
    grad = jnp.concatenate([grad, jnp.zeros_like(grad)], axis=1)
    lane = lanes(kept.shape)
    totals = kept[:, HD : HD + 1]
    center = jnp.sum(jnp.where(lane < HD, grad * kept, 0.0), axis=1, keepdims=True) / totals
    center_high = center.astype(bf16).astype(f32)
    center_rest = center - center_high
    center_mid = center_rest.astype(bf16).astype(f32)
    center_low = center_rest - center_mid
    wide = jnp.where(lane == HD, -center_high, 0.0)
    wide = jnp.where(lane == HD + 1, -center_mid, wide)
    wide = jnp.where(lane == HD + 2, -center_low, wide)
    wide = jnp.where(lane < HD, grad / totals, wide).astype(bf16)

    def chunk(index, query_grad):
        first = pl.multiple_of(index * KEY_TILE, KEY_TILE)
        window = pl.ds(first, KEY_TILE)
        key = key_ref[window, :]
        value = value_ref[window, :]
        expo = jnp.exp(dot(key, query, ((1,), (1,))))
        score_grad = expo * dot(value, wide, ((1,), (1,)))
        score_low = score_grad.astype(bf16)
        value_grad_ref[window, :] += dot(expo.astype(bf16), wide, ((1,), (0,)))
        key_grad_ref[window, :] += dot(score_low, query, ((1,), (0,)))
        return query_grad + dot(score_low, key, ((0,), (0,)))

    query_grad = lax.fori_loop(
        low_ref[tile], high_ref[tile], chunk, jnp.zeros((QUERY_TILE, 128), f32)
    )
    for i, start in enumerate(starts):
        query_grad_ref[pl.ds(start, BLOCK), :] = query_grad[i * BLOCK : (i + 1) * BLOCK]

    @pl.when(tile == pl.num_programs(0) - 1)
    def _():
        blocks = own_ref.shape[0] // BLOCK
        block_lane = lanes((BLOCK, 128))
        variate = (block_lane >= VARIATE_LANE) & (block_lane < VARIATE_LANE + NVAR)
        sums = (jnp.zeros((BLOCK, 128), f32), jnp.zeros((BLOCK, 128), f32))
        for half, target_ref in ((0, own_grad_ref), (1, other_grad_ref)):

            def take(j, sums, half=half, target_ref=target_ref):
                target = pl.multiple_of(j * BLOCK, BLOCK)
                tail = pl.multiple_of((half * blocks + j) * BLOCK, BLOCK)
                source = pl.multiple_of(place_ref[half * blocks + j] * BLOCK, BLOCK)
                key_grad = key_grad_ref[pl.ds(source, BLOCK), :]
                value_grad = value_grad_ref[pl.ds(source, BLOCK), :]
                target_ref[pl.ds(target, BLOCK), :] = jnp.where(
                    block_lane < HD, value_grad, pltpu.roll(key_grad, HD, 1) * HD ** (-0.5)
                )
                every = jnp.where(variate, key_grad, 0.0)
                hot = hot_ref[pl.ds(tail, BLOCK), :].astype(f32)
                return (sums[0] + every, sums[1] + every * hot)

            sums = lax.fori_loop(0, blocks, take, sums)
        every = jnp.sum(sums[0], keepdims=True)
        same = jnp.sum(sums[1], keepdims=True)
        bias_lane = lanes((8, 128))
        bias_ref[...] = jnp.where(bias_lane == 0, every - same, jnp.where(bias_lane == 1, same, 0.0))


def attend_back(order, place, low, high, query, own, other, mask, hot, kept, grad):
    rows = query.shape[0]
    operands = (query, own, other, mask, hot, kept, grad)
    outs = tuple(jax.ShapeDtypeStruct((rows, 128), f32) for unused in range(3)) + (
        jax.ShapeDtypeStruct((8, 128), f32),
    )
    return pl.pallas_call(
        attend_back_kernel,
        grid_spec=pltpu.PrefetchScalarGridSpec(
            num_scalar_prefetch=4,
            grid=(low.shape[0],),
            in_specs=[fixed(array, 4) for array in operands],
            out_specs=[fixed(array, 4) for array in outs],
            scratch_shapes=[
                pltpu.VMEM((2 * rows, 128), bf16),
                pltpu.VMEM((2 * rows, 128), bf16),
                pltpu.VMEM((2 * rows, 128), f32),
                pltpu.VMEM((2 * rows, 128), f32),
            ],
        ),
        out_shape=list(outs),
        name="attend_back",
    )(order, place, low, high, *operands)


def project_back_kernel(
    query_grad_ref,
    own_ref,
    other_ref,
    raw_ref,
    cosine_ref,
    sine_ref,
    gains_ref,
    normed_ref,
    grad_ref,
    weight_grad_ref,
    gain_grad_ref,
    weight_ref,
    gain_ref,
):
    step = pl.program_id(0)

    @pl.when(step == 0)
    def _():
        weight_ref[...] = jnp.zeros_like(weight_ref)
        gain_ref[...] = jnp.zeros_like(gain_ref)

    kv_grad = (own_ref[...] + other_ref[...]).astype(bf16).astype(f32)
    lane = lanes(kv_grad.shape)
    turned = jnp.where(lane < HD, query_grad_ref[...].astype(bf16).astype(f32), kv_grad)
    grad = turned * cosine_ref[...] - swap_halves(turned, lane) * sine_ref[...]
    raw = raw_ref[...]
    factor = lax.rsqrt(half_mean(raw * raw, lane) + EPSILON)
    scaled = grad * gains_ref[...]
    inner = half_mean(scaled * raw, lane)
    both = (factor * (scaled - raw * (factor * factor) * inner)).astype(bf16)
    gain_ref[...] += jnp.sum(grad * raw * factor, axis=0, keepdims=True)
    value = jnp.where(lane < HD, kv_grad, 0.0).astype(bf16)
    full = jnp.concatenate([both, value], axis=1)
    grad_ref[...] = full[:, : 3 * HD]
    weight_ref[...] += dot(normed_ref[...], full, ((0,), (0,)))

    @pl.when(step == pl.num_programs(0) - 1)
    def _():
        weight_grad_ref[...] = weight_ref[:, : 3 * HD].astype(bf16)
        gain_grad_ref[...] = jnp.broadcast_to(gain_ref[...], gain_grad_ref.shape)


def project_back(query_grad, own, other, raw, cosine, sine, gains, normed):
    rows = query_grad.shape[0]
    step_rows = 2 * BLOCK
    row_spec = lambda width: pl.BlockSpec((step_rows, width), lambda j: (j, 0))
    whole = lambda shape: pl.BlockSpec(shape, lambda j: (0, 0))
    return pl.pallas_call(
        project_back_kernel,
        grid=(rows // step_rows,),
        in_specs=[row_spec(128)] * 6 + [whole(gains.shape), row_spec(D)],
        out_specs=[row_spec(3 * HD), whole((D, 3 * HD)), whole((8, 128))],
        out_shape=[
            jax.ShapeDtypeStruct((rows, 3 * HD), bf16),
            jax.ShapeDtypeStruct((D, 3 * HD), bf16),
            jax.ShapeDtypeStruct((8, 128), f32),
        ],
        scratch_shapes=[pltpu.VMEM((D, 4 * HD), f32), pltpu.VMEM((1, 128), f32)],
        name="project_back",
    )(query_grad, own, other, raw, cosine, sine, gains, normed)


def token_meta(seq_lengths, block_order):
    blocks = block_order.shape[0]
    packed_at = jnp.repeat(block_order, BLOCK) * BLOCK + jnp.tile(
        jnp.arange(BLOCK, dtype=jnp.int32), blocks
    )
    ends = jnp.cumsum(seq_lengths)
    after = packed_at[:, None] >= ends[None, :]
    segment = jnp.sum(after.astype(jnp.int32), axis=1)
    begin = jnp.max(jnp.where(after, ends[None, :], jnp.zeros_like(ends)[None, :]), axis=1)
    return (segment, packed_at - begin, ends)


def both_cores(array, core):
    pairs = array.reshape((-1, 2, BLOCK) + array.shape[1:])
    shape = (-1,) + array.shape[1:]
    own = lax.dynamic_index_in_dim(pairs, core, 1, keepdims=False).reshape(shape)
    other = lax.dynamic_index_in_dim(pairs, 1 - core, 1, keepdims=False).reshape(shape)
    return own, other


def one_hot_rows(segment, variate, segments):
    lane = jnp.arange(128, dtype=jnp.int32)[None, :]
    hot = lane == SEGMENT_LANE + segment[:, None]
    for copy in range(3):
        hot = hot | (lane == VARIATE_LANE + copy * NVAR + variate[:, None])
    return hot.astype(bf16)


def mask_rows(segment, variate, segments, bias):
    lane = jnp.arange(128, dtype=jnp.int32)[None, :]
    here = lane - SEGMENT_LANE
    rows = jnp.where(
        (here >= 0) & (here < segments) & (here != segment[:, None]), jnp.float32(MASK), 0.0
    )
    high = lax.reduce_precision(bias, 8, 7)
    mid = lax.reduce_precision(bias - high, 8, 7)
    low = bias - high - mid
    for copy, part in enumerate((high, mid, low)):
        here = lane - VARIATE_LANE - copy * NVAR
        value = jnp.where(here == variate[:, None], part[1], part[0])
        rows = jnp.where((here >= 0) & (here < NVAR), value, rows)
    return rows.astype(bf16)


def sum_everywhere(vector, devices):
    copies = jnp.broadcast_to(vector[None], (devices,) + vector.shape)
    return jnp.sum(lax.all_to_all(copies, DEVICES, 0, 0, tiled=True), axis=0)


def body(
    inputs,
    cotangent,
    attn_gain,
    ffn_gain,
    query_gain,
    key_gain,
    variate_bias,
    qkv_weight,
    out_weight,
    expand_weight,
    down_weight,
    seq_lengths,
    variate_ids,
    block_order,
):
    depth = lax.axis_size("bz")
    chips = depth * 4
    devices = chips * 2
    sharers = chips // H
    core = lax.axis_index("core")
    chip = (lax.axis_index("bz") * 2 + lax.axis_index("by")) * 2 + lax.axis_index("hx")
    head = chip // sharers
    share = chip % sharers
    rows = qkv_weight.shape[0]
    hidden_rows = down_weight.shape[0]
    segments = seq_lengths.shape[0] + 1
    tokens = variate_ids.shape[0]

    gathered = lax.all_gather(
        jnp.concatenate([inputs, out_weight], axis=0), DEVICES, axis=0, tiled=True
    ).reshape(chips, 2, BLOCK + rows, D)

    by_head = qkv_weight.reshape(rows, 3, H, HD)
    to_heads = jnp.repeat(
        by_head.transpose(2, 0, 1, 3).reshape(H, rows, 3 * HD), 2 * sharers, axis=0
    )
    own_qkv = lax.all_to_all(to_heads, DEVICES, 0, 0, tiled=True).reshape(D, 3 * HD)
    own_qkv = jnp.pad(own_qkv, ((0, 0), (0, HD)))
    to_plane = (
        expand_weight.reshape(rows, 2, depth, 8, hidden_rows)
        .transpose(3, 0, 1, 2, 4)
        .reshape(8, rows, 2 * depth * hidden_rows)
    )
    expand_part = lax.all_to_all(to_plane, PLANE, 0, 0, tiled=True).reshape(8 * rows, -1)
    cotangent_plane = plane_gather(cotangent)

    segment, position, ends = token_meta(seq_lengths, block_order)
    own_segment, other_segment = both_cores(segment, core)
    own_variate, other_variate = both_cores(variate_ids, core)
    own_position = both_cores(position, core)[0]
    all_segment = jnp.concatenate([own_segment, other_segment])
    all_variate = jnp.concatenate([own_variate, other_variate])
    bias = lax.dynamic_index_in_dim(variate_bias, head, 1, keepdims=False)
    hot = one_hot_rows(all_segment, all_variate, segments)
    mask = mask_rows(all_segment, all_variate, segments, bias)
    freqs = THETA ** (-jnp.arange(HD // 2, dtype=f32) / (HD // 2))
    angles = own_position.astype(f32)[:, None] * freqs[None, :]
    cosine = jnp.tile(jnp.cos(angles), (1, 4))
    sine = jnp.sin(angles)
    sine = jnp.tile(jnp.concatenate([-sine, sine], axis=1), (1, 2))
    pairs = block_order.reshape(chips, 2)
    own_place = lax.dynamic_index_in_dim(pairs, core, 1, keepdims=False)
    other_place = lax.dynamic_index_in_dim(pairs, 1 - core, 1, keepdims=False)
    place = jnp.concatenate([own_place, other_place])
    rank = jnp.sum((own_place[None, :] < own_place[:, None]).astype(jnp.int32), axis=1)
    taken = chips // sharers
    wanted = share * taken + jnp.arange(taken, dtype=jnp.int32)
    chosen = (rank[None, :] == wanted[:, None]).astype(jnp.int32)
    order = jnp.sum(chosen * jnp.arange(chips, dtype=jnp.int32)[None, :], axis=1)
    sorted_place = jnp.sum(chosen * own_place[None, :], axis=1).reshape(-1, QUERY_TILE // BLOCK)
    first_token = sorted_place[:, 0] * BLOCK
    last_token = sorted_place[:, -1] * BLOCK + BLOCK - 1
    begins = jnp.max(jnp.where(ends[None, :] <= first_token[:, None], ends[None, :], 0), axis=1)
    finish = jnp.min(jnp.where(ends[None, :] > last_token[:, None], ends[None, :], tokens), axis=1)
    low = begins // KEY_TILE
    high = (finish + KEY_TILE - 1) // KEY_TILE
    gains = jnp.concatenate([query_gain, key_gain])[None, :]

    gathered, expand_part, down_part = lax.optimization_barrier(
        (gathered, expand_part, down_weight)
    )
    expand_own = lax.all_gather(expand_part, "bz", axis=0, tiled=True)
    down_own = lax.all_gather(down_part, "bz", axis=0, tiled=True)
    out_full = gathered[:, :, BLOCK:, :].reshape(D, D)

    normed_low, raw, query, own_kv = project(
        core[None], gathered, attn_gain[None], own_qkv, cosine, sine, gains, hot
    )
    other_kv = swap(own_kv, "core")
    kept, attended = attend(order, place, low, high, query, own_kv, other_kv, mask)
    merged = lax.all_to_all(attended.reshape(chips, BLOCK, HD), CHIPS, 0, 0, tiled=True)
    merged = merged.reshape(H, sharers, BLOCK, HD)
    merged = merged[:, 0] if sharers == 1 else jnp.sum(merged, axis=1)
    merged = merged.transpose(1, 0, 2).reshape(BLOCK, D)

    residual = inputs.astype(f32)
    attn_branch = jnp.dot(merged, out_full, preferred_element_type=f32)
    middle = residual + attn_branch
    second_low = plane_gather(norm_rows(middle, ffn_gain).astype(bf16))

    expand = jnp.dot(second_low, expand_own, preferred_element_type=f32)
    hidden, swiglu_back = jax.vjp(swiglu, expand)
    hidden_low = hidden.astype(bf16)
    ffn_part = jnp.dot(hidden_low, down_own, preferred_element_type=f32).astype(bf16)
    grad_hidden = dot(cotangent_plane, down_own, ((1,), (1,)))
    grad_down_part = dot(hidden_low, cotangent_plane, ((0,), (0,))).astype(bf16)
    grad_expand_rows = swiglu_back(grad_hidden)[0].astype(bf16)
    grad_second_part = dot(grad_expand_rows, expand_own, ((1,), (1,))).astype(bf16)
    grad_expand_part = dot(second_low, grad_expand_rows, ((0,), (0,))).astype(bf16)
    grad_second = plane_scatter(grad_second_part)
    grad_middle, grad_ffn_rows = norm_back(middle, ffn_gain, grad_second)
    grad_middle = cotangent.astype(f32) + grad_middle
    branch_grad = grad_middle.astype(bf16)
    grad_merged = dot(branch_grad, out_full, ((1,), (1,))).astype(bf16)
    to_chips = jnp.repeat(grad_merged.reshape(BLOCK, H, HD).transpose(1, 0, 2), sharers, axis=0)
    grad_attended = lax.all_to_all(to_chips, CHIPS, 0, 0, tiled=True).reshape(-1, HD)

    ffn_branch = plane_scatter(ffn_part)
    outputs = (middle + ffn_branch).astype(bf16)
    grad_down = lax.psum_scatter(grad_down_part, "bz", scatter_dimension=0, tiled=True)
    grad_expand = lax.psum_scatter(grad_expand_part, "bz", scatter_dimension=0, tiled=True)
    grad_expand = (
        lax.all_to_all(grad_expand.reshape(8, rows, -1), PLANE, 0, 0, tiled=True)
        .reshape(8, rows, 2, depth, hidden_rows)
        .transpose(1, 2, 3, 0, 4)
        .reshape(rows, -1)
        .astype(f32)
    )

    grad_out_full = dot(merged, branch_grad, ((0,), (0,))).astype(bf16)
    grad_out_rows = grad_out_full.reshape(depth, 8, rows, D)
    grad_out_rows = jnp.concatenate(
        [
            lax.dynamic_index_in_dim(grad_out_rows, member, 1, keepdims=False).reshape(-1, D)
            for member in plane_members()
        ],
        axis=0,
    )
    grad_out_part = plane_scatter(grad_out_rows).astype(bf16)
    grad_out = lax.psum_scatter(grad_out_part, "bz", scatter_dimension=0, tiled=True).astype(f32)

    query_grad, own_grad, other_grad, bias_grad = attend_back(
        order, place, low, high, query, own_kv, other_kv, mask, hot, kept, grad_attended
    )
    grad_project, grad_qkv_part, gain_grad = project_back(
        query_grad, own_grad, swap(other_grad, "core"), raw, cosine, sine, gains, normed_low
    )
    grad_qkv = lax.all_to_all(
        grad_qkv_part.reshape(devices, rows, 3 * HD), DEVICES, 0, 0, tiled=True
    )
    grad_qkv = jnp.sum(grad_qkv.reshape(H, 2 * sharers, rows, 3, HD).astype(f32), axis=1)
    grad_qkv = grad_qkv.transpose(1, 2, 0, 3).reshape(rows, 3 * D)
    qkv_full = lax.all_gather(
        by_head.transpose(0, 2, 1, 3).reshape(rows, 3 * D), DEVICES, axis=0, tiled=True
    )
    grad_rows = lax.all_to_all(
        grad_project.reshape(chips, BLOCK, 3 * HD), CHIPS, 0, 0, tiled=True
    ).reshape(H, sharers, BLOCK, 3 * HD)
    if sharers == 1:
        grad_rows = grad_rows[:, 0]
    else:
        grad_rows = jnp.sum(grad_rows.astype(f32), axis=1).astype(bf16)
    grad_rows = grad_rows.transpose(1, 0, 2).reshape(BLOCK, 3 * D)
    grad_normed = dot(grad_rows, qkv_full, ((1,), (1,)))
    grad_first, grad_attn_rows = norm_back(residual, attn_gain, grad_normed)
    grad_inputs = grad_middle + grad_first

    bias_part = jnp.where(
        jnp.arange(H)[None, :] == head, bias_grad[0, :2][:, None], jnp.zeros((2, H), f32)
    )
    squares = jnp.stack(
        [
            jnp.sum(residual * residual),
            jnp.sum(attn_branch * attn_branch),
            jnp.sum(ffn_branch * ffn_branch),
        ]
    )
    packed = jnp.concatenate(
        [
            jnp.sum(grad_attn_rows, axis=0),
            jnp.sum(grad_ffn_rows, axis=0),
            gain_grad[0],
            bias_part.reshape(-1),
            squares,
            jnp.zeros((93,), f32),
        ]
    )
    summed = sum_everywhere(packed, devices)
    at = 2 * D + 2 * HD
    root_means = jnp.sqrt(summed[at + 2 * H : at + 2 * H + 3] / (tokens * D))
    return (
        outputs,
        grad_inputs,
        grad_qkv,
        grad_out,
        grad_expand,
        grad_down.astype(f32),
        summed[:D],
        summed[D : 2 * D],
        summed[2 * D : 2 * D + HD],
        summed[2 * D + HD : at],
        summed[at : at + 2 * H].reshape(2, H),
        root_means,
    )


def solution(mesh):
    grid = mesh.devices if mesh.axis_names == ("head", "blk") else mesh.devices.T
    heads, blks = grid.shape
    mesh = Mesh(grid.reshape(heads // 2, 2, blks // 2, 2), ("hx", "core", "bz", "by"))
    split = P(DEVICES, None)
    return jax.shard_map(
        body,
        mesh=mesh,
        in_specs=(split,) * 2 + (P(),) * 5 + (split,) * 4 + (P(),) * 3,
        out_specs=(split,) * 6 + (P(),) * 6,
        check_vma=False,
    )
```

```python
from functools import partial

import jax
import jax.numpy as jnp
from jax import lax
from jax.experimental import pallas as pl
from jax.experimental.pallas import tpu as pltpu
from jax.sharding import Mesh
from jax.sharding import PartitionSpec as P

D = 1024
H = 16
HD = 64
BLOCK = 128
NVAR = 4
EPSILON = 1e-05
THETA = 10000.0

DEVICES = ("bz", "by", "hx", "core")
CHIPS = ("bz", "by", "hx")
PLANE = ("by", "hx", "core")

SEGMENT_LANE = 64
VARIATE_LANE = 76
MASK = -512.0
QUERY_TILE = 256
KEY_TILE = 256

bf16 = jnp.bfloat16
f32 = jnp.float32


def dot(left, right, dims):
    return lax.dot_general(left, right, (dims, ((), ())), preferred_element_type=f32)


def norm_rows(values, gain):
    factor = lax.rsqrt(jnp.mean(values * values, axis=-1, keepdims=True) + EPSILON)
    return values * factor * gain


def norm_back(values, gain, grad):
    factor = lax.rsqrt(jnp.mean(values * values, axis=-1, keepdims=True) + EPSILON)
    scaled = grad * gain
    inner = jnp.mean(scaled * values, axis=-1, keepdims=True)
    grad_values = factor * (scaled - values * (factor * factor) * inner)
    return grad_values, grad * values * factor


def swap(shard, axis):
    return lax.ppermute(shard, axis, [(0, 1), (1, 0)])


def plane_gather(shard):
    mine = jnp.concatenate(quarters(shard), axis=0)
    return mine, swap(mine, "core")


def chip_gather(shard):
    depth = lax.axis_size("bz")
    chips = depth * 4
    z, y, x = lax.axis_index("bz"), lax.axis_index("by"), lax.axis_index("hx")
    at = jnp.arange(chips, dtype=jnp.int32)
    if depth > 4:
        return lax.all_gather(shard, CHIPS, axis=0, tiled=True).reshape(chips, BLOCK, D), at
    shifted = [
        lax.ppermute(shard, "bz", [(i, (i + by) % depth) for i in range(depth)])
        for by in range(1, depth)
    ]
    pieces = quarters(shard) + quarters(jnp.concatenate(shifted, axis=0))
    back = (z - at // 4) % depth
    flips = ((at % 2) ^ x) + 2 * (((at // 2) % 2) ^ y)
    where = jnp.where(back == 0, flips, 4 + flips * (depth - 1) + back - 1)
    return jnp.concatenate(pieces, axis=0).reshape(chips, BLOCK, D), where.astype(jnp.int32)


def quarters(shard):
    half = shard.shape[0] // 2
    across_x = swap(shard, "hx")
    across_y = swap(shard, "by")
    return [shard, across_x, across_y, swap(across_y[:half], "hx"), swap(across_x[half:], "by")]


def plane_scatter(mine, other):
    rows = mine.shape[0] // 4
    half = rows // 2
    mine = mine.astype(f32) + swap(other, "core").astype(f32)
    corner = mine[3 * rows :].astype(bf16)
    for_y = swap(corner[:half], "hx").astype(f32)
    for_x = swap(corner[half:], "by").astype(f32)
    to_x = mine[rows : 2 * rows]
    to_y = mine[2 * rows : 3 * rows]
    to_x = jnp.concatenate([to_x[:half], to_x[half:] + for_x], axis=0).astype(bf16)
    to_y = jnp.concatenate([to_y[:half] + for_y, to_y[half:]], axis=0).astype(bf16)
    from_x = swap(to_x, "hx")
    from_y = swap(to_y, "by")
    return mine[:rows] + from_x.astype(f32) + from_y.astype(f32)


def plane_members():
    by, hx, core = lax.axis_index("by"), lax.axis_index("hx"), lax.axis_index("core")
    members = []
    for core_flip in (0, 1):
        for x_flip, y_flip in ((0, 0), (1, 0), (0, 1), (1, 1)):
            members.append((by ^ y_flip) * 4 + (hx ^ x_flip) * 2 + (core ^ core_flip))
    return members


def lanes(shape):
    return lax.broadcasted_iota(jnp.int32, shape, len(shape) - 1)


def half_mean(values, lane):
    low = jnp.sum(jnp.where(lane < HD, values, 0.0), axis=-1, keepdims=True)
    high = jnp.sum(jnp.where(lane < HD, 0.0, values), axis=-1, keepdims=True)
    return jnp.where(lane < HD, low, high) * (1.0 / HD)


def swap_halves(values, lane):
    return jnp.where(
        (lane & (HD - 1)) < HD // 2, pltpu.roll(values, 96, 1), pltpu.roll(values, 32, 1)
    )


def project_kernel(
    where_ref,
    x_ref,
    gain_ref,
    weight_ref,
    cosine_ref,
    sine_ref,
    gains_ref,
    hot_ref,
    normed_ref,
    raw_ref,
    query_ref,
    kv_ref,
):
    x = x_ref[0].astype(f32)
    normed = norm_rows(x, gain_ref[...]).astype(bf16)
    normed_ref[...] = normed
    project = dot(normed, weight_ref[...], ((1,), (0,)))
    both = project[:, : 2 * HD]
    value = project[:, 2 * HD :]
    raw_ref[...] = both
    lane = lanes(both.shape)
    scaled = both * lax.rsqrt(half_mean(both * both, lane) + EPSILON) * gains_ref[...]
    turned = scaled * cosine_ref[...] + swap_halves(scaled, lane) * sine_ref[...]
    turned = turned.astype(bf16).astype(f32)
    query_ref[...] = jnp.where(lane < HD, turned, hot_ref[...].astype(f32)).astype(bf16)
    kv_ref[...] = jnp.where(lane < HD, value, turned * HD ** (-0.5)).astype(bf16)


def project(where, gathered, gain, weight, cosine, sine, gains, hot):
    blocks = gathered.shape[0]
    rows = blocks * BLOCK
    row_spec = lambda width: pl.BlockSpec((BLOCK, width), lambda j, where: (j, 0))
    whole = lambda array: pl.BlockSpec(array.shape, lambda j, where: (0, 0))
    return pl.pallas_call(
        project_kernel,
        grid_spec=pltpu.PrefetchScalarGridSpec(
            num_scalar_prefetch=1,
            grid=(blocks,),
            in_specs=[
                pl.BlockSpec((1, BLOCK, D), lambda j, where: (where[j], 0, 0)),
                whole(gain),
                whole(weight),
                row_spec(128),
                row_spec(128),
                whole(gains),
                row_spec(128),
            ],
            out_specs=[row_spec(D), row_spec(128), row_spec(128), row_spec(128)],
        ),
        out_shape=[
            jax.ShapeDtypeStruct((rows, D), bf16),
            jax.ShapeDtypeStruct((rows, 128), f32),
            jax.ShapeDtypeStruct((rows, 128), bf16),
            jax.ShapeDtypeStruct((rows, 128), bf16),
        ],
        name="project",
    )(where, gathered, gain, weight, cosine, sine, gains, hot)


def sort_keys(place_ref, own_ref, other_ref, mask_ref, key_ref, value_ref):
    blocks = own_ref.shape[0] // BLOCK
    lane = lanes((BLOCK, 128))
    ones = jnp.where((lane >= HD) & (lane < HD + 3), 1.0, 0.0)
    for half, source_ref in ((0, own_ref), (1, other_ref)):

        def put(j, unused, half=half, source_ref=source_ref):
            source = pl.multiple_of(j * BLOCK, BLOCK)
            tail = pl.multiple_of((half * blocks + j) * BLOCK, BLOCK)
            target = pl.multiple_of(place_ref[half * blocks + j] * BLOCK, BLOCK)
            both = source_ref[pl.ds(source, BLOCK), :].astype(f32)
            mask = mask_ref[pl.ds(tail, BLOCK), :].astype(f32)
            key_ref[pl.ds(target, BLOCK), :] = jnp.where(
                lane < HD, pltpu.roll(both, HD, 1), mask
            ).astype(bf16)
            value_ref[pl.ds(target, BLOCK), :] = jnp.where(lane < HD, both, ones).astype(bf16)
            return unused

        lax.fori_loop(0, blocks, put, 0)


def tile_rows(order_ref, tile):
    count = QUERY_TILE // BLOCK
    return [pl.multiple_of(order_ref[tile * count + i] * BLOCK, BLOCK) for i in range(count)]


def load_rows(ref, starts):
    return jnp.concatenate([ref[pl.ds(start, BLOCK), :] for start in starts], axis=0)


def attend_kernel(
    order_ref,
    place_ref,
    low_ref,
    high_ref,
    query_ref,
    own_ref,
    other_ref,
    mask_ref,
    kept_ref,
    attended_ref,
    key_ref,
    value_ref,
):
    tile = pl.program_id(0)

    @pl.when(tile == 0)
    def _():
        sort_keys(place_ref, own_ref, other_ref, mask_ref, key_ref, value_ref)
        kept_ref[...] = jnp.zeros_like(kept_ref)
        attended_ref[...] = jnp.zeros_like(attended_ref)

    starts = tile_rows(order_ref, tile)
    query = load_rows(query_ref, starts)

    def chunk(index, accumulated):
        first = pl.multiple_of(index * KEY_TILE, KEY_TILE)
        key = key_ref[pl.ds(first, KEY_TILE), :]
        value = value_ref[pl.ds(first, KEY_TILE), :]
        expo = jnp.exp(dot(query, key, ((1,), (1,))))
        return accumulated + dot(expo.astype(bf16), value, ((1,), (0,)))

    accumulated = lax.fori_loop(
        low_ref[tile], high_ref[tile], chunk, jnp.zeros((QUERY_TILE, 128), f32)
    )
    totals = accumulated[:, HD : HD + 1]
    lane = lanes(accumulated.shape)
    kept = jnp.where(lane < HD, accumulated / totals, totals)
    for i, start in enumerate(starts):
        piece = kept[i * BLOCK : (i + 1) * BLOCK]
        kept_ref[pl.ds(start, BLOCK), :] = piece
        attended_ref[pl.ds(start, BLOCK), :] = piece[:, :HD].astype(bf16)


def fixed(array, prefetched):
    return pl.BlockSpec(
        array.shape, lambda *unused: (0,) * len(array.shape), pipeline_mode=pl.Buffered(1)
    )


def attend(order, place, low, high, query, own, other, mask):
    rows = query.shape[0]
    operands = (query, own, other, mask)
    outs = (jax.ShapeDtypeStruct((rows, 128), f32), jax.ShapeDtypeStruct((rows, HD), bf16))
    return pl.pallas_call(
        attend_kernel,
        grid_spec=pltpu.PrefetchScalarGridSpec(
            num_scalar_prefetch=4,
            grid=(low.shape[0],),
            in_specs=[fixed(array, 4) for array in operands],
            out_specs=[fixed(array, 4) for array in outs],
            scratch_shapes=[pltpu.VMEM((2 * rows, 128), bf16), pltpu.VMEM((2 * rows, 128), bf16)],
        ),
        out_shape=list(outs),
        name="attend",
    )(order, place, low, high, *operands)


def attend_back_kernel(
    order_ref,
    place_ref,
    low_ref,
    high_ref,
    query_ref,
    own_ref,
    other_ref,
    mask_ref,
    hot_ref,
    kept_ref,
    grad_ref,
    query_grad_ref,
    own_grad_ref,
    other_grad_ref,
    bias_ref,
    key_ref,
    value_ref,
    key_grad_ref,
    value_grad_ref,
):
    tile = pl.program_id(0)

    @pl.when(tile == 0)
    def _():
        sort_keys(place_ref, own_ref, other_ref, mask_ref, key_ref, value_ref)
        query_grad_ref[...] = jnp.zeros_like(query_grad_ref)
        key_grad_ref[...] = jnp.zeros_like(key_grad_ref)
        value_grad_ref[...] = jnp.zeros_like(value_grad_ref)

    starts = tile_rows(order_ref, tile)
    query = load_rows(query_ref, starts)
    kept = load_rows(kept_ref, starts)
    grad = load_rows(grad_ref, starts).astype(f32)
    grad = jnp.concatenate([grad, jnp.zeros_like(grad)], axis=1)
    lane = lanes(kept.shape)
    totals = kept[:, HD : HD + 1]
    center = jnp.sum(jnp.where(lane < HD, grad * kept, 0.0), axis=1, keepdims=True) / totals
    center_high = center.astype(bf16).astype(f32)
    center_rest = center - center_high
    center_mid = center_rest.astype(bf16).astype(f32)
    center_low = center_rest - center_mid
    wide = jnp.where(lane == HD, -center_high, 0.0)
    wide = jnp.where(lane == HD + 1, -center_mid, wide)
    wide = jnp.where(lane == HD + 2, -center_low, wide)
    wide = jnp.where(lane < HD, grad / totals, wide).astype(bf16)

    def chunk(index, query_grad):
        first = pl.multiple_of(index * KEY_TILE, KEY_TILE)
        window = pl.ds(first, KEY_TILE)
        key = key_ref[window, :]
        value = value_ref[window, :]
        expo = jnp.exp(dot(key, query, ((1,), (1,))))
        score_grad = expo * dot(value, wide, ((1,), (1,)))
        score_low = score_grad.astype(bf16)
        value_grad_ref[window, :] += dot(expo.astype(bf16), wide, ((1,), (0,)))
        key_grad_ref[window, :] += dot(score_low, query, ((1,), (0,)))
        return query_grad + dot(score_low, key, ((0,), (0,)))

    query_grad = lax.fori_loop(
        low_ref[tile], high_ref[tile], chunk, jnp.zeros((QUERY_TILE, 128), f32)
    )
    for i, start in enumerate(starts):
        query_grad_ref[pl.ds(start, BLOCK), :] = query_grad[i * BLOCK : (i + 1) * BLOCK]

    @pl.when(tile == pl.num_programs(0) - 1)
    def _():
        blocks = own_ref.shape[0] // BLOCK
        block_lane = lanes((BLOCK, 128))
        variate = (block_lane >= VARIATE_LANE) & (block_lane < VARIATE_LANE + NVAR)
        sums = (jnp.zeros((BLOCK, 128), f32), jnp.zeros((BLOCK, 128), f32))
        for half, target_ref in ((0, own_grad_ref), (1, other_grad_ref)):

            def take(j, sums, half=half, target_ref=target_ref):
                target = pl.multiple_of(j * BLOCK, BLOCK)
                tail = pl.multiple_of((half * blocks + j) * BLOCK, BLOCK)
                source = pl.multiple_of(place_ref[half * blocks + j] * BLOCK, BLOCK)
                key_grad = key_grad_ref[pl.ds(source, BLOCK), :]
                value_grad = value_grad_ref[pl.ds(source, BLOCK), :]
                target_ref[pl.ds(target, BLOCK), :] = jnp.where(
                    block_lane < HD, value_grad, pltpu.roll(key_grad, HD, 1) * HD ** (-0.5)
                )
                every = jnp.where(variate, key_grad, 0.0)
                hot = hot_ref[pl.ds(tail, BLOCK), :].astype(f32)
                return (sums[0] + every, sums[1] + every * hot)

            sums = lax.fori_loop(0, blocks, take, sums)
        every = jnp.sum(sums[0], keepdims=True)
        same = jnp.sum(sums[1], keepdims=True)
        bias_lane = lanes((8, 128))
        bias_ref[...] = jnp.where(bias_lane == 0, every - same, jnp.where(bias_lane == 1, same, 0.0))


def attend_back(order, place, low, high, query, own, other, mask, hot, kept, grad):
    rows = query.shape[0]
    operands = (query, own, other, mask, hot, kept, grad)
    outs = tuple(jax.ShapeDtypeStruct((rows, 128), f32) for unused in range(3)) + (
        jax.ShapeDtypeStruct((8, 128), f32),
    )
    return pl.pallas_call(
        attend_back_kernel,
        grid_spec=pltpu.PrefetchScalarGridSpec(
            num_scalar_prefetch=4,
            grid=(low.shape[0],),
            in_specs=[fixed(array, 4) for array in operands],
            out_specs=[fixed(array, 4) for array in outs],
            scratch_shapes=[
                pltpu.VMEM((2 * rows, 128), bf16),
                pltpu.VMEM((2 * rows, 128), bf16),
                pltpu.VMEM((2 * rows, 128), f32),
                pltpu.VMEM((2 * rows, 128), f32),
            ],
        ),
        out_shape=list(outs),
        name="attend_back",
    )(order, place, low, high, *operands)


def project_back_kernel(
    query_grad_ref,
    own_ref,
    other_ref,
    raw_ref,
    cosine_ref,
    sine_ref,
    gains_ref,
    normed_ref,
    grad_ref,
    weight_grad_ref,
    gain_grad_ref,
    weight_ref,
    gain_ref,
):
    step = pl.program_id(0)

    @pl.when(step == 0)
    def _():
        weight_ref[...] = jnp.zeros_like(weight_ref)
        gain_ref[...] = jnp.zeros_like(gain_ref)

    kv_grad = (own_ref[...] + other_ref[...]).astype(bf16).astype(f32)
    lane = lanes(kv_grad.shape)
    turned = jnp.where(lane < HD, query_grad_ref[...].astype(bf16).astype(f32), kv_grad)
    grad = turned * cosine_ref[...] - swap_halves(turned, lane) * sine_ref[...]
    raw = raw_ref[...]
    factor = lax.rsqrt(half_mean(raw * raw, lane) + EPSILON)
    scaled = grad * gains_ref[...]
    inner = half_mean(scaled * raw, lane)
    both = (factor * (scaled - raw * (factor * factor) * inner)).astype(bf16)
    gain_ref[...] += jnp.sum(grad * raw * factor, axis=0, keepdims=True)
    value = jnp.where(lane < HD, kv_grad, 0.0).astype(bf16)
    full = jnp.concatenate([both, value], axis=1)
    grad_ref[...] = full[:, : 3 * HD]
    weight_ref[...] += dot(normed_ref[...], full, ((0,), (0,)))

    @pl.when(step == pl.num_programs(0) - 1)
    def _():
        weight_grad_ref[...] = weight_ref[:, : 3 * HD].astype(bf16)
        gain_grad_ref[...] = jnp.broadcast_to(gain_ref[...], gain_grad_ref.shape)


def project_back(query_grad, own, other, raw, cosine, sine, gains, normed):
    rows = query_grad.shape[0]
    step_rows = 2 * BLOCK
    row_spec = lambda width: pl.BlockSpec((step_rows, width), lambda j: (j, 0))
    whole = lambda shape: pl.BlockSpec(shape, lambda j: (0, 0))
    return pl.pallas_call(
        project_back_kernel,
        grid=(rows // step_rows,),
        in_specs=[row_spec(128)] * 6 + [whole(gains.shape), row_spec(D)],
        out_specs=[row_spec(3 * HD), whole((D, 3 * HD)), whole((8, 128))],
        out_shape=[
            jax.ShapeDtypeStruct((rows, 3 * HD), bf16),
            jax.ShapeDtypeStruct((D, 3 * HD), bf16),
            jax.ShapeDtypeStruct((8, 128), f32),
        ],
        scratch_shapes=[pltpu.VMEM((D, 4 * HD), f32), pltpu.VMEM((1, 128), f32)],
        name="project_back",
    )(query_grad, own, other, raw, cosine, sine, gains, normed)


def feed_kernel(
    second_mine_ref,
    second_other_ref,
    grad_mine_ref,
    grad_other_ref,
    weight_ref,
    ffn_mine_ref,
    ffn_other_ref,
    back_mine_ref,
    back_other_ref,
    weight_grad_ref,
    expand_ref,
    down_ref,
    expand_grad_ref,
    down_grad_ref,
):
    step = pl.program_id(0)
    half = pl.num_programs(0) // 2
    depth, both_rows, width = weight_ref.shape
    down_rows = down_ref.shape[0] // depth
    expand_rows = both_rows - down_rows

    @pl.when(step == 0)
    def _():
        for z in range(depth):
            expand_ref[z * expand_rows : (z + 1) * expand_rows] = weight_ref[z, :expand_rows]
            down_ref[z * down_rows : (z + 1) * down_rows] = weight_ref[z, expand_rows:]
        expand_grad_ref[...] = jnp.zeros_like(expand_grad_ref)
        down_grad_ref[...] = jnp.zeros_like(down_grad_ref)

    second = jnp.where(step < half, second_mine_ref[...], second_other_ref[...])
    grad = jnp.where(step < half, grad_mine_ref[...], grad_other_ref[...])
    expand = dot(second, expand_ref[...], ((1,), (0,)))
    gate = expand[:, : width // 2]
    up = expand[:, width // 2 :]
    sigmoid = 1.0 / (1.0 + jnp.exp(-gate))
    silu = gate * sigmoid
    hidden = (silu * up).astype(bf16)
    grad_hidden = dot(grad, down_ref[...], ((1,), (1,)))
    grad_gate = grad_hidden * up * (sigmoid * (1.0 + gate * (1.0 - sigmoid)))
    rows = jnp.concatenate([grad_gate, grad_hidden * silu], axis=1).astype(bf16)
    ffn = dot(hidden, down_ref[...], ((1,), (0,))).astype(bf16)
    back = dot(rows, expand_ref[...], ((1,), (1,))).astype(bf16)
    expand_grad_ref[...] += dot(second, rows, ((0,), (0,)))
    down_grad_ref[...] += dot(hidden, grad, ((0,), (0,)))

    @pl.when(step < half)
    def _():
        ffn_mine_ref[...] = ffn
        back_mine_ref[...] = back

    @pl.when(step >= half)
    def _():
        ffn_other_ref[...] = ffn
        back_other_ref[...] = back

    @pl.when(step == pl.num_programs(0) - 1)
    def _():
        for z in range(depth):
            weight_grad_ref[z, :expand_rows] = expand_grad_ref[
                z * expand_rows : (z + 1) * expand_rows
            ].astype(bf16)
            weight_grad_ref[z, expand_rows:] = down_grad_ref[
                z * down_rows : (z + 1) * down_rows
            ].astype(bf16)


def feed(second, grad, weight, down_rows):
    rows = second[0].shape[0]
    tile = 256
    steps = rows // tile
    depth, both_rows, width = weight.shape
    mine = pl.BlockSpec((tile, D), lambda i: (jnp.minimum(i, steps - 1), 0))
    other = pl.BlockSpec((tile, D), lambda i: (jnp.maximum(i - steps, 0), 0))
    whole = pl.BlockSpec(weight.shape, lambda i: (0, 0, 0), pipeline_mode=pl.Buffered(1))
    token_rows = jax.ShapeDtypeStruct((rows, D), bf16)
    return pl.pallas_call(
        feed_kernel,
        grid=(2 * steps,),
        in_specs=[mine, other, mine, other, whole],
        out_specs=[mine, other, mine, other, whole],
        out_shape=[token_rows] * 4 + [jax.ShapeDtypeStruct(weight.shape, bf16)],
        scratch_shapes=[
            pltpu.VMEM((depth * (both_rows - down_rows), width), bf16),
            pltpu.VMEM((depth * down_rows, D), bf16),
            pltpu.VMEM((depth * (both_rows - down_rows), width), f32),
            pltpu.VMEM((depth * down_rows, D), f32),
        ],
        name="feed",
    )(*second, *grad, weight)


def token_meta(seq_lengths, block_order):
    blocks = block_order.shape[0]
    packed_at = jnp.repeat(block_order, BLOCK) * BLOCK + jnp.tile(
        jnp.arange(BLOCK, dtype=jnp.int32), blocks
    )
    ends = jnp.cumsum(seq_lengths)
    after = packed_at[:, None] >= ends[None, :]
    segment = jnp.sum(after.astype(jnp.int32), axis=1)
    begin = jnp.max(jnp.where(after, ends[None, :], jnp.zeros_like(ends)[None, :]), axis=1)
    return (segment, packed_at - begin, ends)


def both_cores(array, core):
    pairs = array.reshape((-1, 2, BLOCK) + array.shape[1:])
    shape = (-1,) + array.shape[1:]
    own = lax.dynamic_index_in_dim(pairs, core, 1, keepdims=False).reshape(shape)
    other = lax.dynamic_index_in_dim(pairs, 1 - core, 1, keepdims=False).reshape(shape)
    return own, other


def one_hot_rows(segment, variate, segments):
    lane = jnp.arange(128, dtype=jnp.int32)[None, :]
    hot = lane == SEGMENT_LANE + segment[:, None]
    for copy in range(3):
        hot = hot | (lane == VARIATE_LANE + copy * NVAR + variate[:, None])
    return hot.astype(bf16)


def mask_rows(segment, variate, segments, bias):
    lane = jnp.arange(128, dtype=jnp.int32)[None, :]
    here = lane - SEGMENT_LANE
    rows = jnp.where(
        (here >= 0) & (here < segments) & (here != segment[:, None]), jnp.float32(MASK), 0.0
    )
    high = lax.reduce_precision(bias, 8, 7)
    mid = lax.reduce_precision(bias - high, 8, 7)
    low = bias - high - mid
    for copy, part in enumerate((high, mid, low)):
        here = lane - VARIATE_LANE - copy * NVAR
        value = jnp.where(here == variate[:, None], part[1], part[0])
        rows = jnp.where((here >= 0) & (here < NVAR), value, rows)
    return rows.astype(bf16)


def sum_everywhere(vector, devices):
    copies = jnp.broadcast_to(vector[None], (devices,) + vector.shape)
    return jnp.sum(lax.all_to_all(copies, DEVICES, 0, 0, tiled=True), axis=0)


def body(
    inputs,
    cotangent,
    attn_gain,
    ffn_gain,
    query_gain,
    key_gain,
    variate_bias,
    qkv_weight,
    out_weight,
    expand_weight,
    down_weight,
    seq_lengths,
    variate_ids,
    block_order,
):
    depth = lax.axis_size("bz")
    chips = depth * 4
    devices = chips * 2
    sharers = chips // H
    core = lax.axis_index("core")
    chip = (lax.axis_index("bz") * 2 + lax.axis_index("by")) * 2 + lax.axis_index("hx")
    head = chip // sharers
    share = chip % sharers
    rows = qkv_weight.shape[0]
    hidden_rows = down_weight.shape[0]
    segments = seq_lengths.shape[0] + 1
    tokens = variate_ids.shape[0]

    gathered, where = chip_gather(inputs)
    out_full = lax.all_gather(out_weight, DEVICES, axis=0, tiled=True)

    by_head = qkv_weight.reshape(rows, 3, H, HD)
    to_heads = jnp.repeat(
        by_head.transpose(2, 0, 1, 3).reshape(H, rows, 3 * HD), 2 * sharers, axis=0
    )
    own_qkv = lax.all_to_all(to_heads, DEVICES, 0, 0, tiled=True).reshape(D, 3 * HD)
    own_qkv = jnp.pad(own_qkv, ((0, 0), (0, HD)))
    to_plane = (
        expand_weight.reshape(rows, 2, depth, 8, hidden_rows)
        .transpose(3, 0, 1, 2, 4)
        .reshape(8, rows, 2 * depth * hidden_rows)
    )
    expand_part = lax.all_to_all(to_plane, PLANE, 0, 0, tiled=True).reshape(8 * rows, -1)

    segment, position, ends = token_meta(seq_lengths, block_order)
    own_segment, other_segment = both_cores(segment, core)
    own_variate, other_variate = both_cores(variate_ids, core)
    own_position = both_cores(position, core)[0]
    all_segment = jnp.concatenate([own_segment, other_segment])
    all_variate = jnp.concatenate([own_variate, other_variate])
    bias = lax.dynamic_index_in_dim(variate_bias, head, 1, keepdims=False)
    hot = one_hot_rows(all_segment, all_variate, segments)
    mask = mask_rows(all_segment, all_variate, segments, bias)
    freqs = THETA ** (-jnp.arange(HD // 2, dtype=f32) / (HD // 2))
    angles = own_position.astype(f32)[:, None] * freqs[None, :]
    cosine = jnp.tile(jnp.cos(angles), (1, 4))
    sine = jnp.sin(angles)
    sine = jnp.tile(jnp.concatenate([-sine, sine], axis=1), (1, 2))
    pairs = block_order.reshape(chips, 2)
    own_place = lax.dynamic_index_in_dim(pairs, core, 1, keepdims=False)
    other_place = lax.dynamic_index_in_dim(pairs, 1 - core, 1, keepdims=False)
    place = jnp.concatenate([own_place, other_place])
    rank = jnp.sum((own_place[None, :] < own_place[:, None]).astype(jnp.int32), axis=1)
    taken = chips // sharers
    wanted = share * taken + jnp.arange(taken, dtype=jnp.int32)
    chosen = (rank[None, :] == wanted[:, None]).astype(jnp.int32)
    order = jnp.sum(chosen * jnp.arange(chips, dtype=jnp.int32)[None, :], axis=1)
    sorted_place = jnp.sum(chosen * own_place[None, :], axis=1).reshape(-1, QUERY_TILE // BLOCK)
    first_token = sorted_place[:, 0] * BLOCK
    last_token = sorted_place[:, -1] * BLOCK + BLOCK - 1
    begins = jnp.max(jnp.where(ends[None, :] <= first_token[:, None], ends[None, :], 0), axis=1)
    finish = jnp.min(jnp.where(ends[None, :] > last_token[:, None], ends[None, :], tokens), axis=1)
    low = begins // KEY_TILE
    high = (finish + KEY_TILE - 1) // KEY_TILE
    gains = jnp.concatenate([query_gain, key_gain])[None, :]

    feed_part = jnp.concatenate([expand_part, down_weight], axis=0)
    gathered, late_cotangent, out_full, feed_part = lax.optimization_barrier(
        (gathered, cotangent, out_full, feed_part)
    )
    feed_own = lax.all_gather(feed_part[None], "bz", axis=0, tiled=True)
    cotangent_plane = plane_gather(late_cotangent)

    normed_low, raw, query, own_kv = project(
        where, gathered, attn_gain[None], own_qkv, cosine, sine, gains, hot
    )
    other_kv = swap(own_kv, "core")
    kept, attended = attend(order, place, low, high, query, own_kv, other_kv, mask)
    merged = lax.all_to_all(attended.reshape(chips, BLOCK, HD), CHIPS, 0, 0, tiled=True)
    merged = merged.reshape(H, sharers, BLOCK, HD)
    merged = merged[:, 0] if sharers == 1 else jnp.sum(merged, axis=1)
    merged = merged.transpose(1, 0, 2).reshape(BLOCK, D)

    residual = inputs.astype(f32)
    attn_branch = jnp.dot(merged, out_full, preferred_element_type=f32)
    middle = residual + attn_branch
    second_low = plane_gather(norm_rows(middle, ffn_gain).astype(bf16))

    ffn_mine, ffn_other, back_mine, back_other, feed_grad = feed(
        second_low, cotangent_plane, feed_own, hidden_rows
    )
    grad_second = plane_scatter(back_mine, back_other)
    grad_middle, grad_ffn_rows = norm_back(middle, ffn_gain, grad_second)
    grad_middle = cotangent.astype(f32) + grad_middle
    branch_grad = grad_middle.astype(bf16)
    grad_merged = dot(branch_grad, out_full, ((1,), (1,))).astype(bf16)
    to_chips = jnp.repeat(grad_merged.reshape(BLOCK, H, HD).transpose(1, 0, 2), sharers, axis=0)
    grad_attended = lax.all_to_all(to_chips, CHIPS, 0, 0, tiled=True).reshape(-1, HD)

    ffn_branch = plane_scatter(ffn_mine, ffn_other)
    outputs = (middle + ffn_branch).astype(bf16)
    feed_grad = lax.psum_scatter(feed_grad, "bz", scatter_dimension=0, tiled=True)[0]
    grad_down = feed_grad[8 * rows :].astype(f32)
    grad_expand = (
        lax.all_to_all(feed_grad[: 8 * rows].reshape(8, rows, -1), PLANE, 0, 0, tiled=True)
        .reshape(8, rows, 2, depth, hidden_rows)
        .transpose(1, 2, 3, 0, 4)
        .reshape(rows, -1)
        .astype(f32)
    )

    grad_out_full = dot(merged, branch_grad, ((0,), (0,))).astype(bf16)
    grad_out_rows = grad_out_full.reshape(depth, 8, rows, D)
    grad_out_rows = jnp.concatenate(
        [
            lax.dynamic_index_in_dim(grad_out_rows, member, 1, keepdims=False).reshape(-1, D)
            for member in plane_members()
        ],
        axis=0,
    )
    middle_row = grad_out_rows.shape[0] // 2
    grad_out_part = plane_scatter(grad_out_rows[:middle_row], grad_out_rows[middle_row:])
    grad_out_part = grad_out_part.astype(bf16)
    grad_out = lax.psum_scatter(grad_out_part, "bz", scatter_dimension=0, tiled=True).astype(f32)

    query_grad, own_grad, other_grad, bias_grad = attend_back(
        order, place, low, high, query, own_kv, other_kv, mask, hot, kept, grad_attended
    )
    grad_project, grad_qkv_part, gain_grad = project_back(
        query_grad, own_grad, swap(other_grad, "core"), raw, cosine, sine, gains, normed_low
    )
    qkv_full = lax.all_gather(
        by_head.transpose(0, 2, 1, 3).reshape(rows, 3 * D), DEVICES, axis=0, tiled=True
    )
    grad_rows = lax.all_to_all(
        grad_project.reshape(chips, BLOCK, 3 * HD), CHIPS, 0, 0, tiled=True
    ).reshape(H, sharers, BLOCK, 3 * HD)
    grad_rows, grad_qkv_part = lax.optimization_barrier((grad_rows, grad_qkv_part))
    grad_qkv = lax.all_to_all(
        grad_qkv_part.reshape(devices, rows, 3 * HD), DEVICES, 0, 0, tiled=True
    )
    grad_qkv = jnp.sum(grad_qkv.reshape(H, 2 * sharers, rows, 3, HD).astype(f32), axis=1)
    grad_qkv = grad_qkv.transpose(1, 2, 0, 3).reshape(rows, 3 * D)
    if sharers == 1:
        grad_rows = grad_rows[:, 0]
    else:
        grad_rows = jnp.sum(grad_rows.astype(f32), axis=1).astype(bf16)
    grad_rows = grad_rows.transpose(1, 0, 2).reshape(BLOCK, 3 * D)
    grad_normed = dot(grad_rows, qkv_full, ((1,), (1,)))
    grad_first, grad_attn_rows = norm_back(residual, attn_gain, grad_normed)
    grad_inputs = grad_middle + grad_first

    bias_part = jnp.where(
        jnp.arange(H)[None, :] == head, bias_grad[0, :2][:, None], jnp.zeros((2, H), f32)
    )
    squares = jnp.stack(
        [
            jnp.sum(residual * residual),
            jnp.sum(attn_branch * attn_branch),
            jnp.sum(ffn_branch * ffn_branch),
        ]
    )
    packed = jnp.concatenate(
        [
            jnp.sum(grad_attn_rows, axis=0),
            jnp.sum(grad_ffn_rows, axis=0),
            gain_grad[0],
            bias_part.reshape(-1),
            squares,
            jnp.zeros((93,), f32),
        ]
    )
    summed = sum_everywhere(packed, devices)
    at = 2 * D + 2 * HD
    root_means = jnp.sqrt(summed[at + 2 * H : at + 2 * H + 3] / (tokens * D))
    return (
        outputs,
        grad_inputs,
        grad_qkv,
        grad_out,
        grad_expand,
        grad_down,
        summed[:D],
        summed[D : 2 * D],
        summed[2 * D : 2 * D + HD],
        summed[2 * D + HD : at],
        summed[at : at + 2 * H].reshape(2, H),
        root_means,
    )


def solution(mesh):
    grid = mesh.devices if mesh.axis_names == ("head", "blk") else mesh.devices.T
    heads, blks = grid.shape
    mesh = Mesh(grid.reshape(heads // 2, 2, blks // 2, 2), ("hx", "core", "bz", "by"))
    split = P(DEVICES, None)
    return jax.shard_map(
        body,
        mesh=mesh,
        in_specs=(split,) * 2 + (P(),) * 5 + (split,) * 4 + (P(),) * 3,
        out_specs=(split,) * 6 + (P(),) * 6,
        check_vma=False,
    )
```

```python
from functools import partial

import jax
import jax.numpy as jnp
from jax import lax
from jax.experimental import pallas as pl
from jax.experimental.pallas import tpu as pltpu
from jax.sharding import Mesh
from jax.sharding import PartitionSpec as P


D = 1024
H = 16
HD = 64
BLOCK = 128
NVAR = 4
EPSILON = 1e-05
THETA = 10000.0

DEVICES = ("bz", "by", "hx", "core")
CHIPS = ("bz", "by", "hx")
PLANE = ("by", "hx", "core")

SEGMENT_LANE = 64
VARIATE_LANE = 76
MASK = -512.0
QUERY_TILE = 256
KEY_TILE = 256
PROJECT_BLOCKS = 4

bf16 = jnp.bfloat16
f32 = jnp.float32


def dot(left, right, dims):
    return lax.dot_general(left, right, (dims, ((), ())), preferred_element_type=f32)


def norm_rows(values, gain):
    factor = lax.rsqrt(jnp.mean(values * values, axis=-1, keepdims=True) + EPSILON)
    return values * factor * gain


def norm_back(values, gain, grad):
    factor = lax.rsqrt(jnp.mean(values * values, axis=-1, keepdims=True) + EPSILON)
    scaled = grad * gain
    inner = jnp.mean(scaled * values, axis=-1, keepdims=True)
    grad_values = factor * (scaled - values * (factor * factor) * inner)
    return grad_values, grad * values * factor


def swap(shard, axis):
    return lax.ppermute(shard, axis, [(0, 1), (1, 0)])


def plane_gather(shard):
    mine = jnp.concatenate(quarters(shard), axis=0)
    return mine, swap(mine, "core")


def chip_gather(shard, rider, tables):
    depth = lax.axis_size("bz")
    chips = depth * 4
    rows = shard.shape[0]
    z, y, x = lax.axis_index("bz"), lax.axis_index("by"), lax.axis_index("hx")
    at = jnp.arange(chips, dtype=jnp.int32)
    if depth > 4:
        gathered = lax.all_gather(shard, CHIPS, axis=0, tiled=True).reshape(chips, rows, D)
        return gathered, at, jnp.concatenate(quarters(rider), axis=0), tables
    shifted = [
        lax.ppermute(shard, "bz", [(i, (i + by) % depth) for i in range(depth)])
        for by in range(1, depth)
    ]
    near = quarters(jnp.concatenate([shard, rider], axis=0))
    shifted, tables = lax.optimization_barrier((shifted, tables))
    pieces = [near[0][:rows], near[1][:rows], near[2][:rows], near[3]]
    riders = [near[0][rows:], near[1][rows:], near[2][rows:], near[4]]
    pieces = pieces + quarters(jnp.concatenate(shifted, axis=0))
    back = (z - at // 4) % depth
    flips = ((at % 2) ^ x) + 2 * (((at // 2) % 2) ^ y)
    where = jnp.where(back == 0, flips, 4 + flips * (depth - 1) + back - 1).astype(jnp.int32)
    gathered = jnp.concatenate(pieces, axis=0).reshape(chips, rows, D)
    return gathered, where, jnp.concatenate(riders, axis=0), tables


def sum_everywhere(values):
    for axis in ("core", "hx", "by"):
        values = values + swap(values, axis)
    depth = lax.axis_size("bz")
    step = 1
    while step < depth:
        values = values + lax.ppermute(values, "bz", [(i, i ^ step) for i in range(depth)])
        step *= 2
    return values


def quarters(shard):
    half = shard.shape[0] // 2
    across_x = swap(shard, "hx")
    across_y = swap(shard, "by")
    return [shard, across_x, across_y, swap(across_y[:half], "hx"), swap(across_x[half:], "by")]


def plane_scatter(mine, other):
    rows = mine.shape[0] // 4
    half = rows // 2
    mine = mine.astype(f32) + swap(other, "core").astype(f32)
    corner = mine[3 * rows :].astype(bf16)
    for_y = swap(corner[:half], "hx").astype(f32)
    for_x = swap(corner[half:], "by").astype(f32)
    to_x = mine[rows : 2 * rows]
    to_y = mine[2 * rows : 3 * rows]
    to_x = jnp.concatenate([to_x[:half], to_x[half:] + for_x], axis=0).astype(bf16)
    to_y = jnp.concatenate([to_y[:half] + for_y, to_y[half:]], axis=0).astype(bf16)
    from_x = swap(to_x, "hx")
    from_y = swap(to_y, "by")
    return mine[:rows], from_x, from_y


def plane_members():
    by, hx, core = lax.axis_index("by"), lax.axis_index("hx"), lax.axis_index("core")
    members = []
    for core_flip in (0, 1):
        for x_flip, y_flip in ((0, 0), (1, 0), (0, 1), (1, 1)):
            members.append((by ^ y_flip) * 4 + (hx ^ x_flip) * 2 + (core ^ core_flip))
    return members


def lanes(shape):
    return lax.broadcasted_iota(jnp.int32, shape, len(shape) - 1)


def half_mean(values, lane):
    low = jnp.sum(jnp.where(lane < HD, values, 0.0), axis=-1, keepdims=True)
    high = jnp.sum(jnp.where(lane < HD, 0.0, values), axis=-1, keepdims=True)
    return jnp.where(lane < HD, low, high) * (1.0 / HD)


def swap_halves(values, lane):
    return jnp.where(
        (lane & (HD - 1)) < HD // 2, pltpu.roll(values, 96, 1), pltpu.roll(values, 32, 1)
    )


def project_kernel(where_ref, *refs):
    x_refs = refs[:PROJECT_BLOCKS]
    gain_ref, weight_ref, cosine_ref, sine_ref, gains_ref, hot_ref = refs[PROJECT_BLOCKS:-4]
    normed_ref, raw_ref, query_ref, kv_ref = refs[-4:]
    x = jnp.concatenate([x_ref[0] for x_ref in x_refs], axis=0).astype(f32)
    normed = norm_rows(x, gain_ref[...]).astype(bf16)
    normed_ref[...] = normed
    project = dot(normed, weight_ref[...], ((1,), (0,)))
    both = project[:, : 2 * HD]
    value = project[:, 2 * HD :]
    raw_ref[...] = both
    lane = lanes(both.shape)
    scaled = both * lax.rsqrt(half_mean(both * both, lane) + EPSILON) * gains_ref[...]
    turned = scaled * cosine_ref[...] + swap_halves(scaled, lane) * sine_ref[...]
    turned = turned.astype(bf16).astype(f32)
    query_ref[...] = jnp.where(lane < HD, turned, hot_ref[...].astype(f32)).astype(bf16)
    kv_ref[...] = jnp.where(lane < HD, value, turned * HD ** (-0.5)).astype(bf16)


def project(where, gathered, gain, weight, cosine, sine, gains, hot):
    blocks = gathered.shape[0]
    rows = blocks * BLOCK
    step_rows = PROJECT_BLOCKS * BLOCK
    row_spec = lambda width: pl.BlockSpec((step_rows, width), lambda j, where: (j, 0))
    whole = lambda array: pl.BlockSpec(array.shape, lambda j, where: (0, 0))
    block = lambda i: pl.BlockSpec(
        (1, BLOCK, D), lambda j, where: (where[j * PROJECT_BLOCKS + i], 0, 0)
    )
    return pl.pallas_call(
        project_kernel,
        grid_spec=pltpu.PrefetchScalarGridSpec(
            num_scalar_prefetch=1,
            grid=(blocks // PROJECT_BLOCKS,),
            in_specs=[block(i) for i in range(PROJECT_BLOCKS)]
            + [
                whole(gain),
                whole(weight),
                row_spec(128),
                row_spec(128),
                whole(gains),
                row_spec(128),
            ],
            out_specs=[row_spec(D), row_spec(128), row_spec(128), row_spec(128)],
        ),
        out_shape=[
            jax.ShapeDtypeStruct((rows, D), bf16),
            jax.ShapeDtypeStruct((rows, 128), f32),
            jax.ShapeDtypeStruct((rows, 128), bf16),
            jax.ShapeDtypeStruct((rows, 128), bf16),
        ],
        name="project",
    )(where, *[gathered] * PROJECT_BLOCKS, gain, weight, cosine, sine, gains, hot)


def sort_keys(place_ref, own_ref, other_ref, mask_ref, key_ref, value_ref):
    blocks = own_ref.shape[0] // BLOCK
    lane = lanes((BLOCK, 128))
    ones = jnp.where((lane >= HD) & (lane < HD + 3), 1.0, 0.0)
    for half, source_ref in ((0, own_ref), (1, other_ref)):

        def put(j, unused, half=half, source_ref=source_ref):
            source = pl.multiple_of(j * BLOCK, BLOCK)
            tail = pl.multiple_of((half * blocks + j) * BLOCK, BLOCK)
            target = pl.multiple_of(place_ref[half * blocks + j] * BLOCK, BLOCK)
            both = source_ref[pl.ds(source, BLOCK), :].astype(f32)
            mask = mask_ref[pl.ds(tail, BLOCK), :].astype(f32)
            key_ref[pl.ds(target, BLOCK), :] = jnp.where(
                lane < HD, pltpu.roll(both, HD, 1), mask
            ).astype(bf16)
            value_ref[pl.ds(target, BLOCK), :] = jnp.where(lane < HD, both, ones).astype(bf16)
            return unused

        lax.fori_loop(0, blocks, put, 0)


def tile_rows(order_ref, tile):
    count = QUERY_TILE // BLOCK
    return [pl.multiple_of(order_ref[tile * count + i] * BLOCK, BLOCK) for i in range(count)]


def load_rows(ref, starts):
    return jnp.concatenate([ref[pl.ds(start, BLOCK), :] for start in starts], axis=0)


def attend_kernel(
    order_ref,
    place_ref,
    low_ref,
    high_ref,
    query_ref,
    own_ref,
    other_ref,
    mask_ref,
    kept_ref,
    attended_ref,
    key_ref,
    value_ref,
):
    tile = pl.program_id(0)

    @pl.when(tile == 0)
    def _():
        sort_keys(place_ref, own_ref, other_ref, mask_ref, key_ref, value_ref)
        kept_ref[...] = jnp.zeros_like(kept_ref)
        attended_ref[...] = jnp.zeros_like(attended_ref)

    starts = tile_rows(order_ref, tile)
    query = load_rows(query_ref, starts)

    def chunk(index, accumulated):
        first = pl.multiple_of(index * KEY_TILE, KEY_TILE)
        key = key_ref[pl.ds(first, KEY_TILE), :]
        value = value_ref[pl.ds(first, KEY_TILE), :]
        expo = jnp.exp(dot(query, key, ((1,), (1,))))
        return accumulated + dot(expo.astype(bf16), value, ((1,), (0,)))

    accumulated = lax.fori_loop(
        low_ref[tile], high_ref[tile], chunk, jnp.zeros((QUERY_TILE, 128), f32)
    )
    totals = accumulated[:, HD : HD + 1]
    lane = lanes(accumulated.shape)
    kept = jnp.where(lane < HD, accumulated / totals, totals)
    for i, start in enumerate(starts):
        piece = kept[i * BLOCK : (i + 1) * BLOCK]
        kept_ref[pl.ds(start, BLOCK), :] = piece
        attended_ref[pl.ds(start, BLOCK), :] = piece[:, :HD].astype(bf16)


def fixed(array):
    return pl.BlockSpec(
        array.shape, lambda *unused: (0,) * len(array.shape), pipeline_mode=pl.Buffered(1)
    )


def attend(order, place, low, high, query, own, other, mask):
    rows = query.shape[0]
    operands = (query, own, other, mask)
    outs = (jax.ShapeDtypeStruct((rows, 128), f32), jax.ShapeDtypeStruct((rows, HD), bf16))
    return pl.pallas_call(
        attend_kernel,
        grid_spec=pltpu.PrefetchScalarGridSpec(
            num_scalar_prefetch=4,
            grid=(low.shape[0],),
            in_specs=[fixed(array) for array in operands],
            out_specs=[fixed(array) for array in outs],
            scratch_shapes=[pltpu.VMEM((2 * rows, 128), bf16), pltpu.VMEM((2 * rows, 128), bf16)],
        ),
        out_shape=list(outs),
        name="attend",
    )(order, place, low, high, *operands)


def attend_back_kernel(
    order_ref,
    place_ref,
    low_ref,
    high_ref,
    query_ref,
    own_ref,
    other_ref,
    mask_ref,
    hot_ref,
    kept_ref,
    grad_ref,
    query_grad_ref,
    own_grad_ref,
    other_grad_ref,
    bias_ref,
    key_ref,
    value_ref,
    key_grad_ref,
    value_grad_ref,
):
    tile = pl.program_id(0)

    @pl.when(tile == 0)
    def _():
        sort_keys(place_ref, own_ref, other_ref, mask_ref, key_ref, value_ref)
        query_grad_ref[...] = jnp.zeros_like(query_grad_ref)
        key_grad_ref[...] = jnp.zeros_like(key_grad_ref)
        value_grad_ref[...] = jnp.zeros_like(value_grad_ref)

    starts = tile_rows(order_ref, tile)
    query = load_rows(query_ref, starts)
    kept = load_rows(kept_ref, starts)
    grad = load_rows(grad_ref, starts).astype(f32)
    grad = jnp.concatenate([grad, jnp.zeros_like(grad)], axis=1)
    lane = lanes(kept.shape)
    totals = kept[:, HD : HD + 1]
    center = jnp.sum(jnp.where(lane < HD, grad * kept, 0.0), axis=1, keepdims=True) / totals
    center_high = center.astype(bf16).astype(f32)
    center_rest = center - center_high
    center_mid = center_rest.astype(bf16).astype(f32)
    center_low = center_rest - center_mid
    wide = jnp.where(lane == HD, -center_high, 0.0)
    wide = jnp.where(lane == HD + 1, -center_mid, wide)
    wide = jnp.where(lane == HD + 2, -center_low, wide)
    wide = jnp.where(lane < HD, grad / totals, wide).astype(bf16)

    def chunk(index, query_grad):
        first = pl.multiple_of(index * KEY_TILE, KEY_TILE)
        window = pl.ds(first, KEY_TILE)
        key = key_ref[window, :]
        value = value_ref[window, :]
        expo = jnp.exp(dot(key, query, ((1,), (1,))))
        score_grad = expo * dot(value, wide, ((1,), (1,)))
        score_low = score_grad.astype(bf16)
        value_grad_ref[window, :] += dot(expo.astype(bf16), wide, ((1,), (0,)))
        key_grad_ref[window, :] += dot(score_low, query, ((1,), (0,)))
        return query_grad + dot(score_low, key, ((0,), (0,)))

    query_grad = lax.fori_loop(
        low_ref[tile], high_ref[tile], chunk, jnp.zeros((QUERY_TILE, 128), f32)
    )
    for i, start in enumerate(starts):
        query_grad_ref[pl.ds(start, BLOCK), :] = query_grad[i * BLOCK : (i + 1) * BLOCK]

    @pl.when(tile == pl.num_programs(0) - 1)
    def _():
        blocks = own_ref.shape[0] // BLOCK
        block_lane = lanes((BLOCK, 128))
        variate = (block_lane >= VARIATE_LANE) & (block_lane < VARIATE_LANE + NVAR)
        sums = (jnp.zeros((BLOCK, 128), f32), jnp.zeros((BLOCK, 128), f32))
        for half, target_ref in ((0, own_grad_ref), (1, other_grad_ref)):

            def take(j, sums, half=half, target_ref=target_ref):
                target = pl.multiple_of(j * BLOCK, BLOCK)
                tail = pl.multiple_of((half * blocks + j) * BLOCK, BLOCK)
                source = pl.multiple_of(place_ref[half * blocks + j] * BLOCK, BLOCK)
                key_grad = key_grad_ref[pl.ds(source, BLOCK), :]
                value_grad = value_grad_ref[pl.ds(source, BLOCK), :]
                target_ref[pl.ds(target, BLOCK), :] = jnp.where(
                    block_lane < HD, value_grad, pltpu.roll(key_grad, HD, 1) * HD ** (-0.5)
                )
                every = jnp.where(variate, key_grad, 0.0)
                hot = hot_ref[pl.ds(tail, BLOCK), :].astype(f32)
                return (sums[0] + every, sums[1] + every * hot)

            sums = lax.fori_loop(0, blocks, take, sums)
        every = jnp.sum(sums[0], keepdims=True)
        same = jnp.sum(sums[1], keepdims=True)
        bias_lane = lanes((8, 128))
        bias_ref[...] = jnp.where(bias_lane == 0, every - same, jnp.where(bias_lane == 1, same, 0.0))


def attend_back(order, place, low, high, query, own, other, mask, hot, kept, grad):
    rows = query.shape[0]
    operands = (query, own, other, mask, hot, kept, grad)
    outs = tuple(jax.ShapeDtypeStruct((rows, 128), f32) for _ in range(3)) + (
        jax.ShapeDtypeStruct((8, 128), f32),
    )
    return pl.pallas_call(
        attend_back_kernel,
        grid_spec=pltpu.PrefetchScalarGridSpec(
            num_scalar_prefetch=4,
            grid=(low.shape[0],),
            in_specs=[fixed(array) for array in operands],
            out_specs=[fixed(array) for array in outs],
            scratch_shapes=[
                pltpu.VMEM((2 * rows, 128), bf16),
                pltpu.VMEM((2 * rows, 128), bf16),
                pltpu.VMEM((2 * rows, 128), f32),
                pltpu.VMEM((2 * rows, 128), f32),
            ],
        ),
        out_shape=list(outs),
        name="attend_back",
    )(order, place, low, high, *operands)


def project_back_kernel(
    query_grad_ref,
    own_ref,
    other_ref,
    raw_ref,
    cosine_ref,
    sine_ref,
    gains_ref,
    normed_ref,
    forward_ref,
    grad_ref,
    weight_grad_ref,
    gain_grad_ref,
    attn_grad_ref,
    weight_ref,
    gain_ref,
):
    step = pl.program_id(0)

    @pl.when(step == 0)
    def _():
        weight_ref[...] = jnp.zeros_like(weight_ref)
        gain_ref[...] = jnp.zeros_like(gain_ref)

    kv_grad = (own_ref[...] + other_ref[...]).astype(bf16).astype(f32)
    lane = lanes(kv_grad.shape)
    turned = jnp.where(lane < HD, query_grad_ref[...].astype(bf16).astype(f32), kv_grad)
    grad = turned * cosine_ref[...] - swap_halves(turned, lane) * sine_ref[...]
    raw = raw_ref[...]
    factor = lax.rsqrt(half_mean(raw * raw, lane) + EPSILON)
    scaled = grad * gains_ref[...]
    inner = half_mean(scaled * raw, lane)
    both = (factor * (scaled - raw * (factor * factor) * inner)).astype(bf16)
    gain_ref[...] += jnp.sum(grad * raw * factor, axis=0, keepdims=True)
    value = jnp.where(lane < HD, kv_grad, 0.0).astype(bf16)
    full = jnp.concatenate([both, value], axis=1)
    grad_ref[...] = full[:, : 3 * HD]
    weight_ref[...] += dot(normed_ref[...], full, ((0,), (0,)))

    @pl.when(step == pl.num_programs(0) - 1)
    def _():
        weight_grad_ref[...] = weight_ref[:, : 3 * HD].astype(bf16)
        gain_grad_ref[...] = jnp.broadcast_to(gain_ref[...], gain_grad_ref.shape)
        forward = forward_ref[...].astype(f32)
        attn = jnp.sum(weight_ref[...] * forward, axis=1, keepdims=True)
        attn_grad_ref[...] = jnp.broadcast_to(attn, attn_grad_ref.shape)


def project_back(query_grad, own, other, raw, cosine, sine, gains, normed, forward):
    rows = query_grad.shape[0]
    step_rows = 2 * BLOCK
    row_spec = lambda width: pl.BlockSpec((step_rows, width), lambda j: (j, 0))
    whole = lambda shape: pl.BlockSpec(shape, lambda j: (0, 0))
    return pl.pallas_call(
        project_back_kernel,
        grid=(rows // step_rows,),
        in_specs=[row_spec(128)] * 6 + [whole(gains.shape), row_spec(D), whole(forward.shape)],
        out_specs=[row_spec(3 * HD), whole((D, 3 * HD)), whole((8, 128)), whole((D, 128))],
        out_shape=[
            jax.ShapeDtypeStruct((rows, 3 * HD), bf16),
            jax.ShapeDtypeStruct((D, 3 * HD), bf16),
            jax.ShapeDtypeStruct((8, 128), f32),
            jax.ShapeDtypeStruct((D, 128), f32),
        ],
        scratch_shapes=[pltpu.VMEM((D, 4 * HD), f32), pltpu.VMEM((1, 128), f32)],
        name="project_back",
    )(query_grad, own, other, raw, cosine, sine, gains, normed, forward)


def feed_kernel(
    second_mine_ref,
    second_other_ref,
    grad_mine_ref,
    grad_other_ref,
    weight_ref,
    ffn_mine_ref,
    ffn_other_ref,
    back_mine_ref,
    back_other_ref,
    weight_grad_ref,
    expand_ref,
    down_ref,
    expand_grad_ref,
    down_grad_ref,
):
    step = pl.program_id(0)
    half = pl.num_programs(0) // 2
    depth, both_rows, width = weight_ref.shape
    down_rows = down_ref.shape[0] // depth
    expand_rows = both_rows - down_rows

    @pl.when(step == 0)
    def _():
        for z in range(depth):
            expand_ref[z * expand_rows : (z + 1) * expand_rows] = weight_ref[z, :expand_rows]
            down_ref[z * down_rows : (z + 1) * down_rows] = weight_ref[z, expand_rows:]
        expand_grad_ref[...] = jnp.zeros_like(expand_grad_ref)
        down_grad_ref[...] = jnp.zeros_like(down_grad_ref)

    second = jnp.where(step < half, second_mine_ref[...], second_other_ref[...])
    grad = jnp.where(step < half, grad_mine_ref[...], grad_other_ref[...])
    expand = dot(second, expand_ref[...], ((1,), (0,)))
    gate = expand[:, : width // 2]
    up = expand[:, width // 2 :]
    sigmoid = 1.0 / (1.0 + jnp.exp(-gate))
    silu = gate * sigmoid
    hidden = (silu * up).astype(bf16)
    grad_hidden = dot(grad, down_ref[...], ((1,), (1,)))
    grad_gate = grad_hidden * up * (sigmoid * (1.0 + gate * (1.0 - sigmoid)))
    rows = jnp.concatenate([grad_gate, grad_hidden * silu], axis=1).astype(bf16)
    ffn = dot(hidden, down_ref[...], ((1,), (0,))).astype(bf16)
    back = dot(rows, expand_ref[...], ((1,), (1,))).astype(bf16)
    expand_grad_ref[...] += dot(second, rows, ((0,), (0,)))
    down_grad_ref[...] += dot(hidden, grad, ((0,), (0,)))

    @pl.when(step < half)
    def _():
        ffn_mine_ref[...] = ffn
        back_mine_ref[...] = back

    @pl.when(step >= half)
    def _():
        ffn_other_ref[...] = ffn
        back_other_ref[...] = back

    @pl.when(step == pl.num_programs(0) - 1)
    def _():
        for z in range(depth):
            weight_grad_ref[z, :expand_rows] = expand_grad_ref[
                z * expand_rows : (z + 1) * expand_rows
            ].astype(bf16)
            weight_grad_ref[z, expand_rows:] = down_grad_ref[
                z * down_rows : (z + 1) * down_rows
            ].astype(bf16)


def feed(second, grad, weight, down_rows):
    rows = second[0].shape[0]
    tile = 256
    steps = rows // tile
    depth, both_rows, width = weight.shape
    mine = pl.BlockSpec((tile, D), lambda i: (jnp.minimum(i, steps - 1), 0))
    other = pl.BlockSpec((tile, D), lambda i: (jnp.maximum(i - steps, 0), 0))
    whole = pl.BlockSpec(weight.shape, lambda i: (0, 0, 0), pipeline_mode=pl.Buffered(1))
    token_rows = jax.ShapeDtypeStruct((rows, D), bf16)
    return pl.pallas_call(
        feed_kernel,
        grid=(2 * steps,),
        in_specs=[mine, other, mine, other, whole],
        out_specs=[mine, other, mine, other, whole],
        out_shape=[token_rows] * 4 + [jax.ShapeDtypeStruct(weight.shape, bf16)],
        scratch_shapes=[
            pltpu.VMEM((depth * (both_rows - down_rows), width), bf16),
            pltpu.VMEM((depth * down_rows, D), bf16),
            pltpu.VMEM((depth * (both_rows - down_rows), width), f32),
            pltpu.VMEM((depth * down_rows, D), f32),
        ],
        name="feed",
    )(*second, *grad, weight)


def out_kernel(
    parts_ref, x_ref, weight_ref, gain_ref, merged_ref, middle_ref, second_ref, squares_ref
):
    heads = parts_ref.shape[0]
    for pair in range(heads // 2):
        merged_ref[:, pair * 2 * HD : (pair + 1) * 2 * HD] = jnp.concatenate(
            [parts_ref[2 * pair], parts_ref[2 * pair + 1]], axis=1
        )
    branch = dot(merged_ref[...], weight_ref[...], ((1,), (0,)))
    x = x_ref[...].astype(f32)
    middle = x + branch
    middle_ref[...] = middle
    second_ref[...] = norm_rows(middle, gain_ref[...]).astype(bf16)
    row = lax.broadcasted_iota(jnp.int32, squares_ref.shape, 0)
    x_sum = jnp.sum(x * x, keepdims=True)
    branch_sum = jnp.sum(branch * branch, keepdims=True)
    squares_ref[...] = jnp.where(row == 0, x_sum, branch_sum)


def out_project(parts, x, weight, gain):
    rows = x.shape[0]
    return pl.pallas_call(
        out_kernel,
        out_shape=[
            jax.ShapeDtypeStruct((rows, D), bf16),
            jax.ShapeDtypeStruct((rows, D), f32),
            jax.ShapeDtypeStruct((rows, D), bf16),
            jax.ShapeDtypeStruct((8, 128), f32),
        ],
        name="out_project",
    )(parts, x, weight, gain)


def middle_back_kernel(
    own_ref,
    from_x_ref,
    from_y_ref,
    middle_ref,
    cotangent_ref,
    gain_ref,
    weight_ref,
    grad_middle_ref,
    branch_ref,
    parts_ref,
    gain_grad_ref,
):
    grad_second = own_ref[...] + from_x_ref[...].astype(f32) + from_y_ref[...].astype(f32)
    grad_middle, gain_rows = norm_back(middle_ref[...], gain_ref[...], grad_second)
    grad_middle = cotangent_ref[...].astype(f32) + grad_middle
    grad_middle_ref[...] = grad_middle
    branch = grad_middle.astype(bf16)
    branch_ref[...] = branch
    merged = dot(branch, weight_ref[...], ((1,), (1,))).astype(bf16)
    for head in range(parts_ref.shape[0]):
        parts_ref[head] = merged[:, head * HD : (head + 1) * HD]
    gain_grad_ref[...] = jnp.broadcast_to(
        jnp.sum(gain_rows, axis=0, keepdims=True), gain_grad_ref.shape
    )


def middle_back(own, from_x, from_y, middle, cotangent, gain, weight):
    rows = middle.shape[0]
    return pl.pallas_call(
        middle_back_kernel,
        out_shape=[
            jax.ShapeDtypeStruct((rows, D), f32),
            jax.ShapeDtypeStruct((rows, D), bf16),
            jax.ShapeDtypeStruct((H, rows, HD), bf16),
            jax.ShapeDtypeStruct((8, D), f32),
        ],
        name="middle_back",
    )(own, from_x, from_y, middle, cotangent, gain, weight)


def out_grad_kernel(
    members_ref,
    merged_ref,
    branch_ref,
    ffn_mine_ref,
    ffn_other_ref,
    mine_ref,
    other_ref,
    grad_ref,
    depth,
):
    shard = mine_ref.shape[0] // 4
    rows = shard // depth
    grad_ref[...] = dot(merged_ref[...], branch_ref[...], ((0,), (0,)))
    mine_ref[:, :D] = ffn_mine_ref[...]
    other_ref[:, :D] = ffn_other_ref[...]
    for place in range(8):
        target_ref = mine_ref if place < 4 else other_ref
        for z in range(depth):
            source = pl.multiple_of((z * 8 + members_ref[place]) * rows, rows)
            target = (place % 4) * shard + z * rows
            target_ref[target : target + rows, D:] = grad_ref[pl.ds(source, rows), :].astype(bf16)


def out_grad(members, merged, branch, ffn_mine, ffn_other, depth):
    joined = jax.ShapeDtypeStruct((ffn_mine.shape[0], 2 * D), bf16)
    operands = (merged, branch, ffn_mine, ffn_other)
    return pl.pallas_call(
        partial(out_grad_kernel, depth=depth),
        grid_spec=pltpu.PrefetchScalarGridSpec(
            num_scalar_prefetch=1,
            grid=(1,),
            in_specs=[fixed(array) for array in operands],
            out_specs=[fixed(joined), fixed(joined)],
            scratch_shapes=[pltpu.VMEM((D, D), f32)],
        ),
        out_shape=[joined, joined],
        name="out_grad",
    )(members, *operands)


def input_back_kernel(
    joined_ref, weight_ref, x_ref, gain_ref, middle_ref, grad_ref, qkv_ref, wide_ref
):
    heads = joined_ref.shape[0]
    rows = x_ref.shape[0]
    for pair in range(heads // 2):
        left = joined_ref[2 * pair]
        right = joined_ref[2 * pair + 1]
        wide_ref[:, pair * 6 * HD : (pair + 1) * 6 * HD] = jnp.concatenate(
            [left[:rows], right[:rows]], axis=1
        )
        for part in range(3):
            at = part * D + pair * 2 * HD
            window = slice(part * HD, (part + 1) * HD)
            qkv_ref[:, at : at + 2 * HD] = jnp.concatenate(
                [left[rows:, window], right[rows:, window]], axis=1
            ).astype(f32)
    grad_normed = dot(wide_ref[...], weight_ref[...], ((1,), (1,)))
    grad, _ = norm_back(x_ref[...].astype(f32), gain_ref[...], grad_normed)
    grad_ref[...] = middle_ref[...] + grad


def input_back(joined, weight, x, gain, middle):
    rows = x.shape[0]
    return pl.pallas_call(
        input_back_kernel,
        out_shape=[
            jax.ShapeDtypeStruct((rows, D), f32),
            jax.ShapeDtypeStruct((joined.shape[1] - rows, 3 * D), f32),
        ],
        scratch_shapes=[pltpu.VMEM((rows, 3 * D), bf16)],
        name="input_back",
    )(joined, weight, x, gain, middle)


def widen_kernel(parts_ref, grad_ref):
    sources, _, width = parts_ref.shape
    for source in range(sources):
        for at in range(width // 128):
            to = (at * sources + source) * 128
            grad_ref[:, to : to + 128] = parts_ref[source, :, at * 128 : (at + 1) * 128].astype(f32)


def widen(parts, depth, hidden_rows):
    sources, rows, width = parts.shape
    if hidden_rows != 128:
        parts = parts.reshape(sources, rows, 2, depth, hidden_rows)
        return parts.transpose(1, 2, 3, 0, 4).reshape(rows, -1).astype(f32)
    return pl.pallas_call(
        widen_kernel, out_shape=jax.ShapeDtypeStruct((rows, sources * width), f32), name="widen"
    )(parts)


def token_meta(seq_lengths, block_order):
    blocks = block_order.shape[0]
    packed_at = jnp.repeat(block_order, BLOCK) * BLOCK + jnp.tile(
        jnp.arange(BLOCK, dtype=jnp.int32), blocks
    )
    ends = jnp.cumsum(seq_lengths)
    after = packed_at[:, None] >= ends[None, :]
    segment = jnp.sum(after.astype(jnp.int32), axis=1)
    begin = jnp.max(jnp.where(after, ends[None, :], jnp.zeros_like(ends)[None, :]), axis=1)
    return (segment, packed_at - begin, ends)


def both_cores(array, core):
    pairs = array.reshape((-1, 2, BLOCK) + array.shape[1:])
    shape = (-1,) + array.shape[1:]
    own = lax.dynamic_index_in_dim(pairs, core, 1, keepdims=False).reshape(shape)
    other = lax.dynamic_index_in_dim(pairs, 1 - core, 1, keepdims=False).reshape(shape)
    return own, other


def one_hot_rows(segment, variate):
    lane = jnp.arange(128, dtype=jnp.int32)[None, :]
    hot = lane == SEGMENT_LANE + segment[:, None]
    for copy in range(3):
        hot = hot | (lane == VARIATE_LANE + copy * NVAR + variate[:, None])
    return hot.astype(bf16)


def mask_rows(segment, variate, segments, bias):
    lane = jnp.arange(128, dtype=jnp.int32)[None, :]
    here = lane - SEGMENT_LANE
    rows = jnp.where(
        (here >= 0) & (here < segments) & (here != segment[:, None]), jnp.float32(MASK), 0.0
    )
    high = lax.reduce_precision(bias, 8, 7)
    mid = lax.reduce_precision(bias - high, 8, 7)
    low = bias - high - mid
    for copy, part in enumerate((high, mid, low)):
        here = lane - VARIATE_LANE - copy * NVAR
        value = jnp.where(here == variate[:, None], part[1], part[0])
        rows = jnp.where((here >= 0) & (here < NVAR), value, rows)
    return rows.astype(bf16)


def over_sharers(parts, sharers):
    if sharers == 1:
        return parts
    parts = parts.reshape((H, sharers) + parts.shape[1:]).astype(f32)
    return jnp.sum(parts, axis=1).astype(bf16)


def body(
    inputs,
    cotangent,
    attn_gain,
    ffn_gain,
    query_gain,
    key_gain,
    variate_bias,
    qkv_weight,
    out_weight,
    expand_weight,
    down_weight,
    seq_lengths,
    variate_ids,
    block_order,
):
    depth = lax.axis_size("bz")
    chips = depth * 4
    sharers = chips // H
    core = lax.axis_index("core")
    chip = (lax.axis_index("bz") * 2 + lax.axis_index("by")) * 2 + lax.axis_index("hx")
    head = chip // sharers
    share = chip % sharers
    rows = qkv_weight.shape[0]
    hidden_rows = down_weight.shape[0]
    segments = seq_lengths.shape[0] + 1
    tokens = variate_ids.shape[0]

    out_full = lax.all_gather(out_weight, DEVICES, axis=0, tiled=True)

    by_head = qkv_weight.reshape(rows, 3, H, HD)
    to_heads = jnp.repeat(
        by_head.transpose(2, 0, 1, 3).reshape(H, rows, 3 * HD), 2 * sharers, axis=0
    )
    own_qkv = lax.all_to_all(to_heads, DEVICES, 0, 0, tiled=True).reshape(D, 3 * HD)
    own_qkv = jnp.pad(own_qkv, ((0, 0), (0, HD)))
    to_plane = (
        expand_weight.reshape(rows, 2, depth, 8, hidden_rows)
        .transpose(3, 0, 1, 2, 4)
        .reshape(8, rows, 2 * depth * hidden_rows)
    )
    expand_part = lax.all_to_all(to_plane, PLANE, 0, 0, tiled=True).reshape(8 * rows, -1)

    segment, position, ends = token_meta(seq_lengths, block_order)
    own_segment, other_segment = both_cores(segment, core)
    own_variate, other_variate = both_cores(variate_ids, core)
    own_position = both_cores(position, core)[0]
    all_segment = jnp.concatenate([own_segment, other_segment])
    all_variate = jnp.concatenate([own_variate, other_variate])
    bias = lax.dynamic_index_in_dim(variate_bias, head, 1, keepdims=False)
    hot = one_hot_rows(all_segment, all_variate)
    mask = mask_rows(all_segment, all_variate, segments, bias)
    freqs = THETA ** (-jnp.arange(HD // 2, dtype=f32) / (HD // 2))
    angles = own_position.astype(f32)[:, None] * freqs[None, :]
    cosine = jnp.tile(jnp.cos(angles), (1, 4))
    sine = jnp.sin(angles)
    sine = jnp.tile(jnp.concatenate([-sine, sine], axis=1), (1, 2))
    pairs = block_order.reshape(chips, 2)
    own_place = lax.dynamic_index_in_dim(pairs, core, 1, keepdims=False)
    other_place = lax.dynamic_index_in_dim(pairs, 1 - core, 1, keepdims=False)
    place = jnp.concatenate([own_place, other_place])
    rank = jnp.sum((own_place[None, :] < own_place[:, None]).astype(jnp.int32), axis=1)
    taken = chips // sharers
    wanted = share * taken + jnp.arange(taken, dtype=jnp.int32)
    chosen = (rank[None, :] == wanted[:, None]).astype(jnp.int32)
    order = jnp.sum(chosen * jnp.arange(chips, dtype=jnp.int32)[None, :], axis=1)
    sorted_place = jnp.sum(chosen * own_place[None, :], axis=1).reshape(-1, QUERY_TILE // BLOCK)
    first_token = sorted_place[:, 0] * BLOCK
    last_token = sorted_place[:, -1] * BLOCK + BLOCK - 1
    begins = jnp.max(jnp.where(ends[None, :] <= first_token[:, None], ends[None, :], 0), axis=1)
    finish = jnp.min(jnp.where(ends[None, :] > last_token[:, None], ends[None, :], tokens), axis=1)
    low = begins // KEY_TILE
    high = (finish + KEY_TILE - 1) // KEY_TILE
    gains = jnp.concatenate([query_gain, key_gain])[None, :]

    tables = (hot, mask, cosine, sine, place, order, low, high, own_qkv)
    gathered, where, cotangent_mine, tables = chip_gather(inputs, cotangent, tables)
    hot, mask, cosine, sine, place, order, low, high, own_qkv = tables

    feed_part = jnp.concatenate([expand_part, down_weight], axis=0)
    gathered, out_full, feed_part = lax.optimization_barrier((gathered, out_full, feed_part))
    feed_own = lax.all_gather(feed_part[None], "bz", axis=0, tiled=True)
    cotangent_plane = (cotangent_mine, swap(cotangent_mine, "core"))

    normed_low, raw, query, own_kv = project(
        where, gathered, attn_gain[None], own_qkv, cosine, sine, gains, hot
    )
    other_kv = swap(own_kv, "core")
    kept, attended = attend(order, place, low, high, query, own_kv, other_kv, mask)
    parts = lax.all_to_all(attended.reshape(chips, BLOCK, HD), CHIPS, 0, 0, tiled=True)
    parts = over_sharers(parts, sharers)
    merged, middle, second, squares = out_project(parts, inputs, out_full, ffn_gain[None])
    second_plane = plane_gather(second)

    ffn_mine, ffn_other, back_mine, back_other, feed_grad = feed(
        second_plane, cotangent_plane, feed_own, hidden_rows
    )
    feed_grad = lax.psum_scatter(feed_grad, "bz", scatter_dimension=0, tiled=True)[0]
    ffn_mine, late_qkv = lax.optimization_barrier(
        (ffn_mine, by_head.transpose(0, 2, 1, 3).reshape(rows, 3 * D))
    )
    qkv_full = lax.all_gather(late_qkv, DEVICES, axis=0, tiled=True)
    grad_middle, branch_grad, to_chips, grad_ffn = middle_back(
        *plane_scatter(back_mine, back_other), middle, cotangent, ffn_gain[None], out_full
    )
    grad_attended = lax.all_to_all(jnp.repeat(to_chips, sharers, axis=0), CHIPS, 0, 0, tiled=True)
    grad_attended = grad_attended.reshape(-1, HD)

    joined_mine, joined_other = out_grad(
        jnp.stack(plane_members()), merged, branch_grad, ffn_mine, ffn_other, depth
    )
    joined = joined_mine.astype(f32) + swap(joined_other, "core").astype(f32)
    joined = joined.reshape(4, BLOCK, 2 * D)
    to_x = jnp.concatenate([joined[1], joined[3]], axis=0).astype(bf16)
    grad_attended, to_x = lax.optimization_barrier((grad_attended, to_x))
    from_x = swap(to_x, "hx")

    query_grad, own_grad, other_grad, bias_grad = attend_back(
        order, place, low, high, query, own_kv, other_kv, mask, hot, kept, grad_attended
    )
    query_grad, from_x, feed_grad = lax.optimization_barrier((query_grad, from_x, feed_grad))
    from_x = from_x.astype(f32)
    from_y = swap((joined[2] + from_x[BLOCK:]).astype(bf16), "by")
    expand_grad = lax.all_to_all(
        feed_grad[: 8 * rows].reshape(8, rows, -1), PLANE, 0, 0, tiled=True
    )
    grad_project, grad_qkv_part, gain_grad, attn_grad = project_back(
        query_grad,
        own_grad,
        swap(other_grad, "core"),
        raw,
        cosine,
        sine,
        gains,
        normed_low,
        own_qkv,
    )
    grad_qkv_part, from_y, expand_grad = lax.optimization_barrier(
        (grad_qkv_part, from_y, expand_grad)
    )
    joined = joined[0] + from_x[:BLOCK] + from_y.astype(f32)
    ffn_branch = joined[:, :D]
    outputs = (middle + ffn_branch).astype(bf16)
    grad_out = lax.psum_scatter(joined[:, D:].astype(bf16), "bz", scatter_dimension=0, tiled=True)
    grad_out = grad_out.astype(f32)
    grad_qkv_part = grad_qkv_part.reshape(chips, 2, rows, 3 * HD)
    grad_qkv_own = lax.dynamic_index_in_dim(grad_qkv_part, core, 1, keepdims=False)
    grad_qkv_other = lax.dynamic_index_in_dim(grad_qkv_part, 1 - core, 1, keepdims=False)
    grad_qkv_own = grad_qkv_own.astype(f32) + swap(grad_qkv_other, "core").astype(f32)
    joined = jnp.concatenate(
        [grad_project.reshape(chips, BLOCK, 3 * HD), grad_qkv_own.astype(bf16)], axis=1
    )

    bias_part = jnp.where(
        jnp.arange(H)[None, :] == head, bias_grad[0, :2][:, None], jnp.zeros((2, H), f32)
    )
    packed = jnp.concatenate(
        [
            attn_grad[:, 0] / attn_gain,
            grad_ffn[0],
            gain_grad[0],
            bias_part.reshape(-1),
            squares[:2, 0],
            jnp.sum(ffn_branch * ffn_branch)[None],
            jnp.zeros((93,), f32),
        ]
    )
    joined, packed = lax.optimization_barrier((joined, packed))
    joined = lax.all_to_all(joined, CHIPS, 0, 0, tiled=True)
    summed = sum_everywhere(packed.reshape(-1, 128))
    grad_down = feed_grad[8 * rows :].astype(f32)
    grad_expand = widen(expand_grad, depth, hidden_rows)
    joined, summed, grad_down, grad_expand = lax.optimization_barrier(
        (joined, summed, grad_down, grad_expand)
    )
    joined = over_sharers(joined, sharers)
    grad_inputs, grad_qkv = input_back(joined, qkv_full, inputs, attn_gain[None], grad_middle)
    summed = summed.reshape(-1)
    at = 2 * D + 2 * HD
    root_means = jnp.sqrt(summed[at + 2 * H : at + 2 * H + 3] / (tokens * D))
    return (
        outputs,
        grad_inputs,
        grad_qkv,
        grad_out,
        grad_expand,
        grad_down,
        summed[:D],
        summed[D : 2 * D],
        summed[2 * D : 2 * D + HD],
        summed[2 * D + HD : at],
        summed[at : at + 2 * H].reshape(2, H),
        root_means,
    )


def solution(mesh):
    grid = mesh.devices if mesh.axis_names == ("head", "blk") else mesh.devices.T
    heads, blks = grid.shape
    mesh = Mesh(grid.reshape(heads // 2, 2, blks // 2, 2), ("hx", "core", "bz", "by"))
    split = P(DEVICES, None)

    return jax.shard_map(
        body,
        mesh=mesh,
        in_specs=(split,) * 2 + (P(),) * 5 + (split,) * 4 + (P(),) * 3,
        out_specs=(split,) * 6 + (P(),) * 6,
        check_vma=False,
    )
```

```python
from functools import partial

import jax
import jax.numpy as jnp
from jax import lax
from jax.experimental import pallas as pl
from jax.experimental.pallas import tpu as pltpu
from jax.sharding import Mesh
from jax.sharding import PartitionSpec as P


D = 1024
H = 16
HD = 64
BLOCK = 128
NVAR = 4
EPSILON = 1e-05
THETA = 10000.0

DEVICES = ("bz", "by", "hx", "core")
CHIPS = ("bz", "by", "hx")
PLANE = ("by", "hx", "core")

SEGMENT_LANE = 64
VARIATE_LANE = 76
OWN_VARIATE_LANE = 88
MASK = -512.0
QUERY_TILE = 512
KEY_TILE = 512
PROJECT_BLOCKS = 4

bf16 = jnp.bfloat16
f32 = jnp.float32


def dot(left, right, dims):
    return lax.dot_general(left, right, (dims, ((), ())), preferred_element_type=f32)


def norm_rows(values, gain):
    factor = lax.rsqrt(jnp.mean(values * values, axis=-1, keepdims=True) + EPSILON)
    return values * factor * gain


def norm_back(values, gain, grad):
    factor = lax.rsqrt(jnp.mean(values * values, axis=-1, keepdims=True) + EPSILON)
    scaled = grad * gain
    inner = jnp.mean(scaled * values, axis=-1, keepdims=True)
    grad_values = factor * (scaled - values * (factor * factor) * inner)
    return grad_values, grad * values * factor


def swap(shard, axis):
    return lax.ppermute(shard, axis, [(0, 1), (1, 0)])


def plane_gather(shard):
    mine = jnp.concatenate(quarters(shard), axis=0)
    return mine, swap(mine, "core")


def chip_gather(shard, rider, late):
    depth = lax.axis_size("bz")
    chips = depth * 4
    z, y, x = lax.axis_index("bz"), lax.axis_index("by"), lax.axis_index("hx")
    at = jnp.arange(chips, dtype=jnp.int32)
    if depth > 4:
        pieces = lax.all_gather(shard, CHIPS, axis=0)
        return list(pieces), at, (swap(rider, "hx"), swap(rider, "by")), late
    column = [
        lax.ppermute(shard, "bz", [(i, (i + by) % depth) for i in range(depth)])
        for by in range(1, depth)
    ]
    across_x, across_y = [swap(shard, "hx")], [swap(shard, "by")]
    across_x += [swap(piece, "hx") for piece in column]
    across_y += [swap(piece, "by") for piece in column]
    across_x, across_y, late = lax.optimization_barrier((across_x, across_y, late))
    corner = [swap(across_x[i], "by") if i > 1 else swap(across_y[i], "hx") for i in range(depth)]
    riders = swap(rider, "hx"), swap(rider, "by")
    pieces = [shard, across_x[0], across_y[0], corner[0]]
    pieces += column + across_x[1:] + across_y[1:] + corner[1:]
    back = (z - at // 4) % depth
    flips = ((at % 2) ^ x) + 2 * (((at // 2) % 2) ^ y)
    where = jnp.where(back == 0, flips, 4 + flips * (depth - 1) + back - 1).astype(jnp.int32)
    return pieces, where, riders, late


def sum_everywhere(values):
    for axis in ("core", "hx", "by"):
        values = values + swap(values, axis)
    depth = lax.axis_size("bz")
    step = 1
    while step < depth:
        values = values + lax.ppermute(values, "bz", [(i, i ^ step) for i in range(depth)])
        step *= 2
    return values


def quarters(shard):
    half = shard.shape[0] // 2
    across_x = swap(shard, "hx")
    across_y = swap(shard, "by")
    return [shard, across_x, across_y, swap(across_y[:half], "hx"), swap(across_x[half:], "by")]


def plane_scatter(mine, other):
    rows = mine.shape[0] // 4
    half = rows // 2
    mine = mine.astype(f32) + swap(other, "core").astype(f32)
    corner = mine[3 * rows :].astype(bf16)
    for_y = swap(corner[:half], "hx").astype(f32)
    for_x = swap(corner[half:], "by").astype(f32)
    to_x = mine[rows : 2 * rows]
    to_y = mine[2 * rows : 3 * rows]
    to_x = jnp.concatenate([to_x[:half], to_x[half:] + for_x], axis=0).astype(bf16)
    to_y = jnp.concatenate([to_y[:half] + for_y, to_y[half:]], axis=0).astype(bf16)
    from_x = swap(to_x, "hx")
    from_y = swap(to_y, "by")
    return mine[:rows], from_x, from_y


def plane_members():
    by, hx, core = lax.axis_index("by"), lax.axis_index("hx"), lax.axis_index("core")
    members = []
    for core_flip in (0, 1):
        for x_flip, y_flip in ((0, 0), (1, 0), (0, 1), (1, 1)):
            members.append((by ^ y_flip) * 4 + (hx ^ x_flip) * 2 + (core ^ core_flip))
    return members


def lanes(shape):
    return lax.broadcasted_iota(jnp.int32, shape, len(shape) - 1)


def half_mean(values, lane):
    low = jnp.sum(jnp.where(lane < HD, values, 0.0), axis=-1, keepdims=True)
    high = jnp.sum(jnp.where(lane < HD, 0.0, values), axis=-1, keepdims=True)
    return jnp.where(lane < HD, low, high) * (1.0 / HD)


def swap_halves(values, lane):
    return jnp.where(
        (lane & (HD - 1)) < HD // 2, pltpu.roll(values, 96, 1), pltpu.roll(values, 32, 1)
    )


def project_kernel(where_ref, *refs, chips):
    piece_refs, refs = refs[:chips], refs[chips:]
    gain_ref, weight_ref, cosine_ref, sine_ref, gains_ref, hot_ref, mask_ref = refs[:7]
    normed_ref, raw_ref, query_ref, kv_ref, out_ref, x_ref, arrived = refs[7:]
    step = pl.program_id(0)

    @pl.when(step == 0)
    def _():
        copies = [
            pltpu.make_async_copy(piece_refs[i], x_ref.at[i], arrived.at[i]) for i in range(chips)
        ]
        for copy in copies:
            copy.start()
        for copy in copies:
            copy.wait()

    places = [where_ref[step * PROJECT_BLOCKS + i] for i in range(PROJECT_BLOCKS)]
    for i, place in enumerate(places):
        out_ref[i] = x_ref[place, BLOCK:]
    x = jnp.concatenate([x_ref[place, :BLOCK] for place in places], axis=0).astype(f32)
    normed = norm_rows(x, gain_ref[...]).astype(bf16)
    normed_ref[...] = normed
    project = dot(normed, weight_ref[...], ((1,), (0,)))
    both = project[:, : 2 * HD]
    value = project[:, 2 * HD :]
    raw_ref[...] = both
    lane = lanes(both.shape)
    scaled = both * lax.rsqrt(half_mean(both * both, lane) + EPSILON) * gains_ref[...]
    turned = scaled * cosine_ref[...] + swap_halves(scaled, lane) * sine_ref[...]
    turned = turned.astype(bf16).astype(f32)
    query_ref[...] = jnp.where(lane < HD, turned, hot_ref[...].astype(f32)).astype(bf16)
    key = pltpu.roll(turned * HD ** (-0.5), HD, 1)
    ones = jnp.where((lane >= HD) & (lane < HD + 3), 1.0, 0.0)
    kv_ref[:, :128] = jnp.where(lane < HD, key, mask_ref[...].astype(f32)).astype(bf16)
    kv_ref[:, 128:] = jnp.where(lane < HD, value, ones).astype(bf16)


def project(where, pieces, gain, weight, cosine, sine, gains, hot, mask):
    blocks = len(pieces)
    rows = blocks * BLOCK
    step_rows = PROJECT_BLOCKS * BLOCK
    out_rows = pieces[0].shape[0] - BLOCK
    row_spec = lambda width: pl.BlockSpec((step_rows, width), lambda j, *unused: (j, 0))
    whole = lambda array: pl.BlockSpec(array.shape, lambda j, *unused: (0, 0))
    anywhere = pl.BlockSpec(memory_space=pl.ANY)
    tables = [whole(gain), whole(weight), row_spec(128), row_spec(128), whole(gains)]
    return pl.pallas_call(
        partial(project_kernel, chips=blocks),
        grid_spec=pltpu.PrefetchScalarGridSpec(
            num_scalar_prefetch=1,
            grid=(blocks // PROJECT_BLOCKS,),
            in_specs=[anywhere] * blocks + tables + [row_spec(128), row_spec(128)],
            out_specs=[
                row_spec(D),
                row_spec(128),
                row_spec(128),
                row_spec(256),
                pl.BlockSpec((PROJECT_BLOCKS, out_rows, D), lambda j, *unused: (j, 0, 0)),
            ],
            scratch_shapes=[
                pltpu.VMEM((blocks, BLOCK + out_rows, D), bf16),
                pltpu.SemaphoreType.DMA((blocks,)),
            ],
        ),
        out_shape=[
            jax.ShapeDtypeStruct((rows, D), bf16),
            jax.ShapeDtypeStruct((rows, 128), f32),
            jax.ShapeDtypeStruct((rows, 128), bf16),
            jax.ShapeDtypeStruct((rows, 256), bf16),
            jax.ShapeDtypeStruct((blocks, out_rows, D), bf16),
        ],
        name="project",
    )(where, *pieces, gain, weight, cosine, sine, gains, hot, mask)


def sort_keys(place_ref, own_ref, other_ref, keys_ref):
    blocks = own_ref.shape[0] // BLOCK
    for half, source_ref in ((0, own_ref), (1, other_ref)):

        def put(j, unused, half=half, source_ref=source_ref):
            source = pl.multiple_of(j * BLOCK, BLOCK)
            target = pl.multiple_of(place_ref[half * blocks + j] * BLOCK, BLOCK)
            keys_ref[pl.ds(target, BLOCK), :] = source_ref[pl.ds(source, BLOCK), :]
            return unused

        lax.fori_loop(0, blocks, put, 0, unroll=4)


def block_start(order_ref, index):
    return pl.multiple_of(order_ref[index] * BLOCK, BLOCK)


def attend_kernel(
    order_ref,
    place_ref,
    low_ref,
    high_ref,
    query_ref,
    own_ref,
    other_ref,
    kept_ref,
    attended_ref,
    keys_ref,
):
    tile = pl.program_id(0)
    count = QUERY_TILE // BLOCK

    @pl.when(tile == 0)
    def _():
        sort_keys(place_ref, own_ref, other_ref, keys_ref)
        if order_ref.shape[0] * BLOCK != query_ref.shape[0]:
            kept_ref[...] = jnp.zeros_like(kept_ref)
            attended_ref[...] = jnp.zeros_like(attended_ref)

    starts = [block_start(order_ref, tile * count + i) for i in range(count)]
    query = jnp.concatenate([query_ref[pl.ds(start, BLOCK), :] for start in starts], axis=0)

    def chunk(index, accumulated):
        window = pl.ds(pl.multiple_of(index * KEY_TILE, KEY_TILE), KEY_TILE)
        expo = jnp.exp(dot(query, keys_ref[window, :128], ((1,), (1,))))
        return accumulated + dot(expo.astype(bf16), keys_ref[window, 128:], ((1,), (0,)))

    accumulated = lax.fori_loop(
        low_ref[tile], high_ref[tile], chunk, jnp.zeros((QUERY_TILE, 128), f32)
    )
    totals = accumulated[:, HD : HD + 1]
    lane = lanes(accumulated.shape)
    kept = jnp.where(lane < HD, accumulated / totals, totals)
    for i, start in enumerate(starts):
        piece = kept[i * BLOCK : (i + 1) * BLOCK]
        kept_ref[pl.ds(start, BLOCK), :] = piece
        attended_ref[order_ref[tile * count + i]] = piece.T[:HD].astype(bf16)


def fixed(array):
    return pl.BlockSpec(
        array.shape, lambda *unused: (0,) * len(array.shape), pipeline_mode=pl.Buffered(1)
    )


def attend(order, place, low, high, query, own, other):
    rows = query.shape[0]
    operands = (query, own, other)
    outs = (
        jax.ShapeDtypeStruct((rows, 128), f32),
        jax.ShapeDtypeStruct((rows // BLOCK, HD, BLOCK), bf16),
    )
    return pl.pallas_call(
        attend_kernel,
        grid_spec=pltpu.PrefetchScalarGridSpec(
            num_scalar_prefetch=4,
            grid=(low.shape[0],),
            in_specs=[fixed(array) for array in operands],
            out_specs=[fixed(array) for array in outs],
            scratch_shapes=[pltpu.VMEM((2 * rows, 256), bf16)],
        ),
        out_shape=list(outs),
        name="attend",
    )(order, place, low, high, *operands)


def attend_back_kernel(
    order_ref,
    place_ref,
    source_ref,
    low_ref,
    high_ref,
    query_ref,
    own_ref,
    other_ref,
    kept_ref,
    grad_ref,
    query_grad_ref,
    own_grad_ref,
    other_grad_ref,
    bias_ref,
    keys_ref,
    sorted_ref,
    wide_ref,
    sums_ref,
    every_ref,
    same_ref,
):
    step = pl.program_id(0)
    own_rows = own_ref.shape[0]
    taken = order_ref.shape[0]

    @pl.when(step == 0)
    def _():
        sort_keys(place_ref, own_ref, other_ref, keys_ref)
        every_ref[...] = jnp.zeros_like(every_ref)
        same_ref[...] = jnp.zeros_like(same_ref)
        sums_ref[...] = jnp.zeros_like(sums_ref)
        if taken * BLOCK != own_rows:
            query_grad_ref[...] = jnp.zeros_like(query_grad_ref)
        lane = lanes((BLOCK, 128))

        def put(i, unused):
            source = pl.ds(block_start(order_ref, i), BLOCK)
            target = pl.ds(pl.multiple_of(i * BLOCK, BLOCK), BLOCK)
            sorted_ref[target, :] = query_ref[source, :]
            kept = kept_ref[source, :]
            grad = grad_ref[order_ref[i]].astype(f32)
            grad = jnp.concatenate([grad, jnp.zeros_like(grad)], axis=0).T
            inverse = 1.0 / kept[:, HD : HD + 1]
            center = jnp.sum(grad * kept, axis=1, keepdims=True) * inverse
            center_high = center.astype(bf16).astype(f32)
            center_rest = center - center_high
            center_mid = center_rest.astype(bf16).astype(f32)
            center_low = center_rest - center_mid
            wide = jnp.where(lane == HD, -center_high, 0.0)
            wide = jnp.where(lane == HD + 1, -center_mid, wide)
            wide = jnp.where(lane == HD + 2, -center_low, wide)
            wide_ref[target, :] = jnp.where(lane < HD, grad * inverse, wide).astype(bf16)
            return unused

        lax.fori_loop(0, taken, put, 0, unroll=4)

    window = pl.ds(pl.multiple_of(step * KEY_TILE, KEY_TILE), KEY_TILE)
    key = keys_ref[window, :128]
    value = keys_ref[window, 128:]

    def tile(index, grads):
        rows = pl.ds(pl.multiple_of(index * QUERY_TILE, QUERY_TILE), QUERY_TILE)
        query = sorted_ref[rows, :]
        wide = wide_ref[rows, :]
        expo = jnp.exp(dot(key, query, ((1,), (1,))))
        score_low = (expo * dot(value, wide, ((1,), (1,)))).astype(bf16)
        sums_ref[rows, :] += dot(score_low, key, ((0,), (0,)))
        return (
            grads[0] + dot(score_low, query, ((1,), (0,))),
            grads[1] + dot(expo.astype(bf16), wide, ((1,), (0,))),
        )

    empty = jnp.zeros((KEY_TILE, 128), f32)
    key_grad, value_grad = lax.fori_loop(low_ref[step], high_ref[step], tile, (empty, empty))
    lane = lanes(key_grad.shape)
    joined = jnp.where(lane < HD, value_grad, pltpu.roll(key_grad, HD, 1) * HD ** (-0.5))
    joined = joined.astype(bf16)
    for i in range(KEY_TILE // BLOCK):
        source = source_ref[step * (KEY_TILE // BLOCK) + i] * BLOCK
        piece = joined[i * BLOCK : (i + 1) * BLOCK]

        @pl.when(source < own_rows)
        def _(source=source, piece=piece):
            own_grad_ref[pl.ds(pl.multiple_of(source, BLOCK), BLOCK), :] = piece

        @pl.when(source >= own_rows)
        def _(source=source, piece=piece):
            other_grad_ref[pl.ds(pl.multiple_of(source - own_rows, BLOCK), BLOCK), :] = piece

    every = jnp.where((lane >= VARIATE_LANE) & (lane < VARIATE_LANE + NVAR), key_grad, 0.0)
    shift = 128 + VARIATE_LANE - OWN_VARIATE_LANE
    same = every * pltpu.roll(key.astype(f32), shift, 1)
    every_ref[...] += jnp.sum(every.reshape(-1, 8, 128), axis=0)
    same_ref[...] += jnp.sum(same.reshape(-1, 8, 128), axis=0)

    @pl.when(step == pl.num_programs(0) - 1)
    def _():
        def put(i, unused):
            target = pl.ds(block_start(order_ref, i), BLOCK)
            rows = pl.ds(pl.multiple_of(i * BLOCK, BLOCK), BLOCK)
            query_grad_ref[target, :] = sums_ref[rows, :].astype(bf16)
            return unused

        lax.fori_loop(0, taken, put, 0, unroll=4)
        every = jnp.sum(every_ref[...], keepdims=True)
        same = jnp.sum(same_ref[...], keepdims=True)
        bias_lane = lanes((8, 128))
        bias_ref[...] = jnp.where(
            bias_lane == 0, every - same, jnp.where(bias_lane == 1, same, 0.0)
        )


def attend_back(order, place, source, low, high, query, own, other, kept, grad):
    rows = query.shape[0]
    taken = order.shape[0] * BLOCK
    operands = (query, own, other, kept, grad)
    outs = tuple(jax.ShapeDtypeStruct((rows, 128), bf16) for _ in range(3)) + (
        jax.ShapeDtypeStruct((8, 128), f32),
    )
    return pl.pallas_call(
        attend_back_kernel,
        grid_spec=pltpu.PrefetchScalarGridSpec(
            num_scalar_prefetch=5,
            grid=(low.shape[0],),
            in_specs=[fixed(array) for array in operands],
            out_specs=[fixed(array) for array in outs],
            scratch_shapes=[
                pltpu.VMEM((2 * rows, 256), bf16),
                pltpu.VMEM((taken, 128), bf16),
                pltpu.VMEM((taken, 128), bf16),
                pltpu.VMEM((taken, 128), f32),
                pltpu.VMEM((8, 128), f32),
                pltpu.VMEM((8, 128), f32),
            ],
        ),
        out_shape=list(outs),
        name="attend_back",
    )(order, place, source, low, high, *operands)


def project_back_kernel(
    query_grad_ref,
    own_ref,
    other_ref,
    raw_ref,
    cosine_ref,
    sine_ref,
    gains_ref,
    normed_ref,
    forward_ref,
    grad_ref,
    weight_grad_ref,
    gain_grad_ref,
    attn_grad_ref,
    weight_ref,
    gain_ref,
):
    step = pl.program_id(0)

    @pl.when(step == 0)
    def _():
        weight_ref[...] = jnp.zeros_like(weight_ref)
        gain_ref[...] = jnp.zeros_like(gain_ref)

    kv_grad = own_ref[...].astype(f32) + other_ref[...].astype(f32)
    kv_grad = kv_grad.astype(bf16).astype(f32)
    lane = lanes(kv_grad.shape)
    turned = jnp.where(lane < HD, query_grad_ref[...].astype(f32), kv_grad)
    grad = turned * cosine_ref[...] - swap_halves(turned, lane) * sine_ref[...]
    raw = raw_ref[...]
    factor = lax.rsqrt(half_mean(raw * raw, lane) + EPSILON)
    scaled = grad * gains_ref[...]
    inner = half_mean(scaled * raw, lane)
    both = (factor * (scaled - raw * (factor * factor) * inner)).astype(bf16)
    gain_ref[...] += jnp.sum(grad * raw * factor, axis=0, keepdims=True)
    value = jnp.where(lane < HD, kv_grad, 0.0).astype(bf16)
    full = jnp.concatenate([both, value], axis=1)
    grad_ref[...] = full[:, : 3 * HD]
    weight_ref[...] += dot(normed_ref[...], full, ((0,), (0,)))

    @pl.when(step == pl.num_programs(0) - 1)
    def _():
        weight_grad_ref[...] = weight_ref[:, : 3 * HD].astype(bf16)
        gain_grad_ref[...] = jnp.broadcast_to(gain_ref[...], gain_grad_ref.shape)
        forward = forward_ref[...].astype(f32)
        attn = jnp.sum(weight_ref[...] * forward, axis=1, keepdims=True)
        attn_grad_ref[...] = jnp.broadcast_to(attn, attn_grad_ref.shape)


def project_back(query_grad, own, other, raw, cosine, sine, gains, normed, forward):
    rows = query_grad.shape[0]
    step_rows = 4 * BLOCK
    row_spec = lambda width: pl.BlockSpec((step_rows, width), lambda j: (j, 0))
    whole = lambda shape: pl.BlockSpec(shape, lambda j: (0, 0))
    return pl.pallas_call(
        project_back_kernel,
        grid=(rows // step_rows,),
        in_specs=[row_spec(128)] * 6 + [whole(gains.shape), row_spec(D), whole(forward.shape)],
        out_specs=[row_spec(3 * HD), whole((D, 3 * HD)), whole((8, 128)), whole((D, 128))],
        out_shape=[
            jax.ShapeDtypeStruct((rows, 3 * HD), bf16),
            jax.ShapeDtypeStruct((D, 3 * HD), bf16),
            jax.ShapeDtypeStruct((8, 128), f32),
            jax.ShapeDtypeStruct((D, 128), f32),
        ],
        scratch_shapes=[pltpu.VMEM((D, 4 * HD), f32), pltpu.VMEM((1, 128), f32)],
        name="project_back",
    )(query_grad, own, other, raw, cosine, sine, gains, normed, forward)


def feed_kernel(
    second_mine_ref,
    second_other_ref,
    grad_mine_ref,
    grad_other_ref,
    weight_ref,
    ffn_mine_ref,
    ffn_other_ref,
    back_mine_ref,
    back_other_ref,
    weight_grad_ref,
    expand_ref,
    down_ref,
    expand_grad_ref,
    down_grad_ref,
):
    step = pl.program_id(0)
    half = pl.num_programs(0) // 2
    depth, both_rows, width = weight_ref.shape
    down_rows = down_ref.shape[0] // depth
    expand_rows = both_rows - down_rows

    @pl.when(step == 0)
    def _():
        for z in range(depth):
            expand_ref[z * expand_rows : (z + 1) * expand_rows] = weight_ref[z, :expand_rows]
            down_ref[z * down_rows : (z + 1) * down_rows] = weight_ref[z, expand_rows:]
        expand_grad_ref[...] = jnp.zeros_like(expand_grad_ref)
        down_grad_ref[...] = jnp.zeros_like(down_grad_ref)

    second = jnp.where(step < half, second_mine_ref[...], second_other_ref[...])
    grad = jnp.where(step < half, grad_mine_ref[...], grad_other_ref[...])
    expand = dot(second, expand_ref[...], ((1,), (0,)))
    gate = expand[:, : width // 2]
    up = expand[:, width // 2 :]
    sigmoid = 1.0 / (1.0 + jnp.exp(-gate))
    silu = gate * sigmoid
    hidden = (silu * up).astype(bf16)
    grad_hidden = dot(grad, down_ref[...], ((1,), (1,)))
    grad_gate = grad_hidden * up * (sigmoid * (1.0 + gate * (1.0 - sigmoid)))
    rows = jnp.concatenate([grad_gate, grad_hidden * silu], axis=1).astype(bf16)
    ffn = dot(hidden, down_ref[...], ((1,), (0,))).astype(bf16)
    back = dot(rows, expand_ref[...], ((1,), (1,))).astype(bf16)
    expand_grad_ref[...] += dot(second, rows, ((0,), (0,)))
    down_grad_ref[...] += dot(hidden, grad, ((0,), (0,)))

    @pl.when(step < half)
    def _():
        ffn_mine_ref[...] = ffn
        back_mine_ref[...] = back

    @pl.when(step >= half)
    def _():
        ffn_other_ref[...] = ffn
        back_other_ref[...] = back

    @pl.when(step == pl.num_programs(0) - 1)
    def _():
        for z in range(depth):
            weight_grad_ref[z, :expand_rows] = expand_grad_ref[
                z * expand_rows : (z + 1) * expand_rows
            ].astype(bf16)
            weight_grad_ref[z, expand_rows:] = down_grad_ref[
                z * down_rows : (z + 1) * down_rows
            ].astype(bf16)


def feed(second, grad, weight, down_rows):
    rows = second[0].shape[0]
    tile = 256
    steps = rows // tile
    depth, both_rows, width = weight.shape
    mine = pl.BlockSpec((tile, D), lambda i: (jnp.minimum(i, steps - 1), 0))
    other = pl.BlockSpec((tile, D), lambda i: (jnp.maximum(i - steps, 0), 0))
    whole = pl.BlockSpec(weight.shape, lambda i: (0, 0, 0), pipeline_mode=pl.Buffered(1))
    token_rows = jax.ShapeDtypeStruct((rows, D), bf16)
    return pl.pallas_call(
        feed_kernel,
        grid=(2 * steps,),
        in_specs=[mine, other, mine, other, whole],
        out_specs=[mine, other, mine, other, whole],
        out_shape=[token_rows] * 4 + [jax.ShapeDtypeStruct(weight.shape, bf16)],
        scratch_shapes=[
            pltpu.VMEM((depth * (both_rows - down_rows), width), bf16),
            pltpu.VMEM((depth * down_rows, D), bf16),
            pltpu.VMEM((depth * (both_rows - down_rows), width), f32),
            pltpu.VMEM((depth * down_rows, D), f32),
        ],
        name="feed",
    )(*second, *grad, weight)


def out_kernel(parts_ref, x_ref, weight_ref, gain_ref, middle_ref, second_ref, squares_ref):
    branch = dot(parts_ref[...], weight_ref[...], ((0,), (0,)))
    x = x_ref[...].astype(f32)
    middle = x + branch
    middle_ref[...] = middle
    second_ref[...] = norm_rows(middle, gain_ref[...]).astype(bf16)
    row = lax.broadcasted_iota(jnp.int32, squares_ref.shape, 0)
    x_sum = jnp.sum(x * x, keepdims=True)
    branch_sum = jnp.sum(branch * branch, keepdims=True)
    squares_ref[...] = jnp.where(row == 0, x_sum, branch_sum)


def out_project(parts, x, weight, gain):
    rows = x.shape[0]
    return pl.pallas_call(
        out_kernel,
        out_shape=[
            jax.ShapeDtypeStruct((rows, D), f32),
            jax.ShapeDtypeStruct((rows, D), bf16),
            jax.ShapeDtypeStruct((8, 128), f32),
        ],
        name="out_project",
    )(parts, x, weight, gain)


def middle_back_kernel(
    own_ref,
    from_x_ref,
    from_y_ref,
    middle_ref,
    cotangent_ref,
    gain_ref,
    weight_ref,
    grad_middle_ref,
    branch_ref,
    parts_ref,
    gain_grad_ref,
):
    grad_second = own_ref[...] + from_x_ref[...].astype(f32) + from_y_ref[...].astype(f32)
    grad_middle, gain_rows = norm_back(middle_ref[...], gain_ref[...], grad_second)
    grad_middle = cotangent_ref[...].astype(f32) + grad_middle
    grad_middle_ref[...] = grad_middle
    branch = grad_middle.astype(bf16)
    branch_ref[...] = branch
    parts_ref[...] = dot(weight_ref[...], branch, ((1,), (1,))).astype(bf16)
    gain_grad_ref[...] = jnp.broadcast_to(
        jnp.sum(gain_rows, axis=0, keepdims=True), gain_grad_ref.shape
    )


def middle_back(own, from_x, from_y, middle, cotangent, gain, weight):
    rows = middle.shape[0]
    return pl.pallas_call(
        middle_back_kernel,
        out_shape=[
            jax.ShapeDtypeStruct((rows, D), f32),
            jax.ShapeDtypeStruct((rows, D), bf16),
            jax.ShapeDtypeStruct((D, rows), bf16),
            jax.ShapeDtypeStruct((8, D), f32),
        ],
        name="middle_back",
    )(own, from_x, from_y, middle, cotangent, gain, weight)


def out_grad_kernel(
    members_ref,
    merged_ref,
    branch_ref,
    ffn_mine_ref,
    ffn_other_ref,
    mine_ref,
    other_ref,
    grad_ref,
    depth,
):
    shard = mine_ref.shape[0] // 4
    rows = shard // depth
    grad_ref[...] = dot(merged_ref[...], branch_ref[...], ((1,), (0,)))
    mine_ref[:, :D] = ffn_mine_ref[...]
    other_ref[:, :D] = ffn_other_ref[...]
    for place in range(8):
        target_ref = mine_ref if place < 4 else other_ref
        for z in range(depth):
            source = pl.multiple_of((z * 8 + members_ref[place]) * rows, rows)
            target = (place % 4) * shard + z * rows
            target_ref[target : target + rows, D:] = grad_ref[pl.ds(source, rows), :].astype(bf16)


def out_grad(members, merged, branch, ffn_mine, ffn_other, depth):
    joined = jax.ShapeDtypeStruct((ffn_mine.shape[0], 2 * D), bf16)
    operands = (merged, branch, ffn_mine, ffn_other)
    return pl.pallas_call(
        partial(out_grad_kernel, depth=depth),
        grid_spec=pltpu.PrefetchScalarGridSpec(
            num_scalar_prefetch=1,
            grid=(1,),
            in_specs=[fixed(array) for array in operands],
            out_specs=[fixed(joined), fixed(joined)],
            scratch_shapes=[pltpu.VMEM((D, D), f32)],
        ),
        out_shape=[joined, joined],
        name="out_grad",
    )(members, *operands)


def input_back_kernel(
    joined_ref, weight_ref, x_ref, gain_ref, middle_ref, grad_ref, qkv_ref, wide_ref
):
    heads = joined_ref.shape[0]
    rows = x_ref.shape[0]
    for pair in range(heads // 2):
        left = joined_ref[2 * pair]
        right = joined_ref[2 * pair + 1]
        wide_ref[:, pair * 6 * HD : (pair + 1) * 6 * HD] = jnp.concatenate(
            [left[:rows], right[:rows]], axis=1
        )
        for part in range(3):
            at = part * D + pair * 2 * HD
            window = slice(part * HD, (part + 1) * HD)
            qkv_ref[:, at : at + 2 * HD] = jnp.concatenate(
                [left[rows:, window], right[rows:, window]], axis=1
            ).astype(f32)
    grad_normed = dot(wide_ref[...], weight_ref[...], ((1,), (1,)))
    grad, _ = norm_back(x_ref[...].astype(f32), gain_ref[...], grad_normed)
    grad_ref[...] = middle_ref[...] + grad


def input_back(joined, weight, x, gain, middle):
    rows = x.shape[0]
    return pl.pallas_call(
        input_back_kernel,
        out_shape=[
            jax.ShapeDtypeStruct((rows, D), f32),
            jax.ShapeDtypeStruct((joined.shape[1] - rows, 3 * D), f32),
        ],
        scratch_shapes=[pltpu.VMEM((rows, 3 * D), bf16)],
        name="input_back",
    )(joined, weight, x, gain, middle)


def widen_kernel(parts_ref, grad_ref):
    sources, _, width = parts_ref.shape
    for source in range(sources):
        for at in range(width // 128):
            to = (at * sources + source) * 128
            grad_ref[:, to : to + 128] = parts_ref[source, :, at * 128 : (at + 1) * 128].astype(f32)


def widen(parts, depth, hidden_rows):
    sources, rows, width = parts.shape
    if hidden_rows != 128:
        parts = parts.reshape(sources, rows, 2, depth, hidden_rows)
        return parts.transpose(1, 2, 3, 0, 4).reshape(rows, -1).astype(f32)
    return pl.pallas_call(
        widen_kernel, out_shape=jax.ShapeDtypeStruct((rows, sources * width), f32), name="widen"
    )(parts)


def token_meta(seq_lengths, block_order):
    blocks = block_order.shape[0]
    packed_at = jnp.repeat(block_order, BLOCK) * BLOCK + jnp.tile(
        jnp.arange(BLOCK, dtype=jnp.int32), blocks
    )
    ends = jnp.cumsum(seq_lengths)
    after = packed_at[:, None] >= ends[None, :]
    segment = jnp.sum(after.astype(jnp.int32), axis=1)
    begin = jnp.max(jnp.where(after, ends[None, :], jnp.zeros_like(ends)[None, :]), axis=1)
    return (segment, packed_at - begin, ends)


def own_rows(array, core):
    pairs = array.reshape(-1, 2, BLOCK)
    return lax.dynamic_index_in_dim(pairs, core, 1, keepdims=False).reshape(-1)


def one_hot_rows(segment, variate):
    lane = jnp.arange(128, dtype=jnp.int32)[None, :]
    hot = lane == SEGMENT_LANE + segment[:, None]
    for copy in range(3):
        hot = hot | (lane == VARIATE_LANE + copy * NVAR + variate[:, None])
    return hot.astype(bf16)


def mask_rows(segment, variate, segments, bias):
    lane = jnp.arange(128, dtype=jnp.int32)[None, :]
    here = lane - SEGMENT_LANE
    rows = jnp.where(
        (here >= 0) & (here < segments) & (here != segment[:, None]), jnp.float32(MASK), 0.0
    )
    high = lax.reduce_precision(bias, 8, 7)
    mid = lax.reduce_precision(bias - high, 8, 7)
    low = bias - high - mid
    for copy, part in enumerate((high, mid, low)):
        here = lane - VARIATE_LANE - copy * NVAR
        value = jnp.where(here == variate[:, None], part[1], part[0])
        rows = jnp.where((here >= 0) & (here < NVAR), value, rows)
    rows = jnp.where(lane == OWN_VARIATE_LANE + variate[:, None], 1.0, rows)
    return rows.astype(bf16)


def over_sharers(parts, sharers):
    if sharers == 1:
        return parts
    parts = parts.reshape((H, sharers) + parts.shape[1:]).astype(f32)
    return jnp.sum(parts, axis=1).astype(bf16)


def body(
    inputs,
    cotangent,
    attn_gain,
    ffn_gain,
    query_gain,
    key_gain,
    variate_bias,
    qkv_weight,
    out_weight,
    expand_weight,
    down_weight,
    seq_lengths,
    variate_ids,
    block_order,
):
    depth = lax.axis_size("bz")
    chips = depth * 4
    sharers = chips // H
    core = lax.axis_index("core")
    chip = (lax.axis_index("bz") * 2 + lax.axis_index("by")) * 2 + lax.axis_index("hx")
    head = chip // sharers
    share = chip % sharers
    rows = qkv_weight.shape[0]
    hidden_rows = down_weight.shape[0]
    segments = seq_lengths.shape[0] + 1
    tokens = variate_ids.shape[0]

    by_head = qkv_weight.reshape(rows, 3, H, HD)
    to_heads = jnp.repeat(
        by_head.transpose(2, 0, 1, 3).reshape(H, rows, 3 * HD), 2 * sharers, axis=0
    )
    own_qkv = lax.all_to_all(to_heads, DEVICES, 0, 0, tiled=True)
    own_qkv = jnp.pad(own_qkv.reshape(D, 3 * HD), ((0, 0), (0, HD)))
    to_plane = (
        expand_weight.reshape(rows, 2, depth, 8, hidden_rows)
        .transpose(3, 0, 1, 2, 4)
        .reshape(8, rows, 2 * depth * hidden_rows)
    )
    expand_part = lax.all_to_all(to_plane, PLANE, 0, 0, tiled=True)
    expand_part = expand_part.reshape(8 * rows, -1)

    segment, position, ends = token_meta(seq_lengths, block_order)
    own_segment = own_rows(segment, core)
    own_variate = own_rows(variate_ids, core)
    own_position = own_rows(position, core)
    bias = lax.dynamic_index_in_dim(variate_bias, head, 1, keepdims=False)
    hot = one_hot_rows(own_segment, own_variate)
    mask = mask_rows(own_segment, own_variate, segments, bias)
    freqs = THETA ** (-jnp.arange(HD // 2, dtype=f32) / (HD // 2))
    angles = own_position.astype(f32)[:, None] * freqs[None, :]
    cosine = jnp.tile(jnp.cos(angles), (1, 4))
    sine = jnp.sin(angles)
    sine = jnp.tile(jnp.concatenate([-sine, sine], axis=1), (1, 2))
    pairs = block_order.reshape(chips, 2)
    own_place = lax.dynamic_index_in_dim(pairs, core, 1, keepdims=False)
    other_place = lax.dynamic_index_in_dim(pairs, 1 - core, 1, keepdims=False)
    place = jnp.concatenate([own_place, other_place])
    rank = jnp.sum((own_place[None, :] < own_place[:, None]).astype(jnp.int32), axis=1)
    taken = chips // sharers
    wanted = share * taken + jnp.arange(taken, dtype=jnp.int32)
    chosen = (rank[None, :] == wanted[:, None]).astype(jnp.int32)
    order = jnp.sum(chosen * jnp.arange(chips, dtype=jnp.int32)[None, :], axis=1)
    sorted_place = jnp.sum(chosen * own_place[None, :], axis=1).reshape(-1, QUERY_TILE // BLOCK)
    first_token = sorted_place[:, 0] * BLOCK
    last_token = sorted_place[:, -1] * BLOCK + BLOCK - 1
    begins = jnp.max(jnp.where(ends[None, :] <= first_token[:, None], ends[None, :], 0), axis=1)
    finish = jnp.min(jnp.where(ends[None, :] > last_token[:, None], ends[None, :], tokens), axis=1)
    low = begins // KEY_TILE
    high = (finish + KEY_TILE - 1) // KEY_TILE
    slots = jnp.arange(2 * chips, dtype=jnp.int32)
    source = jnp.sum(
        jnp.where(place[None, :] == slots[:, None], slots[None, :], 0), axis=1, dtype=jnp.int32
    )
    chunks = jnp.arange(tokens // KEY_TILE, dtype=jnp.int32)[:, None]
    low_tile = jnp.sum((high[None, :] <= chunks).astype(jnp.int32), axis=1)
    high_tile = jnp.sum((low[None, :] <= chunks).astype(jnp.int32), axis=1)
    gains = jnp.concatenate([query_gain, key_gain])[None, :]

    late = (hot, mask, cosine, sine, own_qkv, place, order, low, high, source, low_tile, high_tile)
    pieces, where, riders, late = chip_gather(
        jnp.concatenate([inputs, out_weight], axis=0), cotangent, late
    )
    hot, mask, cosine, sine, own_qkv, place, order, low, high, source, low_tile, high_tile = late

    feed_part = jnp.concatenate([expand_part, down_weight], axis=0)
    feed_own = lax.all_gather(feed_part[None], "bz", axis=0, tiled=True)

    normed_low, raw, query, own_kv, out_mine = project(
        where, pieces, attn_gain[None], own_qkv, cosine, sine, gains, hot, mask
    )
    own_kv, riders = lax.optimization_barrier((own_kv, riders))
    other_kv = swap(own_kv, "core")
    rider_corner = swap(riders[0], "by")
    kept, attended = attend(order, place, low, high, query, own_kv, other_kv)
    attended, rider_corner = lax.optimization_barrier((attended, rider_corner))
    cotangent_mine = jnp.concatenate([cotangent, *riders, rider_corner], axis=0)
    cotangent_other = swap(cotangent_mine, "core")
    out_other = swap(out_mine, "core")
    out_full = jnp.stack(
        [jnp.where(core == 0, out_mine, out_other), jnp.where(core == 0, out_other, out_mine)],
        axis=1,
    ).reshape(D, D)
    merged = lax.all_to_all(attended, CHIPS, 0, 0, tiled=True)
    merged, cotangent_other = lax.optimization_barrier((merged, cotangent_other))
    cotangent_plane = (cotangent_mine, cotangent_other)
    merged = over_sharers(merged, sharers).reshape(D, BLOCK)
    middle, second, squares = out_project(merged, inputs, out_full, ffn_gain[None])
    second_plane = plane_gather(second)

    ffn_mine, ffn_other, back_mine, back_other, feed_grad = feed(
        second_plane, cotangent_plane, feed_own, hidden_rows
    )
    feed_grad = lax.psum_scatter(feed_grad, "bz", scatter_dimension=0, tiled=True)
    feed_grad = feed_grad[0]

    qkv_full = lax.all_gather(
        by_head.transpose(0, 2, 1, 3).reshape(rows, 3 * D), DEVICES, axis=0, tiled=True
    )
    grad_middle, branch_grad, to_chips, grad_ffn = middle_back(
        *plane_scatter(back_mine, back_other), middle, cotangent, ffn_gain[None], out_full
    )
    grad_attended = lax.all_to_all(
        jnp.repeat(to_chips.reshape(H, HD, BLOCK), sharers, axis=0), CHIPS, 0, 0, tiled=True
    )

    joined_mine, joined_other = out_grad(
        jnp.stack(plane_members()), merged, branch_grad, ffn_mine, ffn_other, depth
    )
    joined_other = swap(joined_other, "core")
    joined = (joined_mine.astype(f32) + joined_other.astype(f32)).astype(bf16)
    joined = joined.reshape(4, BLOCK, 2 * D)
    to_x = jnp.concatenate([joined[1], joined[3]], axis=0)
    grad_attended, to_x = lax.optimization_barrier((grad_attended, to_x))
    from_x = swap(to_x, "hx")

    query_grad, own_grad, other_grad, bias_grad = attend_back(
        order, place, source, low_tile, high_tile, query, own_kv, other_kv, kept, grad_attended
    )
    query_grad, from_x, feed_grad = lax.optimization_barrier((query_grad, from_x, feed_grad))
    from_x = from_x.astype(f32)
    from_y = swap((joined[2].astype(f32) + from_x[BLOCK:]).astype(bf16), "by")
    expand_grad = lax.all_to_all(
        feed_grad[: 8 * rows].reshape(8, rows, -1), PLANE, 0, 0, tiled=True
    )
    grad_project, grad_qkv_part, gain_grad, attn_grad = project_back(
        query_grad,
        own_grad,
        swap(other_grad, "core"),
        raw,
        cosine,
        sine,
        gains,
        normed_low,
        own_qkv,
    )
    grad_qkv_part, from_y, expand_grad = lax.optimization_barrier(
        (grad_qkv_part, from_y, expand_grad)
    )
    joined = joined[0].astype(f32) + from_x[:BLOCK] + from_y.astype(f32)
    ffn_branch = joined[:, :D]
    outputs = (middle + ffn_branch).astype(bf16)
    grad_out = lax.psum_scatter(joined[:, D:].astype(bf16), "bz", scatter_dimension=0, tiled=True)
    grad_out = grad_out.astype(f32)
    grad_qkv_part = grad_qkv_part.reshape(chips, 2, rows, 3 * HD)
    grad_qkv_own = lax.dynamic_index_in_dim(grad_qkv_part, core, 1, keepdims=False)
    grad_qkv_other = lax.dynamic_index_in_dim(grad_qkv_part, 1 - core, 1, keepdims=False)
    grad_qkv_own = grad_qkv_own.astype(f32) + swap(grad_qkv_other, "core").astype(f32)
    joined = jnp.concatenate(
        [grad_project.reshape(chips, BLOCK, 3 * HD), grad_qkv_own.astype(bf16)], axis=1
    )

    bias_part = jnp.where(
        jnp.arange(H)[None, :] == head, bias_grad[0, :2][:, None], jnp.zeros((2, H), f32)
    )
    packed = jnp.concatenate(
        [
            attn_grad[:, 0] / attn_gain,
            grad_ffn[0],
            gain_grad[0],
            bias_part.reshape(-1),
            squares[:2, 0],
            jnp.sum(ffn_branch * ffn_branch)[None],
            jnp.zeros((93,), f32),
        ]
    )
    joined = lax.all_to_all(joined, CHIPS, 0, 0, tiled=True)
    summed = sum_everywhere(packed.reshape(-1, 128))
    grad_down = feed_grad[8 * rows :].astype(f32)
    grad_expand = widen(expand_grad, depth, hidden_rows)
    joined, summed, grad_down, grad_expand = lax.optimization_barrier(
        (joined, summed, grad_down, grad_expand)
    )
    joined = over_sharers(joined, sharers)
    grad_inputs, grad_qkv = input_back(joined, qkv_full, inputs, attn_gain[None], grad_middle)
    summed = summed.reshape(-1)
    at = 2 * D + 2 * HD
    root_means = jnp.sqrt(summed[at + 2 * H : at + 2 * H + 3] / (tokens * D))
    return (
        outputs,
        grad_inputs,
        grad_qkv,
        grad_out,
        grad_expand,
        grad_down,
        summed[:D],
        summed[D : 2 * D],
        summed[2 * D : 2 * D + HD],
        summed[2 * D + HD : at],
        summed[at : at + 2 * H].reshape(2, H),
        root_means,
    )


def solution(mesh):
    grid = mesh.devices if mesh.axis_names == ("head", "blk") else mesh.devices.T
    heads, blks = grid.shape
    mesh = Mesh(grid.reshape(heads // 2, 2, blks // 2, 2), ("hx", "core", "bz", "by"))
    split = P(DEVICES, None)

    return jax.shard_map(
        body,
        mesh=mesh,
        in_specs=(split,) * 2 + (P(),) * 5 + (split,) * 4 + (P(),) * 3,
        out_specs=(split,) * 6 + (P(),) * 6,
        check_vma=False,
    )
```

```python
from functools import partial

import jax
import jax.numpy as jnp
from jax import lax
from jax.experimental import pallas as pl
from jax.experimental.pallas import tpu as pltpu
from jax.sharding import Mesh
from jax.sharding import PartitionSpec as P


D = 1024
H = 16
HD = 64
BLOCK = 128
NVAR = 4
EPSILON = 1e-05
THETA = 10000.0

DEVICES = ("bz", "by", "hx", "core")
CHIPS = ("bz", "by", "hx")
PLANE = ("by", "hx", "core")

SEGMENT_LANE = 64
VARIATE_LANE = 76
OWN_VARIATE_LANE = 88
MASK = -512.0
QUERY_TILE = 512
KEY_TILE = 512
PROJECT_BLOCKS = 4

bf16 = jnp.bfloat16
f32 = jnp.float32


def dot(left, right, dims):
    return lax.dot_general(left, right, (dims, ((), ())), preferred_element_type=f32)


def norm_rows(values, gain):
    factor = lax.rsqrt(jnp.mean(values * values, axis=-1, keepdims=True) + EPSILON)
    return values * factor * gain


def norm_back(values, gain, grad):
    factor = lax.rsqrt(jnp.mean(values * values, axis=-1, keepdims=True) + EPSILON)
    scaled = grad * gain
    inner = jnp.mean(scaled * values, axis=-1, keepdims=True)
    grad_values = factor * (scaled - values * (factor * factor) * inner)
    return grad_values, grad * values * factor


def swap(shard, axis):
    return lax.ppermute(shard, axis, [(0, 1), (1, 0)])


def plane_gather(shard):
    mine = jnp.concatenate(quarters(shard), axis=0)
    return mine, swap(mine, "core")


def chip_gather(shard, rider, late):
    depth = lax.axis_size("bz")
    chips = depth * 4
    z, y, x = lax.axis_index("bz"), lax.axis_index("by"), lax.axis_index("hx")
    at = jnp.arange(chips, dtype=jnp.int32)
    if depth > 4:
        pieces = lax.all_gather(shard, CHIPS, axis=0)
        return list(pieces), at, (swap(rider, "hx"), swap(rider, "by")), late
    column = z_shifts([shard] * (depth - 1))
    across_x, across_y = [swap(shard, "hx")], [swap(shard, "by")]
    across_x += [swap(piece, "hx") for piece in column]
    across_y += [swap(piece, "by") for piece in column]
    across_x, across_y, late = lax.optimization_barrier((across_x, across_y, late))
    corner = [swap(across_x[i], "by") if i > 1 else swap(across_y[i], "hx") for i in range(depth)]
    riders = swap(rider, "hx"), swap(rider, "by")
    pieces = [shard, across_x[0], across_y[0], corner[0]]
    pieces += column + across_x[1:] + across_y[1:] + corner[1:]
    back = (z - at // 4) % depth
    flips = ((at % 2) ^ x) + 2 * (((at // 2) % 2) ^ y)
    where = jnp.where(back == 0, flips, 4 + flips * (depth - 1) + back - 1).astype(jnp.int32)
    return pieces, where, riders, late


def sum_everywhere(values):
    for axis in ("core", "hx", "by"):
        values = values + swap(values, axis)
    depth = lax.axis_size("bz")
    if depth > 4:
        step = 1
        while step < depth:
            values = values + lax.ppermute(values, "bz", [(i, i ^ step) for i in range(depth)])
            step *= 2
        return values
    shifted = z_shifts([values] * (depth - 1))
    copies = jnp.stack([values] + shifted)
    back = (lax.axis_index("bz") - jnp.arange(depth, dtype=jnp.int32)) % depth
    return sum(lax.dynamic_index_in_dim(copies, back[z], 0, keepdims=False) for z in range(depth))


def z_shifts(values):
    depth = lax.axis_size("bz")
    return [
        lax.ppermute(value, "bz", [(i, (i + by + 1) % depth) for i in range(depth)])
        for by, value in enumerate(values)
    ]


def sum_along_z(parts):
    depth = lax.axis_size("bz")
    if depth > 4:
        parts = parts.reshape(-1, parts.shape[2]).astype(bf16)
        return lax.psum_scatter(parts, "bz", scatter_dimension=0, tiled=True).astype(f32)
    z = lax.axis_index("bz")
    parts = [
        lax.dynamic_index_in_dim(parts, (z + by) % depth, 0, keepdims=False) for by in range(depth)
    ]
    arrived = z_shifts([part.astype(bf16) for part in parts[1:]])
    return sum([part.astype(f32) for part in arrived], parts[0])


def quarters(shard):
    half = shard.shape[0] // 2
    across_x = swap(shard, "hx")
    across_y = swap(shard, "by")
    return [shard, across_x, across_y, swap(across_y[:half], "hx"), swap(across_x[half:], "by")]


def plane_scatter(mine, other):
    rows = mine.shape[0] // 4
    half = rows // 2
    mine = mine.astype(f32) + swap(other, "core").astype(f32)
    corner = mine[3 * rows :].astype(bf16)
    for_y = swap(corner[:half], "hx").astype(f32)
    for_x = swap(corner[half:], "by").astype(f32)
    to_x = mine[rows : 2 * rows]
    to_y = mine[2 * rows : 3 * rows]
    to_x = jnp.concatenate([to_x[:half], to_x[half:] + for_x], axis=0).astype(bf16)
    to_y = jnp.concatenate([to_y[:half] + for_y, to_y[half:]], axis=0).astype(bf16)
    from_x = swap(to_x, "hx")
    from_y = swap(to_y, "by")
    return mine[:rows], from_x, from_y


def plane_members():
    by, hx, core = lax.axis_index("by"), lax.axis_index("hx"), lax.axis_index("core")
    members = []
    for core_flip in (0, 1):
        for x_flip, y_flip in ((0, 0), (1, 0), (0, 1), (1, 1)):
            members.append((by ^ y_flip) * 4 + (hx ^ x_flip) * 2 + (core ^ core_flip))
    return members


def lanes(shape):
    return lax.broadcasted_iota(jnp.int32, shape, len(shape) - 1)


def half_mean(values, lane):
    low = jnp.sum(jnp.where(lane < HD, values, 0.0), axis=-1, keepdims=True)
    high = jnp.sum(jnp.where(lane < HD, 0.0, values), axis=-1, keepdims=True)
    return jnp.where(lane < HD, low, high) * (1.0 / HD)


def swap_halves(values, lane):
    return jnp.where(
        (lane & (HD - 1)) < HD // 2, pltpu.roll(values, 96, 1), pltpu.roll(values, 32, 1)
    )


def project_kernel(where_ref, *refs, chips):
    piece_refs, refs = refs[:chips], refs[chips:]
    gain_ref, weight_ref, cosine_ref, sine_ref, gains_ref, hot_ref, mask_ref = refs[:7]
    normed_ref, raw_ref, query_ref, kv_ref, out_ref, x_ref, arrived = refs[7:]
    step = pl.program_id(0)

    @pl.when(step == 0)
    def _():
        copies = [
            pltpu.make_async_copy(piece_refs[i], x_ref.at[i], arrived.at[i]) for i in range(chips)
        ]
        for copy in copies:
            copy.start()
        for copy in copies:
            copy.wait()

    places = [where_ref[step * PROJECT_BLOCKS + i] for i in range(PROJECT_BLOCKS)]
    for i, place in enumerate(places):
        out_ref[i] = x_ref[place, BLOCK:]
    x = jnp.concatenate([x_ref[place, :BLOCK] for place in places], axis=0).astype(f32)
    normed = norm_rows(x, gain_ref[...]).astype(bf16)
    normed_ref[...] = normed
    project = dot(normed, weight_ref[...], ((1,), (0,)))
    both = project[:, : 2 * HD]
    value = project[:, 2 * HD :]
    raw_ref[...] = both
    lane = lanes(both.shape)
    scaled = both * lax.rsqrt(half_mean(both * both, lane) + EPSILON) * gains_ref[...]
    turned = scaled * cosine_ref[...] + swap_halves(scaled, lane) * sine_ref[...]
    turned = turned.astype(bf16).astype(f32)
    query_ref[...] = jnp.where(lane < HD, turned, hot_ref[...].astype(f32)).astype(bf16)
    key = pltpu.roll(turned * HD ** (-0.5), HD, 1)
    ones = jnp.where((lane >= HD) & (lane < HD + 3), 1.0, 0.0)
    kv_ref[:, :128] = jnp.where(lane < HD, key, mask_ref[...].astype(f32)).astype(bf16)
    kv_ref[:, 128:] = jnp.where(lane < HD, value, ones).astype(bf16)


def project(where, pieces, gain, weight, cosine, sine, gains, hot, mask):
    blocks = len(pieces)
    rows = blocks * BLOCK
    step_rows = PROJECT_BLOCKS * BLOCK
    out_rows = pieces[0].shape[0] - BLOCK
    row_spec = lambda width: pl.BlockSpec((step_rows, width), lambda j, *unused: (j, 0))
    whole = lambda array: pl.BlockSpec(array.shape, lambda j, *unused: (0, 0))
    anywhere = pl.BlockSpec(memory_space=pl.ANY)
    tables = [whole(gain), whole(weight), row_spec(128), row_spec(128), whole(gains)]
    return pl.pallas_call(
        partial(project_kernel, chips=blocks),
        grid_spec=pltpu.PrefetchScalarGridSpec(
            num_scalar_prefetch=1,
            grid=(blocks // PROJECT_BLOCKS,),
            in_specs=[anywhere] * blocks + tables + [row_spec(128), row_spec(128)],
            out_specs=[
                row_spec(D),
                row_spec(128),
                row_spec(128),
                row_spec(256),
                pl.BlockSpec((PROJECT_BLOCKS, out_rows, D), lambda j, *unused: (j, 0, 0)),
            ],
            scratch_shapes=[
                pltpu.VMEM((blocks, BLOCK + out_rows, D), bf16),
                pltpu.SemaphoreType.DMA((blocks,)),
            ],
        ),
        out_shape=[
            jax.ShapeDtypeStruct((rows, D), bf16),
            jax.ShapeDtypeStruct((rows, 128), f32),
            jax.ShapeDtypeStruct((rows, 128), bf16),
            jax.ShapeDtypeStruct((rows, 256), bf16),
            jax.ShapeDtypeStruct((blocks, out_rows, D), bf16),
        ],
        name="project",
    )(where, *pieces, gain, weight, cosine, sine, gains, hot, mask)


def sort_keys(place_ref, own_ref, other_ref, keys_ref):
    blocks = own_ref.shape[0] // BLOCK
    for half, source_ref in ((0, own_ref), (1, other_ref)):

        def put(j, unused, half=half, source_ref=source_ref):
            source = pl.multiple_of(j * BLOCK, BLOCK)
            target = pl.multiple_of(place_ref[half * blocks + j] * BLOCK, BLOCK)
            keys_ref[pl.ds(target, BLOCK), :] = source_ref[pl.ds(source, BLOCK), :]
            return unused

        lax.fori_loop(0, blocks, put, 0, unroll=4)


def block_start(order_ref, index):
    return pl.multiple_of(order_ref[index] * BLOCK, BLOCK)


def attend_kernel(
    order_ref,
    place_ref,
    low_ref,
    high_ref,
    query_ref,
    own_ref,
    other_ref,
    kept_ref,
    attended_ref,
    keys_ref,
):
    tile = pl.program_id(0)
    count = QUERY_TILE // BLOCK

    @pl.when(tile == 0)
    def _():
        sort_keys(place_ref, own_ref, other_ref, keys_ref)
        if order_ref.shape[0] * BLOCK != query_ref.shape[0]:
            kept_ref[...] = jnp.zeros_like(kept_ref)
            attended_ref[...] = jnp.zeros_like(attended_ref)

    starts = [block_start(order_ref, tile * count + i) for i in range(count)]
    query = jnp.concatenate([query_ref[pl.ds(start, BLOCK), :] for start in starts], axis=0)

    def chunk(index, accumulated):
        window = pl.ds(pl.multiple_of(index * KEY_TILE, KEY_TILE), KEY_TILE)
        expo = jnp.exp(dot(query, keys_ref[window, :128], ((1,), (1,))))
        return accumulated + dot(expo.astype(bf16), keys_ref[window, 128:], ((1,), (0,)))

    accumulated = lax.fori_loop(
        low_ref[tile], high_ref[tile], chunk, jnp.zeros((QUERY_TILE, 128), f32)
    )
    totals = accumulated[:, HD : HD + 1]
    lane = lanes(accumulated.shape)
    kept = jnp.where(lane < HD, accumulated / totals, totals)
    for i, start in enumerate(starts):
        piece = kept[i * BLOCK : (i + 1) * BLOCK]
        kept_ref[pl.ds(start, BLOCK), :] = piece
        attended_ref[order_ref[tile * count + i]] = piece.T[:HD].astype(bf16)


def fixed(array):
    return pl.BlockSpec(
        array.shape, lambda *unused: (0,) * len(array.shape), pipeline_mode=pl.Buffered(1)
    )


def attend(order, place, low, high, query, own, other):
    rows = query.shape[0]
    operands = (query, own, other)
    outs = (
        jax.ShapeDtypeStruct((rows, 128), f32),
        jax.ShapeDtypeStruct((rows // BLOCK, HD, BLOCK), bf16),
    )
    return pl.pallas_call(
        attend_kernel,
        grid_spec=pltpu.PrefetchScalarGridSpec(
            num_scalar_prefetch=4,
            grid=(low.shape[0],),
            in_specs=[fixed(array) for array in operands],
            out_specs=[fixed(array) for array in outs],
            scratch_shapes=[pltpu.VMEM((2 * rows, 256), bf16)],
        ),
        out_shape=list(outs),
        name="attend",
    )(order, place, low, high, *operands)


def attend_back_kernel(
    order_ref,
    place_ref,
    source_ref,
    low_ref,
    high_ref,
    query_ref,
    own_ref,
    other_ref,
    kept_ref,
    grad_ref,
    query_grad_ref,
    own_grad_ref,
    other_grad_ref,
    bias_ref,
    keys_ref,
    sorted_ref,
    wide_ref,
    sums_ref,
    every_ref,
    same_ref,
):
    step = pl.program_id(0)
    own_rows = own_ref.shape[0]
    taken = order_ref.shape[0]

    @pl.when(step == 0)
    def _():
        sort_keys(place_ref, own_ref, other_ref, keys_ref)
        every_ref[...] = jnp.zeros_like(every_ref)
        same_ref[...] = jnp.zeros_like(same_ref)
        sums_ref[...] = jnp.zeros_like(sums_ref)
        if taken * BLOCK != own_rows:
            query_grad_ref[...] = jnp.zeros_like(query_grad_ref)
        lane = lanes((BLOCK, 128))

        def put(i, unused):
            source = pl.ds(block_start(order_ref, i), BLOCK)
            target = pl.ds(pl.multiple_of(i * BLOCK, BLOCK), BLOCK)
            sorted_ref[target, :] = query_ref[source, :]
            kept = kept_ref[source, :]
            grad = grad_ref[order_ref[i]].astype(f32)
            grad = jnp.concatenate([grad, jnp.zeros_like(grad)], axis=0).T
            inverse = 1.0 / kept[:, HD : HD + 1]
            center = jnp.sum(grad * kept, axis=1, keepdims=True) * inverse
            center_high = center.astype(bf16).astype(f32)
            center_rest = center - center_high
            center_mid = center_rest.astype(bf16).astype(f32)
            center_low = center_rest - center_mid
            wide = jnp.where(lane == HD, -center_high, 0.0)
            wide = jnp.where(lane == HD + 1, -center_mid, wide)
            wide = jnp.where(lane == HD + 2, -center_low, wide)
            wide_ref[target, :] = jnp.where(lane < HD, grad * inverse, wide).astype(bf16)
            return unused

        lax.fori_loop(0, taken, put, 0, unroll=4)

    window = pl.ds(pl.multiple_of(step * KEY_TILE, KEY_TILE), KEY_TILE)
    key = keys_ref[window, :128]
    value = keys_ref[window, 128:]

    def tile(index, grads):
        rows = pl.ds(pl.multiple_of(index * QUERY_TILE, QUERY_TILE), QUERY_TILE)
        query = sorted_ref[rows, :]
        wide = wide_ref[rows, :]
        expo = jnp.exp(dot(key, query, ((1,), (1,))))
        score_low = (expo * dot(value, wide, ((1,), (1,)))).astype(bf16)
        sums_ref[rows, :] += dot(score_low, key, ((0,), (0,)))
        return (
            grads[0] + dot(score_low, query, ((1,), (0,))),
            grads[1] + dot(expo.astype(bf16), wide, ((1,), (0,))),
        )

    empty = jnp.zeros((KEY_TILE, 128), f32)
    key_grad, value_grad = lax.fori_loop(low_ref[step], high_ref[step], tile, (empty, empty))
    lane = lanes(key_grad.shape)
    joined = jnp.where(lane < HD, value_grad, pltpu.roll(key_grad, HD, 1) * HD ** (-0.5))
    joined = joined.astype(bf16)
    for i in range(KEY_TILE // BLOCK):
        source = source_ref[step * (KEY_TILE // BLOCK) + i] * BLOCK
        piece = joined[i * BLOCK : (i + 1) * BLOCK]

        @pl.when(source < own_rows)
        def _(source=source, piece=piece):
            own_grad_ref[pl.ds(pl.multiple_of(source, BLOCK), BLOCK), :] = piece

        @pl.when(source >= own_rows)
        def _(source=source, piece=piece):
            other_grad_ref[pl.ds(pl.multiple_of(source - own_rows, BLOCK), BLOCK), :] = piece

    every = jnp.where((lane >= VARIATE_LANE) & (lane < VARIATE_LANE + NVAR), key_grad, 0.0)
    shift = 128 + VARIATE_LANE - OWN_VARIATE_LANE
    same = every * pltpu.roll(key.astype(f32), shift, 1)
    every_ref[...] += jnp.sum(every.reshape(-1, 8, 128), axis=0)
    same_ref[...] += jnp.sum(same.reshape(-1, 8, 128), axis=0)

    @pl.when(step == pl.num_programs(0) - 1)
    def _():
        def put(i, unused):
            target = pl.ds(block_start(order_ref, i), BLOCK)
            rows = pl.ds(pl.multiple_of(i * BLOCK, BLOCK), BLOCK)
            query_grad_ref[target, :] = sums_ref[rows, :].astype(bf16)
            return unused

        lax.fori_loop(0, taken, put, 0, unroll=4)
        every = jnp.sum(every_ref[...], keepdims=True)
        same = jnp.sum(same_ref[...], keepdims=True)
        bias_lane = lanes((8, 128))
        bias_ref[...] = jnp.where(
            bias_lane == 0, every - same, jnp.where(bias_lane == 1, same, 0.0)
        )


def attend_back(order, place, source, low, high, query, own, other, kept, grad):
    rows = query.shape[0]
    taken = order.shape[0] * BLOCK
    operands = (query, own, other, kept, grad)
    outs = tuple(jax.ShapeDtypeStruct((rows, 128), bf16) for _ in range(3)) + (
        jax.ShapeDtypeStruct((8, 128), f32),
    )
    return pl.pallas_call(
        attend_back_kernel,
        grid_spec=pltpu.PrefetchScalarGridSpec(
            num_scalar_prefetch=5,
            grid=(low.shape[0],),
            in_specs=[fixed(array) for array in operands],
            out_specs=[fixed(array) for array in outs],
            scratch_shapes=[
                pltpu.VMEM((2 * rows, 256), bf16),
                pltpu.VMEM((taken, 128), bf16),
                pltpu.VMEM((taken, 128), bf16),
                pltpu.VMEM((taken, 128), f32),
                pltpu.VMEM((8, 128), f32),
                pltpu.VMEM((8, 128), f32),
            ],
        ),
        out_shape=list(outs),
        name="attend_back",
    )(order, place, source, low, high, *operands)


def project_back_kernel(
    query_grad_ref,
    own_ref,
    other_ref,
    raw_ref,
    cosine_ref,
    sine_ref,
    gains_ref,
    normed_ref,
    forward_ref,
    grad_ref,
    weight_grad_ref,
    gain_grad_ref,
    attn_grad_ref,
    weight_ref,
    gain_ref,
):
    step = pl.program_id(0)

    @pl.when(step == 0)
    def _():
        weight_ref[...] = jnp.zeros_like(weight_ref)
        gain_ref[...] = jnp.zeros_like(gain_ref)

    kv_grad = own_ref[...].astype(f32) + other_ref[...].astype(f32)
    kv_grad = kv_grad.astype(bf16).astype(f32)
    lane = lanes(kv_grad.shape)
    turned = jnp.where(lane < HD, query_grad_ref[...].astype(f32), kv_grad)
    grad = turned * cosine_ref[...] - swap_halves(turned, lane) * sine_ref[...]
    raw = raw_ref[...]
    factor = lax.rsqrt(half_mean(raw * raw, lane) + EPSILON)
    scaled = grad * gains_ref[...]
    inner = half_mean(scaled * raw, lane)
    both = factor * (scaled - raw * (factor * factor) * inner)
    gain_ref[...] += jnp.sum(grad * raw * factor, axis=0, keepdims=True)
    full = jnp.concatenate([both, jnp.where(lane < HD, kv_grad, 0.0)], axis=1)
    for i in range(grad_ref.shape[0]):
        grad_ref[i] = full[i * BLOCK : (i + 1) * BLOCK].T[: 3 * HD].astype(bf16)
    weight_ref[...] += dot(normed_ref[...], full.astype(bf16), ((0,), (0,)))

    @pl.when(step == pl.num_programs(0) - 1)
    def _():
        weight_grad_ref[...] = weight_ref[:, : 3 * HD].astype(bf16)
        gain_grad_ref[...] = jnp.broadcast_to(gain_ref[...], gain_grad_ref.shape)
        forward = forward_ref[...].astype(f32)
        attn = jnp.sum(weight_ref[...] * forward, axis=1, keepdims=True)
        attn_grad_ref[...] = jnp.broadcast_to(attn, attn_grad_ref.shape)


def project_back(query_grad, own, other, raw, cosine, sine, gains, normed, forward):
    rows = query_grad.shape[0]
    step_rows = 4 * BLOCK
    row_spec = lambda width: pl.BlockSpec((step_rows, width), lambda j: (j, 0))
    whole = lambda shape: pl.BlockSpec(shape, lambda j: (0, 0))
    return pl.pallas_call(
        project_back_kernel,
        grid=(rows // step_rows,),
        in_specs=[row_spec(128)] * 6 + [whole(gains.shape), row_spec(D), whole(forward.shape)],
        out_specs=[
            pl.BlockSpec((step_rows // BLOCK, 3 * HD, BLOCK), lambda j: (j, 0, 0)),
            whole((D, 3 * HD)),
            whole((8, 128)),
            whole((D, 128)),
        ],
        out_shape=[
            jax.ShapeDtypeStruct((rows // BLOCK, 3 * HD, BLOCK), bf16),
            jax.ShapeDtypeStruct((D, 3 * HD), bf16),
            jax.ShapeDtypeStruct((8, 128), f32),
            jax.ShapeDtypeStruct((D, 128), f32),
        ],
        scratch_shapes=[pltpu.VMEM((D, 4 * HD), f32), pltpu.VMEM((1, 128), f32)],
        name="project_back",
    )(query_grad, own, other, raw, cosine, sine, gains, normed, forward)


def feed_kernel(
    second_mine_ref,
    second_other_ref,
    grad_mine_ref,
    grad_other_ref,
    weight_ref,
    ffn_mine_ref,
    ffn_other_ref,
    back_mine_ref,
    back_other_ref,
    weight_grad_ref,
    expand_ref,
    down_ref,
    expand_grad_ref,
    down_grad_ref,
):
    step = pl.program_id(0)
    half = pl.num_programs(0) // 2
    depth, both_rows, width = weight_ref.shape
    down_rows = down_ref.shape[0] // depth
    expand_rows = both_rows - down_rows

    @pl.when(step == 0)
    def _():
        for z in range(depth):
            expand_ref[z * expand_rows : (z + 1) * expand_rows] = weight_ref[z, :expand_rows]
            down_ref[z * down_rows : (z + 1) * down_rows] = weight_ref[z, expand_rows:]
        expand_grad_ref[...] = jnp.zeros_like(expand_grad_ref)
        down_grad_ref[...] = jnp.zeros_like(down_grad_ref)

    second = jnp.where(step < half, second_mine_ref[...], second_other_ref[...])
    grad = jnp.where(step < half, grad_mine_ref[...], grad_other_ref[...])
    expand = dot(second, expand_ref[...], ((1,), (0,)))
    gate = expand[:, : width // 2]
    up = expand[:, width // 2 :]
    sigmoid = 1.0 / (1.0 + jnp.exp(-gate))
    silu = gate * sigmoid
    hidden = (silu * up).astype(bf16)
    grad_hidden = dot(grad, down_ref[...], ((1,), (1,)))
    grad_gate = grad_hidden * up * (sigmoid * (1.0 + gate * (1.0 - sigmoid)))
    rows = jnp.concatenate([grad_gate, grad_hidden * silu], axis=1).astype(bf16)
    ffn = dot(hidden, down_ref[...], ((1,), (0,))).astype(bf16)
    back = dot(rows, expand_ref[...], ((1,), (1,))).astype(bf16)
    expand_grad_ref[...] += dot(second, rows, ((0,), (0,)))
    down_grad_ref[...] += dot(hidden, grad, ((0,), (0,)))

    @pl.when(step < half)
    def _():
        ffn_mine_ref[...] = ffn
        back_mine_ref[...] = back

    @pl.when(step >= half)
    def _():
        ffn_other_ref[...] = ffn
        back_other_ref[...] = back

    @pl.when(step == pl.num_programs(0) - 1)
    def _():
        for z in range(depth):
            weight_grad_ref[z, :expand_rows] = expand_grad_ref[
                z * expand_rows : (z + 1) * expand_rows
            ].astype(bf16)
            weight_grad_ref[z, expand_rows:] = down_grad_ref[
                z * down_rows : (z + 1) * down_rows
            ].astype(bf16)


def feed(second, grad, weight, down_rows):
    rows = second[0].shape[0]
    tile = 256
    steps = rows // tile
    depth, both_rows, width = weight.shape
    mine = pl.BlockSpec((tile, D), lambda i: (jnp.minimum(i, steps - 1), 0))
    other = pl.BlockSpec((tile, D), lambda i: (jnp.maximum(i - steps, 0), 0))
    whole = pl.BlockSpec(weight.shape, lambda i: (0, 0, 0), pipeline_mode=pl.Buffered(1))
    token_rows = jax.ShapeDtypeStruct((rows, D), bf16)
    return pl.pallas_call(
        feed_kernel,
        grid=(2 * steps,),
        in_specs=[mine, other, mine, other, whole],
        out_specs=[mine, other, mine, other, whole],
        out_shape=[token_rows] * 4 + [jax.ShapeDtypeStruct(weight.shape, bf16)],
        scratch_shapes=[
            pltpu.VMEM((depth * (both_rows - down_rows), width), bf16),
            pltpu.VMEM((depth * down_rows, D), bf16),
            pltpu.VMEM((depth * (both_rows - down_rows), width), f32),
            pltpu.VMEM((depth * down_rows, D), f32),
        ],
        name="feed",
    )(*second, *grad, weight)


def out_kernel(parts_ref, x_ref, weight_ref, gain_ref, middle_ref, second_ref, squares_ref):
    branch = dot(parts_ref[...], weight_ref[...], ((0,), (0,)))
    x = x_ref[...].astype(f32)
    middle = x + branch
    middle_ref[...] = middle
    second_ref[...] = norm_rows(middle, gain_ref[...]).astype(bf16)
    row = lax.broadcasted_iota(jnp.int32, squares_ref.shape, 0)
    x_sum = jnp.sum(x * x, keepdims=True)
    branch_sum = jnp.sum(branch * branch, keepdims=True)
    squares_ref[...] = jnp.where(row == 0, x_sum, branch_sum)


def out_project(parts, x, weight, gain):
    rows = x.shape[0]
    return pl.pallas_call(
        out_kernel,
        out_shape=[
            jax.ShapeDtypeStruct((rows, D), f32),
            jax.ShapeDtypeStruct((rows, D), bf16),
            jax.ShapeDtypeStruct((8, 128), f32),
        ],
        name="out_project",
    )(parts, x, weight, gain)


def middle_back_kernel(
    own_ref,
    from_x_ref,
    from_y_ref,
    middle_ref,
    cotangent_ref,
    gain_ref,
    weight_ref,
    grad_middle_ref,
    branch_ref,
    parts_ref,
    gain_grad_ref,
):
    grad_second = own_ref[...] + from_x_ref[...].astype(f32) + from_y_ref[...].astype(f32)
    grad_middle, gain_rows = norm_back(middle_ref[...], gain_ref[...], grad_second)
    grad_middle = cotangent_ref[...].astype(f32) + grad_middle
    grad_middle_ref[...] = grad_middle
    branch = grad_middle.astype(bf16)
    branch_ref[...] = branch
    parts_ref[...] = dot(weight_ref[...], branch, ((1,), (1,))).astype(bf16)
    gain_grad_ref[...] = jnp.broadcast_to(
        jnp.sum(gain_rows, axis=0, keepdims=True), gain_grad_ref.shape
    )


def middle_back(own, from_x, from_y, middle, cotangent, gain, weight):
    rows = middle.shape[0]
    return pl.pallas_call(
        middle_back_kernel,
        out_shape=[
            jax.ShapeDtypeStruct((rows, D), f32),
            jax.ShapeDtypeStruct((rows, D), bf16),
            jax.ShapeDtypeStruct((D, rows), bf16),
            jax.ShapeDtypeStruct((8, D), f32),
        ],
        name="middle_back",
    )(own, from_x, from_y, middle, cotangent, gain, weight)


def out_grad_kernel(
    members_ref,
    merged_ref,
    branch_ref,
    ffn_mine_ref,
    ffn_other_ref,
    mine_ref,
    other_ref,
    grad_ref,
    depth,
):
    shard = mine_ref.shape[0] // 4
    rows = shard // depth
    grad_ref[...] = dot(merged_ref[...], branch_ref[...], ((1,), (0,)))
    mine_ref[:, :D] = ffn_mine_ref[...]
    other_ref[:, :D] = ffn_other_ref[...]
    for place in range(8):
        target_ref = mine_ref if place < 4 else other_ref
        for z in range(depth):
            source = pl.multiple_of((z * 8 + members_ref[place]) * rows, rows)
            target = (place % 4) * shard + z * rows
            target_ref[target : target + rows, D:] = grad_ref[pl.ds(source, rows), :].astype(bf16)


def out_grad(members, merged, branch, ffn_mine, ffn_other, depth):
    joined = jax.ShapeDtypeStruct((ffn_mine.shape[0], 2 * D), bf16)
    operands = (merged, branch, ffn_mine, ffn_other)
    return pl.pallas_call(
        partial(out_grad_kernel, depth=depth),
        grid_spec=pltpu.PrefetchScalarGridSpec(
            num_scalar_prefetch=1,
            grid=(1,),
            in_specs=[fixed(array) for array in operands],
            out_specs=[fixed(joined), fixed(joined)],
            scratch_shapes=[pltpu.VMEM((D, D), f32)],
        ),
        out_shape=[joined, joined],
        name="out_grad",
    )(members, *operands)


def input_back_kernel(
    joined_ref, weight_ref, x_ref, gain_ref, middle_ref, grad_ref, qkv_ref, wide_ref
):
    heads = joined_ref.shape[0]
    rows = qkv_ref.shape[0]
    for head in range(heads):
        wide_ref[head * 3 * HD : (head + 1) * 3 * HD] = joined_ref[head, : 3 * HD]
    for pair in range(heads // 2):
        left = joined_ref[2 * pair, 3 * HD :].astype(f32)
        right = joined_ref[2 * pair + 1, 3 * HD :].astype(f32)
        at = pair * 2 * HD
        low = jnp.concatenate([left[:, :HD], right[:, :HD]], axis=1)
        high = jnp.concatenate([left[:, HD:], right[:, HD:]], axis=1)
        qkv_ref[:, at : at + 2 * HD] = low[:rows]
        qkv_ref[:, D + at : D + at + 2 * HD] = high[:rows]
        qkv_ref[: rows // 2, 2 * D + at : 2 * D + at + 2 * HD] = low[rows:]
        qkv_ref[rows // 2 :, 2 * D + at : 2 * D + at + 2 * HD] = high[rows:]
    grad_normed = dot(wide_ref[...], weight_ref[...], ((0,), (1,)))
    grad, _ = norm_back(x_ref[...].astype(f32), gain_ref[...], grad_normed)
    grad_ref[...] = middle_ref[...] + grad


def input_back(joined, weight, x, gain, middle):
    rows = x.shape[0]
    return pl.pallas_call(
        input_back_kernel,
        out_shape=[
            jax.ShapeDtypeStruct((rows, D), f32),
            jax.ShapeDtypeStruct(((joined.shape[1] - 3 * HD) * 2 // 3, 3 * D), f32),
        ],
        scratch_shapes=[pltpu.VMEM((3 * D, rows), bf16)],
        name="input_back",
    )(joined, weight, x, gain, middle)


def widen_kernel(parts_ref, grad_ref):
    sources, _, width = parts_ref.shape
    for source in range(sources):
        for at in range(width // 128):
            to = (at * sources + source) * 128
            grad_ref[:, to : to + 128] = parts_ref[source, :, at * 128 : (at + 1) * 128].astype(f32)


def widen(parts, depth, hidden_rows):
    sources, rows, width = parts.shape
    if hidden_rows != 128:
        parts = parts.reshape(sources, rows, 2, depth, hidden_rows)
        return parts.transpose(1, 2, 3, 0, 4).reshape(rows, -1).astype(f32)
    return pl.pallas_call(
        widen_kernel, out_shape=jax.ShapeDtypeStruct((rows, sources * width), f32), name="widen"
    )(parts)


def token_meta(seq_lengths, block_order):
    blocks = block_order.shape[0]
    packed_at = jnp.repeat(block_order, BLOCK) * BLOCK + jnp.tile(
        jnp.arange(BLOCK, dtype=jnp.int32), blocks
    )
    ends = jnp.cumsum(seq_lengths)
    after = packed_at[:, None] >= ends[None, :]
    segment = jnp.sum(after.astype(jnp.int32), axis=1)
    begin = jnp.max(jnp.where(after, ends[None, :], jnp.zeros_like(ends)[None, :]), axis=1)
    return (segment, packed_at - begin, ends)


def own_rows(array, core):
    pairs = array.reshape(-1, 2, BLOCK)
    return lax.dynamic_index_in_dim(pairs, core, 1, keepdims=False).reshape(-1)


def one_hot_rows(segment, variate):
    lane = jnp.arange(128, dtype=jnp.int32)[None, :]
    hot = lane == SEGMENT_LANE + segment[:, None]
    for copy in range(3):
        hot = hot | (lane == VARIATE_LANE + copy * NVAR + variate[:, None])
    return hot.astype(bf16)


def mask_rows(segment, variate, segments, bias):
    lane = jnp.arange(128, dtype=jnp.int32)[None, :]
    here = lane - SEGMENT_LANE
    rows = jnp.where(
        (here >= 0) & (here < segments) & (here != segment[:, None]), jnp.float32(MASK), 0.0
    )
    high = lax.reduce_precision(bias, 8, 7)
    mid = lax.reduce_precision(bias - high, 8, 7)
    low = bias - high - mid
    for copy, part in enumerate((high, mid, low)):
        here = lane - VARIATE_LANE - copy * NVAR
        value = jnp.where(here == variate[:, None], part[1], part[0])
        rows = jnp.where((here >= 0) & (here < NVAR), value, rows)
    rows = jnp.where(lane == OWN_VARIATE_LANE + variate[:, None], 1.0, rows)
    return rows.astype(bf16)


def over_sharers(parts, sharers):
    if sharers == 1:
        return parts
    parts = parts.reshape((H, sharers) + parts.shape[1:]).astype(f32)
    return jnp.sum(parts, axis=1).astype(bf16)


def body(
    inputs,
    cotangent,
    attn_gain,
    ffn_gain,
    query_gain,
    key_gain,
    variate_bias,
    qkv_weight,
    out_weight,
    expand_weight,
    down_weight,
    seq_lengths,
    variate_ids,
    block_order,
):
    depth = lax.axis_size("bz")
    chips = depth * 4
    sharers = chips // H
    core = lax.axis_index("core")
    chip = (lax.axis_index("bz") * 2 + lax.axis_index("by")) * 2 + lax.axis_index("hx")
    head = chip // sharers
    share = chip % sharers
    rows = qkv_weight.shape[0]
    hidden_rows = down_weight.shape[0]
    segments = seq_lengths.shape[0] + 1
    tokens = variate_ids.shape[0]

    by_head = qkv_weight.reshape(rows, 3, H, HD)
    to_heads = jnp.repeat(
        by_head.transpose(2, 0, 1, 3).reshape(H, rows, 3 * HD), 2 * sharers, axis=0
    )
    own_qkv = lax.all_to_all(to_heads, DEVICES, 0, 0, tiled=True)
    own_qkv = jnp.pad(own_qkv.reshape(D, 3 * HD), ((0, 0), (0, HD)))
    to_plane = (
        expand_weight.reshape(rows, 2, depth, 8, hidden_rows)
        .transpose(3, 0, 1, 2, 4)
        .reshape(8, rows, 2 * depth * hidden_rows)
    )
    expand_part = lax.all_to_all(to_plane, PLANE, 0, 0, tiled=True)
    expand_part = expand_part.reshape(8 * rows, -1)

    segment, position, ends = token_meta(seq_lengths, block_order)
    own_segment = own_rows(segment, core)
    own_variate = own_rows(variate_ids, core)
    own_position = own_rows(position, core)
    bias = lax.dynamic_index_in_dim(variate_bias, head, 1, keepdims=False)
    hot = one_hot_rows(own_segment, own_variate)
    mask = mask_rows(own_segment, own_variate, segments, bias)
    freqs = THETA ** (-jnp.arange(HD // 2, dtype=f32) / (HD // 2))
    angles = own_position.astype(f32)[:, None] * freqs[None, :]
    cosine = jnp.tile(jnp.cos(angles), (1, 4))
    sine = jnp.sin(angles)
    sine = jnp.tile(jnp.concatenate([-sine, sine], axis=1), (1, 2))
    pairs = block_order.reshape(chips, 2)
    own_place = lax.dynamic_index_in_dim(pairs, core, 1, keepdims=False)
    other_place = lax.dynamic_index_in_dim(pairs, 1 - core, 1, keepdims=False)
    place = jnp.concatenate([own_place, other_place])
    rank = jnp.sum((own_place[None, :] < own_place[:, None]).astype(jnp.int32), axis=1)
    taken = chips // sharers
    wanted = share * taken + jnp.arange(taken, dtype=jnp.int32)
    chosen = (rank[None, :] == wanted[:, None]).astype(jnp.int32)
    order = jnp.sum(chosen * jnp.arange(chips, dtype=jnp.int32)[None, :], axis=1)
    sorted_place = jnp.sum(chosen * own_place[None, :], axis=1).reshape(-1, QUERY_TILE // BLOCK)
    first_token = sorted_place[:, 0] * BLOCK
    last_token = sorted_place[:, -1] * BLOCK + BLOCK - 1
    begins = jnp.max(jnp.where(ends[None, :] <= first_token[:, None], ends[None, :], 0), axis=1)
    finish = jnp.min(jnp.where(ends[None, :] > last_token[:, None], ends[None, :], tokens), axis=1)
    low = begins // KEY_TILE
    high = (finish + KEY_TILE - 1) // KEY_TILE
    slots = jnp.arange(2 * chips, dtype=jnp.int32)
    source = jnp.sum(
        jnp.where(place[None, :] == slots[:, None], slots[None, :], 0), axis=1, dtype=jnp.int32
    )
    chunks = jnp.arange(tokens // KEY_TILE, dtype=jnp.int32)[:, None]
    low_tile = jnp.sum((high[None, :] <= chunks).astype(jnp.int32), axis=1)
    high_tile = jnp.sum((low[None, :] <= chunks).astype(jnp.int32), axis=1)
    gains = jnp.concatenate([query_gain, key_gain])[None, :]

    late = (hot, mask, cosine, sine, own_qkv, place, order, low, high, source, low_tile, high_tile)
    pieces, where, riders, late = chip_gather(
        jnp.concatenate([inputs, out_weight], axis=0), cotangent, late
    )
    hot, mask, cosine, sine, own_qkv, place, order, low, high, source, low_tile, high_tile = late

    feed_part = jnp.concatenate([expand_part, down_weight], axis=0)
    feed_own = lax.all_gather(feed_part[None], "bz", axis=0, tiled=True)

    normed_low, raw, query, own_kv, out_mine = project(
        where, pieces, attn_gain[None], own_qkv, cosine, sine, gains, hot, mask
    )
    own_kv, riders = lax.optimization_barrier((own_kv, riders))
    other_kv = swap(own_kv, "core")
    rider_corner = swap(riders[0], "by")
    kept, attended = attend(order, place, low, high, query, own_kv, other_kv)
    attended, rider_corner = lax.optimization_barrier((attended, rider_corner))
    cotangent_mine = jnp.concatenate([cotangent, *riders, rider_corner], axis=0)
    cotangent_other = swap(cotangent_mine, "core")
    out_other = swap(out_mine, "core")
    out_full = jnp.stack(
        [jnp.where(core == 0, out_mine, out_other), jnp.where(core == 0, out_other, out_mine)],
        axis=1,
    ).reshape(D, D)
    merged = lax.all_to_all(attended, CHIPS, 0, 0, tiled=True)
    merged, cotangent_other = lax.optimization_barrier((merged, cotangent_other))
    cotangent_plane = (cotangent_mine, cotangent_other)
    merged = over_sharers(merged, sharers).reshape(D, BLOCK)
    middle, second, squares = out_project(merged, inputs, out_full, ffn_gain[None])
    second_plane = plane_gather(second)

    ffn_mine, ffn_other, back_mine, back_other, feed_grad = feed(
        second_plane, cotangent_plane, feed_own, hidden_rows
    )
    feed_grad = lax.psum_scatter(feed_grad, "bz", scatter_dimension=0, tiled=True)
    feed_grad = feed_grad[0]

    qkv_full = lax.all_gather(
        by_head.transpose(0, 2, 1, 3).reshape(rows, 3 * D), DEVICES, axis=0, tiled=True
    )
    grad_middle, branch_grad, to_chips, grad_ffn = middle_back(
        *plane_scatter(back_mine, back_other), middle, cotangent, ffn_gain[None], out_full
    )
    grad_attended = lax.all_to_all(
        jnp.repeat(to_chips.reshape(H, HD, BLOCK), sharers, axis=0), CHIPS, 0, 0, tiled=True
    )

    joined_mine, joined_other = out_grad(
        jnp.stack(plane_members()), merged, branch_grad, ffn_mine, ffn_other, depth
    )
    joined_other = swap(joined_other, "core")
    joined = (joined_mine.astype(f32) + joined_other.astype(f32)).astype(bf16)
    joined = joined.reshape(4, BLOCK, 2 * D)
    to_x = jnp.concatenate([joined[1], joined[3]], axis=0)
    grad_attended, to_x = lax.optimization_barrier((grad_attended, to_x))
    from_x = swap(to_x, "hx")

    query_grad, own_grad, other_grad, bias_grad = attend_back(
        order, place, source, low_tile, high_tile, query, own_kv, other_kv, kept, grad_attended
    )
    query_grad, from_x = lax.optimization_barrier((query_grad, from_x))
    from_x = from_x.astype(f32)
    from_y = swap((joined[2].astype(f32) + from_x[BLOCK:]).astype(bf16), "by")
    expand_grad = lax.all_to_all(
        feed_grad[: 8 * rows].reshape(8, rows, -1), PLANE, 0, 0, tiled=True
    )
    grad_project, grad_qkv_part, gain_grad, attn_grad = project_back(
        query_grad,
        own_grad,
        swap(other_grad, "core"),
        raw,
        cosine,
        sine,
        gains,
        normed_low,
        own_qkv,
    )
    grad_qkv_part, from_y = lax.optimization_barrier((grad_qkv_part, from_y))
    joined = joined[0].astype(f32) + from_x[:BLOCK] + from_y.astype(f32)
    ffn_branch = joined[:, :D]
    outputs = (middle + ffn_branch).astype(bf16)
    grad_out = sum_along_z(joined[:, D:].reshape(depth, rows, D))
    grad_qkv_part, expand_grad = lax.optimization_barrier((grad_qkv_part, expand_grad))
    grad_qkv_part = grad_qkv_part.reshape(chips, 2, rows, 3 * HD)
    grad_qkv_own = lax.dynamic_index_in_dim(grad_qkv_part, core, 1, keepdims=False)
    grad_qkv_other = lax.dynamic_index_in_dim(grad_qkv_part, 1 - core, 1, keepdims=False)
    grad_qkv_own = grad_qkv_own.astype(f32) + swap(grad_qkv_other, "core").astype(f32)
    values = grad_qkv_own[:, :, 2 * HD :]
    values = jnp.concatenate([values[:, : rows // 2], values[:, rows // 2 :]], axis=2)
    joined = jnp.concatenate(
        [grad_project, grad_qkv_own[:, :, : 2 * HD].astype(bf16), values.astype(bf16)], axis=1
    )
    joined = lax.all_to_all(joined, CHIPS, 0, 0, tiled=True)

    bias_part = jnp.where(
        jnp.arange(H)[None, :] == head, bias_grad[0, :2][:, None], jnp.zeros((2, H), f32)
    )
    packed = jnp.concatenate(
        [
            attn_grad[:, 0] / attn_gain,
            grad_ffn[0],
            gain_grad[0],
            bias_part.reshape(-1),
            squares[:2, 0],
            jnp.sum(ffn_branch * ffn_branch)[None],
            jnp.zeros((93,), f32),
        ]
    )
    summed = sum_everywhere(packed.reshape(-1, 128))
    grad_down = feed_grad[8 * rows :].astype(f32)
    grad_expand = widen(expand_grad, depth, hidden_rows)
    joined, grad_down, grad_expand = lax.optimization_barrier((joined, grad_down, grad_expand))
    grad_inputs, grad_qkv = input_back(
        over_sharers(joined, sharers), qkv_full, inputs, attn_gain[None], grad_middle
    )
    summed = summed.reshape(-1)
    at = 2 * D + 2 * HD
    root_means = jnp.sqrt(summed[at + 2 * H : at + 2 * H + 3] / (tokens * D))
    return (
        outputs,
        grad_inputs,
        grad_qkv,
        grad_out,
        grad_expand,
        grad_down,
        summed[:D],
        summed[D : 2 * D],
        summed[2 * D : 2 * D + HD],
        summed[2 * D + HD : at],
        summed[at : at + 2 * H].reshape(2, H),
        root_means,
    )


def solution(mesh):
    grid = mesh.devices if mesh.axis_names == ("head", "blk") else mesh.devices.T
    heads, blks = grid.shape
    mesh = Mesh(grid.reshape(heads // 2, 2, blks // 2, 2), ("hx", "core", "bz", "by"))
    split = P(DEVICES, None)

    return jax.shard_map(
        body,
        mesh=mesh,
        in_specs=(split,) * 2 + (P(),) * 5 + (split,) * 4 + (P(),) * 3,
        out_specs=(split,) * 6 + (P(),) * 6,
        check_vma=False,
    )
```

```python
from functools import partial

import jax
import jax.numpy as jnp
from jax import lax
from jax.experimental import pallas as pl
from jax.experimental.pallas import tpu as pltpu
from jax.sharding import Mesh
from jax.sharding import PartitionSpec as P


D = 1024
H = 16
HD = 64
BLOCK = 128
NVAR = 4
EPSILON = 1e-05
THETA = 10000.0

DEVICES = ("bz", "by", "hx", "core")
CHIPS = ("bz", "by", "hx")
PLANE = ("by", "hx", "core")

SEGMENT_LANE = 64
VARIATE_LANE = 76
OWN_VARIATE_LANE = 88
MASK = -512.0
QUERY_TILE = 512
KEY_TILE = 512
PROJECT_BLOCKS = 4

bf16 = jnp.bfloat16
f32 = jnp.float32


def dot(left, right, dims):
    return lax.dot_general(left, right, (dims, ((), ())), preferred_element_type=f32)


def norm_rows(values, gain):
    factor = lax.rsqrt(jnp.mean(values * values, axis=-1, keepdims=True) + EPSILON)
    return values * factor * gain


def norm_back(values, gain, grad):
    factor = lax.rsqrt(jnp.mean(values * values, axis=-1, keepdims=True) + EPSILON)
    scaled = grad * gain
    inner = jnp.mean(scaled * values, axis=-1, keepdims=True)
    grad_values = factor * (scaled - values * (factor * factor) * inner)
    return grad_values, grad * values * factor


def swap(shard, axis):
    return lax.ppermute(shard, axis, [(0, 1), (1, 0)])


def plane_gather(shard):
    mine = jnp.concatenate(quarters(shard), axis=0)
    return mine, swap(mine, "core")


def chip_gather(shard, rider, late):
    depth = lax.axis_size("bz")
    chips = depth * 4
    z, y, x = lax.axis_index("bz"), lax.axis_index("by"), lax.axis_index("hx")
    at = jnp.arange(chips, dtype=jnp.int32)
    if depth > 4:
        pieces = lax.all_gather(shard, CHIPS, axis=0)
        return list(pieces), at, (swap(rider, "hx"), swap(rider, "by")), late
    column = z_shifts([shard] * (depth - 1))
    across_x, across_y = [swap(shard, "hx")], [swap(shard, "by")]
    across_x += [swap(piece, "hx") for piece in column]
    across_y += [swap(piece, "by") for piece in column]
    across_x, across_y, late = lax.optimization_barrier((across_x, across_y, late))
    corner = [swap(across_x[i], "by") if i > 1 else swap(across_y[i], "hx") for i in range(depth)]
    riders = swap(rider, "hx"), swap(rider, "by")
    pieces = [shard, across_x[0], across_y[0], corner[0]]
    pieces += column + across_x[1:] + across_y[1:] + corner[1:]
    back = (z - at // 4) % depth
    flips = ((at % 2) ^ x) + 2 * (((at // 2) % 2) ^ y)
    where = jnp.where(back == 0, flips, 4 + flips * (depth - 1) + back - 1).astype(jnp.int32)
    return pieces, where, riders, late


def sum_everywhere(values):
    for axis in ("core", "hx", "by"):
        values = values + swap(values, axis)
    depth = lax.axis_size("bz")
    if depth > 4:
        step = 1
        while step < depth:
            values = values + lax.ppermute(values, "bz", [(i, i ^ step) for i in range(depth)])
            step *= 2
        return values
    shifted = z_shifts([values] * (depth - 1))
    copies = jnp.stack([values] + shifted)
    back = (lax.axis_index("bz") - jnp.arange(depth, dtype=jnp.int32)) % depth
    return sum(lax.dynamic_index_in_dim(copies, back[z], 0, keepdims=False) for z in range(depth))


def z_shifts(values):
    depth = lax.axis_size("bz")
    return [
        lax.ppermute(value, "bz", [(i, (i + by + 1) % depth) for i in range(depth)])
        for by, value in enumerate(values)
    ]


def sum_along_z(parts):
    depth = lax.axis_size("bz")
    if depth > 4:
        parts = parts.reshape(-1, parts.shape[2]).astype(bf16)
        return lax.psum_scatter(parts, "bz", scatter_dimension=0, tiled=True).astype(f32)
    z = lax.axis_index("bz")
    parts = [
        lax.dynamic_index_in_dim(parts, (z + by) % depth, 0, keepdims=False) for by in range(depth)
    ]
    arrived = z_shifts([part.astype(bf16) for part in parts[1:]])
    return sum([part.astype(f32) for part in arrived], parts[0])


def quarters(shard):
    half = shard.shape[0] // 2
    across_x = swap(shard, "hx")
    across_y = swap(shard, "by")
    return [shard, across_x, across_y, swap(across_y[:half], "hx"), swap(across_x[half:], "by")]


def plane_scatter(mine, other):
    rows = mine.shape[0] // 4
    half = rows // 2
    mine = mine.astype(f32) + swap(other, "core").astype(f32)
    corner = mine[3 * rows :].astype(bf16)
    for_y = swap(corner[:half], "hx").astype(f32)
    for_x = swap(corner[half:], "by").astype(f32)
    to_x = mine[rows : 2 * rows]
    to_y = mine[2 * rows : 3 * rows]
    to_x = jnp.concatenate([to_x[:half], to_x[half:] + for_x], axis=0).astype(bf16)
    to_y = jnp.concatenate([to_y[:half] + for_y, to_y[half:]], axis=0).astype(bf16)
    from_x = swap(to_x, "hx")
    from_y = swap(to_y, "by")
    return mine[:rows], from_x, from_y


def plane_members():
    by, hx, core = lax.axis_index("by"), lax.axis_index("hx"), lax.axis_index("core")
    members = []
    for core_flip in (0, 1):
        for x_flip, y_flip in ((0, 0), (1, 0), (0, 1), (1, 1)):
            members.append((by ^ y_flip) * 4 + (hx ^ x_flip) * 2 + (core ^ core_flip))
    return members


def lanes(shape):
    return lax.broadcasted_iota(jnp.int32, shape, len(shape) - 1)


def half_mean(values, lane):
    low = jnp.sum(jnp.where(lane < HD, values, 0.0), axis=-1, keepdims=True)
    high = jnp.sum(jnp.where(lane < HD, 0.0, values), axis=-1, keepdims=True)
    return jnp.where(lane < HD, low, high) * (1.0 / HD)


def swap_halves(values, lane):
    return jnp.where(
        (lane & (HD - 1)) < HD // 2, pltpu.roll(values, 96, 1), pltpu.roll(values, 32, 1)
    )


def mask_matrix(segments, bias_ref):
    shape = (128, 128)
    row = lax.broadcasted_iota(jnp.int32, shape, 0)
    lane = lax.broadcasted_iota(jnp.int32, shape, 1)
    segment = row - SEGMENT_LANE
    here = lane - SEGMENT_LANE
    apart = (segment >= 0) & (segment < segments) & (here >= 0) & (here < segments)
    matrix = jnp.where(apart & (here != segment), MASK, 0.0)
    variate = row - VARIATE_LANE
    known = (variate >= 0) & (variate < NVAR)
    copy = (lane - VARIATE_LANE) // NVAR
    same = (lane - VARIATE_LANE) % NVAR == variate
    bias = jnp.where(same, bias_ref[1], bias_ref[0])
    high = bias.astype(bf16).astype(f32)
    mid = (bias - high).astype(bf16).astype(f32)
    value = jnp.where(copy == 0, high, jnp.where(copy == 1, mid, bias - high - mid))
    biased = known & (lane >= VARIATE_LANE) & (lane < VARIATE_LANE + 3 * NVAR)
    matrix = jnp.where(biased, value, matrix)
    return jnp.where(known & (lane == OWN_VARIATE_LANE + variate), 1.0, matrix).astype(bf16)


def project_kernel(where_ref, bias_ref, *refs, chips, segments):
    piece_refs, refs = refs[:chips], refs[chips:]
    gain_ref, weight_ref, cosine_ref, sine_ref, gains_ref, hot_ref = refs[:6]
    normed_ref, raw_ref, query_ref, kv_ref, out_ref, x_ref, mask_ref, arrived = refs[6:]
    step = pl.program_id(0)

    @pl.when(step == 0)
    def _():
        copies = [
            pltpu.make_async_copy(piece_refs[i], x_ref.at[i], arrived.at[i]) for i in range(chips)
        ]
        for copy in copies:
            copy.start()
        mask_ref[...] = mask_matrix(segments, bias_ref)
        for copy in copies:
            copy.wait()

    places = [where_ref[step * PROJECT_BLOCKS + i] for i in range(PROJECT_BLOCKS)]
    for i, place in enumerate(places):
        out_ref[i] = x_ref[place, BLOCK:]
    x = jnp.concatenate([x_ref[place, :BLOCK] for place in places], axis=0).astype(f32)
    normed = norm_rows(x, gain_ref[...]).astype(bf16)
    normed_ref[...] = normed
    project = dot(normed, weight_ref[...], ((1,), (0,)))
    both = project[:, : 2 * HD]
    value = project[:, 2 * HD :]
    raw_ref[...] = both
    lane = lanes(both.shape)
    scaled = both * lax.rsqrt(half_mean(both * both, lane) + EPSILON) * gains_ref[...]
    turned = scaled * cosine_ref[...] + swap_halves(scaled, lane) * sine_ref[...]
    turned = turned.astype(bf16).astype(f32)
    hot = hot_ref[...]
    query_ref[...] = jnp.where(lane < HD, turned, hot.astype(f32)).astype(bf16)
    key = pltpu.roll(turned * HD ** (-0.5), HD, 1)
    ones = jnp.where((lane >= HD) & (lane < HD + 3), 1.0, 0.0)
    kv_ref[:, :128] = jnp.where(lane < HD, key, dot(hot, mask_ref[...], ((1,), (0,)))).astype(bf16)
    kv_ref[:, 128:] = jnp.where(lane < HD, value, ones).astype(bf16)


def project(where, bias, pieces, gain, weight, cosine, sine, gains, hot, segments):
    blocks = len(pieces)
    rows = blocks * BLOCK
    step_rows = PROJECT_BLOCKS * BLOCK
    out_rows = pieces[0].shape[0] - BLOCK
    row_spec = lambda width: pl.BlockSpec((step_rows, width), lambda j, *unused: (j, 0))
    whole = lambda array: pl.BlockSpec(array.shape, lambda j, *unused: (0, 0))
    anywhere = pl.BlockSpec(memory_space=pl.ANY)
    tables = [whole(gain), whole(weight), row_spec(128), row_spec(128), whole(gains)]
    return pl.pallas_call(
        partial(project_kernel, chips=blocks, segments=segments),
        grid_spec=pltpu.PrefetchScalarGridSpec(
            num_scalar_prefetch=2,
            grid=(blocks // PROJECT_BLOCKS,),
            in_specs=[anywhere] * blocks + tables + [row_spec(128)],
            out_specs=[
                row_spec(D),
                row_spec(128),
                row_spec(128),
                row_spec(256),
                pl.BlockSpec((PROJECT_BLOCKS, out_rows, D), lambda j, *unused: (j, 0, 0)),
            ],
            scratch_shapes=[
                pltpu.VMEM((blocks, BLOCK + out_rows, D), bf16),
                pltpu.VMEM((128, 128), bf16),
                pltpu.SemaphoreType.DMA((blocks,)),
            ],
        ),
        out_shape=[
            jax.ShapeDtypeStruct((rows, D), bf16),
            jax.ShapeDtypeStruct((rows, 128), f32),
            jax.ShapeDtypeStruct((rows, 128), bf16),
            jax.ShapeDtypeStruct((rows, 256), bf16),
            jax.ShapeDtypeStruct((blocks, out_rows, D), bf16),
        ],
        name="project",
    )(where, bias, *pieces, gain, weight, cosine, sine, gains, hot)


def sort_keys(place_ref, own_ref, other_ref, keys_ref):
    blocks = own_ref.shape[0] // BLOCK
    for half, source_ref in ((0, own_ref), (1, other_ref)):

        def put(j, unused, half=half, source_ref=source_ref):
            source = pl.multiple_of(j * BLOCK, BLOCK)
            target = pl.multiple_of(place_ref[half * blocks + j] * BLOCK, BLOCK)
            keys_ref[pl.ds(target, BLOCK), :] = source_ref[pl.ds(source, BLOCK), :]
            return unused

        lax.fori_loop(0, blocks, put, 0, unroll=4)


def block_start(order_ref, index):
    return pl.multiple_of(order_ref[index] * BLOCK, BLOCK)


def attend_kernel(
    order_ref,
    place_ref,
    low_ref,
    high_ref,
    query_ref,
    own_ref,
    other_ref,
    kept_ref,
    attended_ref,
    keys_ref,
):
    tile = pl.program_id(0)
    count = QUERY_TILE // BLOCK

    @pl.when(tile == 0)
    def _():
        sort_keys(place_ref, own_ref, other_ref, keys_ref)
        if order_ref.shape[0] * BLOCK != query_ref.shape[0]:
            kept_ref[...] = jnp.zeros_like(kept_ref)
            attended_ref[...] = jnp.zeros_like(attended_ref)

    starts = [block_start(order_ref, tile * count + i) for i in range(count)]
    query = jnp.concatenate([query_ref[pl.ds(start, BLOCK), :] for start in starts], axis=0)

    def chunk(index, accumulated):
        window = pl.ds(pl.multiple_of(index * KEY_TILE, KEY_TILE), KEY_TILE)
        expo = jnp.exp(dot(query, keys_ref[window, :128], ((1,), (1,))))
        return accumulated + dot(expo.astype(bf16), keys_ref[window, 128:], ((1,), (0,)))

    accumulated = lax.fori_loop(
        low_ref[tile], high_ref[tile], chunk, jnp.zeros((QUERY_TILE, 128), f32)
    )
    totals = accumulated[:, HD : HD + 1]
    lane = lanes(accumulated.shape)
    kept = jnp.where(lane < HD, accumulated / totals, totals)
    for i, start in enumerate(starts):
        piece = kept[i * BLOCK : (i + 1) * BLOCK]
        kept_ref[pl.ds(start, BLOCK), :] = piece
        attended_ref[order_ref[tile * count + i]] = piece.T[:HD].astype(bf16)


def fixed(array):
    return pl.BlockSpec(
        array.shape, lambda *unused: (0,) * len(array.shape), pipeline_mode=pl.Buffered(1)
    )


def attend(order, place, low, high, query, own, other):
    rows = query.shape[0]
    operands = (query, own, other)
    outs = (
        jax.ShapeDtypeStruct((rows, 128), f32),
        jax.ShapeDtypeStruct((rows // BLOCK, HD, BLOCK), bf16),
    )
    return pl.pallas_call(
        attend_kernel,
        grid_spec=pltpu.PrefetchScalarGridSpec(
            num_scalar_prefetch=4,
            grid=(low.shape[0],),
            in_specs=[fixed(array) for array in operands],
            out_specs=[fixed(array) for array in outs],
            scratch_shapes=[pltpu.VMEM((2 * rows, 256), bf16)],
        ),
        out_shape=list(outs),
        name="attend",
    )(order, place, low, high, *operands)


def attend_back_kernel(
    order_ref,
    place_ref,
    source_ref,
    low_ref,
    high_ref,
    query_ref,
    own_ref,
    other_ref,
    kept_ref,
    grad_ref,
    query_grad_ref,
    own_grad_ref,
    other_grad_ref,
    bias_ref,
    keys_ref,
    sorted_ref,
    wide_ref,
    sums_ref,
    every_ref,
    same_ref,
):
    step = pl.program_id(0)
    own_rows = own_ref.shape[0]
    taken = order_ref.shape[0]

    @pl.when(step == 0)
    def _():
        sort_keys(place_ref, own_ref, other_ref, keys_ref)
        every_ref[...] = jnp.zeros_like(every_ref)
        same_ref[...] = jnp.zeros_like(same_ref)
        sums_ref[...] = jnp.zeros_like(sums_ref)
        if taken * BLOCK != own_rows:
            query_grad_ref[...] = jnp.zeros_like(query_grad_ref)
        lane = lanes((BLOCK, 128))

        def put(i, unused):
            source = pl.ds(block_start(order_ref, i), BLOCK)
            target = pl.ds(pl.multiple_of(i * BLOCK, BLOCK), BLOCK)
            sorted_ref[target, :] = query_ref[source, :]
            kept = kept_ref[source, :]
            grad = grad_ref[order_ref[i]].astype(f32)
            grad = jnp.concatenate([grad, jnp.zeros_like(grad)], axis=0).T
            inverse = 1.0 / kept[:, HD : HD + 1]
            center = jnp.sum(grad * kept, axis=1, keepdims=True) * inverse
            center_high = center.astype(bf16).astype(f32)
            center_rest = center - center_high
            center_mid = center_rest.astype(bf16).astype(f32)
            center_low = center_rest - center_mid
            wide = jnp.where(lane == HD, -center_high, 0.0)
            wide = jnp.where(lane == HD + 1, -center_mid, wide)
            wide = jnp.where(lane == HD + 2, -center_low, wide)
            wide_ref[target, :] = jnp.where(lane < HD, grad * inverse, wide).astype(bf16)
            return unused

        lax.fori_loop(0, taken, put, 0, unroll=4)

    window = pl.ds(pl.multiple_of(step * KEY_TILE, KEY_TILE), KEY_TILE)
    key = keys_ref[window, :128]
    value = keys_ref[window, 128:]

    def tile(index, grads):
        rows = pl.ds(pl.multiple_of(index * QUERY_TILE, QUERY_TILE), QUERY_TILE)
        query = sorted_ref[rows, :]
        wide = wide_ref[rows, :]
        expo = jnp.exp(dot(key, query, ((1,), (1,))))
        score_low = (expo * dot(value, wide, ((1,), (1,)))).astype(bf16)
        sums_ref[rows, :] += dot(score_low, key, ((0,), (0,)))
        return (
            grads[0] + dot(score_low, query, ((1,), (0,))),
            grads[1] + dot(expo.astype(bf16), wide, ((1,), (0,))),
        )

    empty = jnp.zeros((KEY_TILE, 128), f32)
    key_grad, value_grad = lax.fori_loop(low_ref[step], high_ref[step], tile, (empty, empty))
    lane = lanes(key_grad.shape)
    joined = jnp.where(lane < HD, value_grad, pltpu.roll(key_grad, HD, 1) * HD ** (-0.5))
    joined = joined.astype(bf16)
    for i in range(KEY_TILE // BLOCK):
        source = source_ref[step * (KEY_TILE // BLOCK) + i] * BLOCK
        piece = joined[i * BLOCK : (i + 1) * BLOCK]

        @pl.when(source < own_rows)
        def _(source=source, piece=piece):
            own_grad_ref[pl.ds(pl.multiple_of(source, BLOCK), BLOCK), :] = piece

        @pl.when(source >= own_rows)
        def _(source=source, piece=piece):
            other_grad_ref[pl.ds(pl.multiple_of(source - own_rows, BLOCK), BLOCK), :] = piece

    every = jnp.where((lane >= VARIATE_LANE) & (lane < VARIATE_LANE + NVAR), key_grad, 0.0)
    shift = 128 + VARIATE_LANE - OWN_VARIATE_LANE
    same = every * pltpu.roll(key.astype(f32), shift, 1)
    every_ref[...] += jnp.sum(every.reshape(-1, 8, 128), axis=0)
    same_ref[...] += jnp.sum(same.reshape(-1, 8, 128), axis=0)

    @pl.when(step == pl.num_programs(0) - 1)
    def _():
        def put(i, unused):
            target = pl.ds(block_start(order_ref, i), BLOCK)
            rows = pl.ds(pl.multiple_of(i * BLOCK, BLOCK), BLOCK)
            query_grad_ref[target, :] = sums_ref[rows, :].astype(bf16)
            return unused

        lax.fori_loop(0, taken, put, 0, unroll=4)
        every = jnp.sum(every_ref[...], keepdims=True)
        same = jnp.sum(same_ref[...], keepdims=True)
        bias_lane = lanes((8, 128))
        bias_ref[...] = jnp.where(
            bias_lane == 0, every - same, jnp.where(bias_lane == 1, same, 0.0)
        )


def attend_back(order, place, source, low, high, query, own, other, kept, grad):
    rows = query.shape[0]
    taken = order.shape[0] * BLOCK
    operands = (query, own, other, kept, grad)
    outs = tuple(jax.ShapeDtypeStruct((rows, 128), bf16) for _ in range(3)) + (
        jax.ShapeDtypeStruct((8, 128), f32),
    )
    return pl.pallas_call(
        attend_back_kernel,
        grid_spec=pltpu.PrefetchScalarGridSpec(
            num_scalar_prefetch=5,
            grid=(low.shape[0],),
            in_specs=[fixed(array) for array in operands],
            out_specs=[fixed(array) for array in outs],
            scratch_shapes=[
                pltpu.VMEM((2 * rows, 256), bf16),
                pltpu.VMEM((taken, 128), bf16),
                pltpu.VMEM((taken, 128), bf16),
                pltpu.VMEM((taken, 128), f32),
                pltpu.VMEM((8, 128), f32),
                pltpu.VMEM((8, 128), f32),
            ],
        ),
        out_shape=list(outs),
        name="attend_back",
    )(order, place, source, low, high, *operands)


def project_back_kernel(
    query_grad_ref,
    own_ref,
    other_ref,
    raw_ref,
    cosine_ref,
    sine_ref,
    gains_ref,
    normed_ref,
    forward_ref,
    grad_ref,
    weight_grad_ref,
    gain_grad_ref,
    attn_grad_ref,
    weight_ref,
    gain_ref,
):
    step = pl.program_id(0)

    @pl.when(step == 0)
    def _():
        weight_ref[...] = jnp.zeros_like(weight_ref)
        gain_ref[...] = jnp.zeros_like(gain_ref)

    kv_grad = own_ref[...].astype(f32) + other_ref[...].astype(f32)
    kv_grad = kv_grad.astype(bf16).astype(f32)
    lane = lanes(kv_grad.shape)
    turned = jnp.where(lane < HD, query_grad_ref[...].astype(f32), kv_grad)
    grad = turned * cosine_ref[...] - swap_halves(turned, lane) * sine_ref[...]
    raw = raw_ref[...]
    factor = lax.rsqrt(half_mean(raw * raw, lane) + EPSILON)
    scaled = grad * gains_ref[...]
    inner = half_mean(scaled * raw, lane)
    both = factor * (scaled - raw * (factor * factor) * inner)
    gain_ref[...] += jnp.sum(grad * raw * factor, axis=0, keepdims=True)
    full = jnp.concatenate([both, jnp.where(lane < HD, kv_grad, 0.0)], axis=1)
    for i in range(grad_ref.shape[0]):
        grad_ref[i] = full[i * BLOCK : (i + 1) * BLOCK].T[: 3 * HD].astype(bf16)
    weight_ref[...] += dot(normed_ref[...], full.astype(bf16), ((0,), (0,)))

    @pl.when(step == pl.num_programs(0) - 1)
    def _():
        weight_grad_ref[...] = weight_ref[:, : 3 * HD].astype(bf16)
        gain_grad_ref[...] = jnp.broadcast_to(gain_ref[...], gain_grad_ref.shape)
        forward = forward_ref[...].astype(f32)
        attn = jnp.sum(weight_ref[...] * forward, axis=1, keepdims=True)
        attn_grad_ref[...] = jnp.broadcast_to(attn, attn_grad_ref.shape)


def project_back(query_grad, own, other, raw, cosine, sine, gains, normed, forward):
    rows = query_grad.shape[0]
    step_rows = 4 * BLOCK
    row_spec = lambda width: pl.BlockSpec((step_rows, width), lambda j: (j, 0))
    whole = lambda shape: pl.BlockSpec(shape, lambda j: (0, 0))
    return pl.pallas_call(
        project_back_kernel,
        grid=(rows // step_rows,),
        in_specs=[row_spec(128)] * 6 + [whole(gains.shape), row_spec(D), whole(forward.shape)],
        out_specs=[
            pl.BlockSpec((step_rows // BLOCK, 3 * HD, BLOCK), lambda j: (j, 0, 0)),
            whole((D, 3 * HD)),
            whole((8, 128)),
            whole((D, 128)),
        ],
        out_shape=[
            jax.ShapeDtypeStruct((rows // BLOCK, 3 * HD, BLOCK), bf16),
            jax.ShapeDtypeStruct((D, 3 * HD), bf16),
            jax.ShapeDtypeStruct((8, 128), f32),
            jax.ShapeDtypeStruct((D, 128), f32),
        ],
        scratch_shapes=[pltpu.VMEM((D, 4 * HD), f32), pltpu.VMEM((1, 128), f32)],
        name="project_back",
    )(query_grad, own, other, raw, cosine, sine, gains, normed, forward)


def feed_kernel(
    second_mine_ref,
    second_other_ref,
    grad_mine_ref,
    grad_other_ref,
    weight_ref,
    ffn_mine_ref,
    ffn_other_ref,
    back_mine_ref,
    back_other_ref,
    expand_out_ref,
    down_out_ref,
    expand_ref,
    down_ref,
    expand_grad_ref,
    down_grad_ref,
):
    step = pl.program_id(0)
    half = pl.num_programs(0) // 2
    depth, both_rows, width = weight_ref.shape
    down_rows = down_ref.shape[0] // depth
    expand_rows = both_rows - down_rows

    @pl.when(step == 0)
    def _():
        for z in range(depth):
            expand_ref[z * expand_rows : (z + 1) * expand_rows] = weight_ref[z, :expand_rows]
            down_ref[z * down_rows : (z + 1) * down_rows] = weight_ref[z, expand_rows:]
        expand_grad_ref[...] = jnp.zeros_like(expand_grad_ref)
        down_grad_ref[...] = jnp.zeros_like(down_grad_ref)

    second = jnp.where(step < half, second_mine_ref[...], second_other_ref[...])
    grad = jnp.where(step < half, grad_mine_ref[...], grad_other_ref[...])
    expand = dot(second, expand_ref[...], ((1,), (0,)))
    gate = expand[:, : width // 2]
    up = expand[:, width // 2 :]
    sigmoid = 1.0 / (1.0 + jnp.exp(-gate))
    silu = gate * sigmoid
    hidden = (silu * up).astype(bf16)
    grad_hidden = dot(grad, down_ref[...], ((1,), (1,)))
    grad_gate = grad_hidden * up * (sigmoid * (1.0 + gate * (1.0 - sigmoid)))
    rows = jnp.concatenate([grad_gate, grad_hidden * silu], axis=1).astype(bf16)
    ffn = dot(hidden, down_ref[...], ((1,), (0,))).astype(bf16)
    back = dot(rows, expand_ref[...], ((1,), (1,))).astype(bf16)
    expand_grad_ref[...] += dot(second, rows, ((0,), (0,)))
    down_grad_ref[...] += dot(hidden, grad, ((0,), (0,)))

    @pl.when(step < half)
    def _():
        ffn_mine_ref[...] = ffn
        back_mine_ref[...] = back

    @pl.when(step >= half)
    def _():
        ffn_other_ref[...] = ffn
        back_other_ref[...] = back

    @pl.when(step == pl.num_programs(0) - 1)
    def _():
        expand_out_ref[...] = expand_grad_ref[...].astype(bf16)
        down_out_ref[...] = down_grad_ref[...].astype(bf16)


def feed(second, grad, weight, down_rows):
    rows = second[0].shape[0]
    tile = 256
    steps = rows // tile
    depth, both_rows, width = weight.shape
    mine = pl.BlockSpec((tile, D), lambda i: (jnp.minimum(i, steps - 1), 0))
    other = pl.BlockSpec((tile, D), lambda i: (jnp.maximum(i - steps, 0), 0))
    whole = pl.BlockSpec(weight.shape, lambda i: (0, 0, 0), pipeline_mode=pl.Buffered(1))
    token_rows = jax.ShapeDtypeStruct((rows, D), bf16)
    expand_out = jax.ShapeDtypeStruct((depth * (both_rows - down_rows), width), bf16)
    down_out = jax.ShapeDtypeStruct((depth * down_rows, D), bf16)
    return pl.pallas_call(
        feed_kernel,
        grid=(2 * steps,),
        in_specs=[mine, other, mine, other, whole],
        out_specs=[mine, other, mine, other, fixed(expand_out), fixed(down_out)],
        out_shape=[token_rows] * 4 + [expand_out, down_out],
        scratch_shapes=[
            pltpu.VMEM((depth * (both_rows - down_rows), width), bf16),
            pltpu.VMEM((depth * down_rows, D), bf16),
            pltpu.VMEM((depth * (both_rows - down_rows), width), f32),
            pltpu.VMEM((depth * down_rows, D), f32),
        ],
        name="feed",
    )(*second, *grad, weight)


def out_kernel(parts_ref, x_ref, weight_ref, gain_ref, middle_ref, second_ref, squares_ref):
    branch = dot(parts_ref[...], weight_ref[...], ((0,), (0,)))
    x = x_ref[...].astype(f32)
    middle = x + branch
    middle_ref[...] = middle
    second_ref[...] = norm_rows(middle, gain_ref[...]).astype(bf16)
    row = lax.broadcasted_iota(jnp.int32, squares_ref.shape, 0)
    x_sum = jnp.sum(x * x, keepdims=True)
    branch_sum = jnp.sum(branch * branch, keepdims=True)
    squares_ref[...] = jnp.where(row == 0, x_sum, branch_sum)


def out_project(parts, x, weight, gain):
    rows = x.shape[0]
    return pl.pallas_call(
        out_kernel,
        out_shape=[
            jax.ShapeDtypeStruct((rows, D), f32),
            jax.ShapeDtypeStruct((rows, D), bf16),
            jax.ShapeDtypeStruct((8, 128), f32),
        ],
        name="out_project",
    )(parts, x, weight, gain)


def middle_back_kernel(
    own_ref,
    from_x_ref,
    from_y_ref,
    middle_ref,
    cotangent_ref,
    gain_ref,
    weight_ref,
    grad_middle_ref,
    branch_ref,
    parts_ref,
    gain_grad_ref,
):
    grad_second = own_ref[...] + from_x_ref[...].astype(f32) + from_y_ref[...].astype(f32)
    grad_middle, gain_rows = norm_back(middle_ref[...], gain_ref[...], grad_second)
    grad_middle = cotangent_ref[...].astype(f32) + grad_middle
    grad_middle_ref[...] = grad_middle
    branch = grad_middle.astype(bf16)
    branch_ref[...] = branch
    parts_ref[...] = dot(weight_ref[...], branch, ((1,), (1,))).astype(bf16)
    gain_grad_ref[...] = jnp.broadcast_to(
        jnp.sum(gain_rows, axis=0, keepdims=True), gain_grad_ref.shape
    )


def middle_back(own, from_x, from_y, middle, cotangent, gain, weight):
    rows = middle.shape[0]
    return pl.pallas_call(
        middle_back_kernel,
        out_shape=[
            jax.ShapeDtypeStruct((rows, D), f32),
            jax.ShapeDtypeStruct((rows, D), bf16),
            jax.ShapeDtypeStruct((D, rows), bf16),
            jax.ShapeDtypeStruct((8, D), f32),
        ],
        name="middle_back",
    )(own, from_x, from_y, middle, cotangent, gain, weight)


def out_grad_kernel(
    members_ref,
    merged_ref,
    branch_ref,
    ffn_mine_ref,
    ffn_other_ref,
    mine_ref,
    other_ref,
    grad_ref,
    depth,
):
    shard = mine_ref.shape[0] // 4
    rows = shard // depth
    grad_ref[...] = dot(merged_ref[...], branch_ref[...], ((1,), (0,)))
    mine_ref[:, :D] = ffn_mine_ref[...]
    other_ref[:, :D] = ffn_other_ref[...]
    for place in range(8):
        target_ref = mine_ref if place < 4 else other_ref
        for z in range(depth):
            source = pl.multiple_of((z * 8 + members_ref[place]) * rows, rows)
            target = (place % 4) * shard + z * rows
            target_ref[target : target + rows, D:] = grad_ref[pl.ds(source, rows), :].astype(bf16)


def out_grad(members, merged, branch, ffn_mine, ffn_other, depth):
    joined = jax.ShapeDtypeStruct((ffn_mine.shape[0], 2 * D), bf16)
    operands = (merged, branch, ffn_mine, ffn_other)
    return pl.pallas_call(
        partial(out_grad_kernel, depth=depth),
        grid_spec=pltpu.PrefetchScalarGridSpec(
            num_scalar_prefetch=1,
            grid=(1,),
            in_specs=[fixed(array) for array in operands],
            out_specs=[fixed(joined), fixed(joined)],
            scratch_shapes=[pltpu.VMEM((D, D), f32)],
        ),
        out_shape=[joined, joined],
        name="out_grad",
    )(members, *operands)


def input_back_kernel(
    joined_ref, weight_ref, x_ref, gain_ref, middle_ref, grad_ref, qkv_ref, wide_ref
):
    heads = joined_ref.shape[0]
    rows = qkv_ref.shape[0]
    for head in range(heads):
        wide_ref[head * 3 * HD : (head + 1) * 3 * HD] = joined_ref[head, : 3 * HD]
    for pair in range(heads // 2):
        left = joined_ref[2 * pair, 3 * HD :].astype(f32)
        right = joined_ref[2 * pair + 1, 3 * HD :].astype(f32)
        at = pair * 2 * HD
        low = jnp.concatenate([left[:, :HD], right[:, :HD]], axis=1)
        high = jnp.concatenate([left[:, HD:], right[:, HD:]], axis=1)
        qkv_ref[:, at : at + 2 * HD] = low[:rows]
        qkv_ref[:, D + at : D + at + 2 * HD] = high[:rows]
        qkv_ref[: rows // 2, 2 * D + at : 2 * D + at + 2 * HD] = low[rows:]
        qkv_ref[rows // 2 :, 2 * D + at : 2 * D + at + 2 * HD] = high[rows:]
    grad_normed = dot(wide_ref[...], weight_ref[...], ((0,), (1,)))
    grad, _ = norm_back(x_ref[...].astype(f32), gain_ref[...], grad_normed)
    grad_ref[...] = middle_ref[...] + grad


def input_back(joined, weight, x, gain, middle):
    rows = x.shape[0]
    return pl.pallas_call(
        input_back_kernel,
        out_shape=[
            jax.ShapeDtypeStruct((rows, D), f32),
            jax.ShapeDtypeStruct(((joined.shape[1] - 3 * HD) * 2 // 3, 3 * D), f32),
        ],
        scratch_shapes=[pltpu.VMEM((3 * D, rows), bf16)],
        name="input_back",
    )(joined, weight, x, gain, middle)


def widen_kernel(parts_ref, grad_ref):
    sources, _, width = parts_ref.shape
    for source in range(sources):
        for at in range(width // 128):
            to = (at * sources + source) * 128
            grad_ref[:, to : to + 128] = parts_ref[source, :, at * 128 : (at + 1) * 128].astype(f32)


def widen(parts, depth, hidden_rows):
    sources, rows, width = parts.shape
    if hidden_rows != 128:
        parts = parts.reshape(sources, rows, 2, depth, hidden_rows)
        return parts.transpose(1, 2, 3, 0, 4).reshape(rows, -1).astype(f32)
    return pl.pallas_call(
        widen_kernel, out_shape=jax.ShapeDtypeStruct((rows, sources * width), f32), name="widen"
    )(parts)


def token_meta(seq_lengths, block_order):
    blocks = block_order.shape[0]
    packed_at = jnp.repeat(block_order, BLOCK) * BLOCK + jnp.tile(
        jnp.arange(BLOCK, dtype=jnp.int32), blocks
    )
    ends = jnp.cumsum(seq_lengths)
    after = packed_at[:, None] >= ends[None, :]
    segment = jnp.sum(after.astype(jnp.int32), axis=1)
    begin = jnp.max(jnp.where(after, ends[None, :], jnp.zeros_like(ends)[None, :]), axis=1)
    return (segment, packed_at - begin, ends)


def own_rows(array, core):
    pairs = array.reshape(-1, 2, BLOCK)
    return lax.dynamic_index_in_dim(pairs, core, 1, keepdims=False).reshape(-1)


def one_hot_rows(segment, variate):
    lane = jnp.arange(128, dtype=jnp.int32)[None, :]
    hot = lane == SEGMENT_LANE + segment[:, None]
    for copy in range(3):
        hot = hot | (lane == VARIATE_LANE + copy * NVAR + variate[:, None])
    return hot.astype(bf16)


def over_sharers(parts, sharers):
    if sharers == 1:
        return parts
    parts = parts.reshape((H, sharers) + parts.shape[1:]).astype(f32)
    return jnp.sum(parts, axis=1).astype(bf16)


def body(
    inputs,
    cotangent,
    attn_gain,
    ffn_gain,
    query_gain,
    key_gain,
    variate_bias,
    qkv_weight,
    out_weight,
    expand_weight,
    down_weight,
    seq_lengths,
    variate_ids,
    block_order,
):
    depth = lax.axis_size("bz")
    chips = depth * 4
    sharers = chips // H
    core = lax.axis_index("core")
    chip = (lax.axis_index("bz") * 2 + lax.axis_index("by")) * 2 + lax.axis_index("hx")
    head = chip // sharers
    share = chip % sharers
    rows = qkv_weight.shape[0]
    hidden_rows = down_weight.shape[0]
    segments = seq_lengths.shape[0] + 1
    tokens = variate_ids.shape[0]

    by_head = qkv_weight.reshape(rows, 3, H, HD)
    to_heads = jnp.repeat(
        by_head.transpose(2, 0, 1, 3).reshape(H, rows, 3 * HD), 2 * sharers, axis=0
    )
    own_qkv = lax.all_to_all(to_heads, DEVICES, 0, 0, tiled=True)
    own_qkv = jnp.pad(own_qkv.reshape(D, 3 * HD), ((0, 0), (0, HD)))
    to_plane = (
        expand_weight.reshape(rows, 2, depth, 8, hidden_rows)
        .transpose(3, 0, 1, 2, 4)
        .reshape(8, rows, 2 * depth * hidden_rows)
    )
    expand_part = lax.all_to_all(to_plane, PLANE, 0, 0, tiled=True)
    expand_part = expand_part.reshape(8 * rows, -1)

    segment, position, ends = token_meta(seq_lengths, block_order)
    own_segment = own_rows(segment, core)
    own_variate = own_rows(variate_ids, core)
    own_position = own_rows(position, core)
    bias = lax.dynamic_index_in_dim(variate_bias, head, 1, keepdims=False)
    hot = one_hot_rows(own_segment, own_variate)
    freqs = THETA ** (-jnp.arange(HD // 2, dtype=f32) / (HD // 2))
    angles = own_position.astype(f32)[:, None] * freqs[None, :]
    cosine = jnp.tile(jnp.cos(angles), (1, 4))
    sine = jnp.sin(angles)
    sine = jnp.tile(jnp.concatenate([-sine, sine], axis=1), (1, 2))
    pairs = block_order.reshape(chips, 2)
    own_place = lax.dynamic_index_in_dim(pairs, core, 1, keepdims=False)
    other_place = lax.dynamic_index_in_dim(pairs, 1 - core, 1, keepdims=False)
    place = jnp.concatenate([own_place, other_place])
    rank = jnp.sum((own_place[None, :] < own_place[:, None]).astype(jnp.int32), axis=1)
    taken = chips // sharers
    wanted = share * taken + jnp.arange(taken, dtype=jnp.int32)
    chosen = (rank[None, :] == wanted[:, None]).astype(jnp.int32)
    order = jnp.sum(chosen * jnp.arange(chips, dtype=jnp.int32)[None, :], axis=1)
    sorted_place = jnp.sum(chosen * own_place[None, :], axis=1).reshape(-1, QUERY_TILE // BLOCK)
    first_token = sorted_place[:, 0] * BLOCK
    last_token = sorted_place[:, -1] * BLOCK + BLOCK - 1
    begins = jnp.max(jnp.where(ends[None, :] <= first_token[:, None], ends[None, :], 0), axis=1)
    finish = jnp.min(jnp.where(ends[None, :] > last_token[:, None], ends[None, :], tokens), axis=1)
    low = begins // KEY_TILE
    high = (finish + KEY_TILE - 1) // KEY_TILE
    slots = jnp.arange(2 * chips, dtype=jnp.int32)
    source = jnp.sum(
        jnp.where(place[None, :] == slots[:, None], slots[None, :], 0), axis=1, dtype=jnp.int32
    )
    chunks = jnp.arange(tokens // KEY_TILE, dtype=jnp.int32)[:, None]
    low_tile = jnp.sum((high[None, :] <= chunks).astype(jnp.int32), axis=1)
    high_tile = jnp.sum((low[None, :] <= chunks).astype(jnp.int32), axis=1)
    gains = jnp.concatenate([query_gain, key_gain])[None, :]

    late = (hot, cosine, sine, place, order, low, high, source, low_tile, high_tile)
    pieces, where, riders, late = chip_gather(
        jnp.concatenate([inputs, out_weight], axis=0), cotangent, late
    )
    hot, cosine, sine, place, order, low, high, source, low_tile, high_tile = late

    feed_part = jnp.concatenate([expand_part, down_weight], axis=0)
    feed_own = lax.all_gather(feed_part[None], "bz", axis=0, tiled=True)

    normed_low, raw, query, own_kv, out_mine = project(
        where, bias, pieces, attn_gain[None], own_qkv, cosine, sine, gains, hot, segments
    )
    own_kv, riders = lax.optimization_barrier((own_kv, riders))
    other_kv = swap(own_kv, "core")
    rider_corner = swap(riders[0], "by")
    kept, attended = attend(order, place, low, high, query, own_kv, other_kv)
    attended, rider_corner = lax.optimization_barrier((attended, rider_corner))
    cotangent_mine = jnp.concatenate([cotangent, *riders, rider_corner], axis=0)
    cotangent_other = swap(cotangent_mine, "core")
    out_other = swap(out_mine, "core")
    out_full = jnp.stack(
        [jnp.where(core == 0, out_mine, out_other), jnp.where(core == 0, out_other, out_mine)],
        axis=1,
    ).reshape(D, D)
    merged = lax.all_to_all(attended, CHIPS, 0, 0, tiled=True)
    merged, cotangent_other = lax.optimization_barrier((merged, cotangent_other))
    cotangent_plane = (cotangent_mine, cotangent_other)
    merged = over_sharers(merged, sharers).reshape(D, BLOCK)
    middle, second, squares = out_project(merged, inputs, out_full, ffn_gain[None])
    second_plane = plane_gather(second)

    ffn_mine, ffn_other, back_mine, back_other, expand_grad, down_grad = feed(
        second_plane, cotangent_plane, feed_own, hidden_rows
    )
    expand_grad = lax.psum_scatter(expand_grad, "bz", scatter_dimension=0, tiled=True)
    down_grad = lax.psum_scatter(down_grad, "bz", scatter_dimension=0, tiled=True)

    qkv_full = lax.all_gather(
        by_head.transpose(0, 2, 1, 3).reshape(rows, 3 * D), DEVICES, axis=0, tiled=True
    )
    grad_middle, branch_grad, to_chips, grad_ffn = middle_back(
        *plane_scatter(back_mine, back_other), middle, cotangent, ffn_gain[None], out_full
    )
    grad_attended = lax.all_to_all(
        jnp.repeat(to_chips.reshape(H, HD, BLOCK), sharers, axis=0), CHIPS, 0, 0, tiled=True
    )

    joined_mine, joined_other = out_grad(
        jnp.stack(plane_members()), merged, branch_grad, ffn_mine, ffn_other, depth
    )
    joined_other = swap(joined_other, "core")
    joined = (joined_mine.astype(f32) + joined_other.astype(f32)).astype(bf16)
    joined = joined.reshape(4, BLOCK, 2 * D)
    to_x = jnp.concatenate([joined[1], joined[3]], axis=0)
    grad_attended, to_x = lax.optimization_barrier((grad_attended, to_x))
    from_x = swap(to_x, "hx")

    query_grad, own_grad, other_grad, bias_grad = attend_back(
        order, place, source, low_tile, high_tile, query, own_kv, other_kv, kept, grad_attended
    )
    query_grad, from_x = lax.optimization_barrier((query_grad, from_x))
    from_y = swap((joined[2].astype(f32) + from_x[BLOCK:].astype(f32)).astype(bf16), "by")
    expand_grad = lax.all_to_all(
        expand_grad.reshape(8, rows, -1), PLANE, 0, 0, tiled=True
    )
    grad_project, grad_qkv_part, gain_grad, attn_grad = project_back(
        query_grad,
        own_grad,
        swap(other_grad, "core"),
        raw,
        cosine,
        sine,
        gains,
        normed_low,
        own_qkv,
    )
    grad_qkv_part, from_y = lax.optimization_barrier((grad_qkv_part, from_y))
    joined = joined[0].astype(f32) + from_x[:BLOCK].astype(f32) + from_y.astype(f32)
    ffn_branch = joined[:, :D]
    outputs = (middle + ffn_branch).astype(bf16)
    grad_out = sum_along_z(joined[:, D:].reshape(depth, rows, D))
    grad_qkv_part, expand_grad = lax.optimization_barrier((grad_qkv_part, expand_grad))
    grad_qkv_part = grad_qkv_part.reshape(chips, 2, rows, 3 * HD)
    grad_qkv_own = lax.dynamic_index_in_dim(grad_qkv_part, core, 1, keepdims=False)
    grad_qkv_other = lax.dynamic_index_in_dim(grad_qkv_part, 1 - core, 1, keepdims=False)
    grad_qkv_own = grad_qkv_own.astype(f32) + swap(grad_qkv_other, "core").astype(f32)
    values = grad_qkv_own[:, :, 2 * HD :]
    values = jnp.concatenate([values[:, : rows // 2], values[:, rows // 2 :]], axis=2)
    joined = jnp.concatenate(
        [grad_project, grad_qkv_own[:, :, : 2 * HD].astype(bf16), values.astype(bf16)], axis=1
    )
    joined = lax.all_to_all(joined, CHIPS, 0, 0, tiled=True)

    bias_part = jnp.where(
        jnp.arange(H)[None, :] == head, bias_grad[0, :2][:, None], jnp.zeros((2, H), f32)
    )
    packed = jnp.concatenate(
        [
            attn_grad[:, 0] / attn_gain,
            grad_ffn[0],
            gain_grad[0],
            bias_part.reshape(-1),
            squares[:2, 0],
            jnp.sum(ffn_branch * ffn_branch)[None],
            jnp.zeros((93,), f32),
        ]
    )
    summed = sum_everywhere(packed.reshape(-1, 128))
    grad_down = down_grad.astype(f32)
    grad_expand = widen(expand_grad, depth, hidden_rows)
    joined, grad_down, grad_expand = lax.optimization_barrier((joined, grad_down, grad_expand))
    grad_inputs, grad_qkv = input_back(
        over_sharers(joined, sharers), qkv_full, inputs, attn_gain[None], grad_middle
    )
    summed = summed.reshape(-1)
    at = 2 * D + 2 * HD
    root_means = jnp.sqrt(summed[at + 2 * H : at + 2 * H + 3] / (tokens * D))
    return (
        outputs,
        grad_inputs,
        grad_qkv,
        grad_out,
        grad_expand,
        grad_down,
        summed[:D],
        summed[D : 2 * D],
        summed[2 * D : 2 * D + HD],
        summed[2 * D + HD : at],
        summed[at : at + 2 * H].reshape(2, H),
        root_means,
    )


def solution(mesh):
    grid = mesh.devices if mesh.axis_names == ("head", "blk") else mesh.devices.T
    heads, blks = grid.shape
    mesh = Mesh(grid.reshape(heads // 2, 2, blks // 2, 2), ("hx", "core", "bz", "by"))
    split = P(DEVICES, None)

    return jax.shard_map(
        body,
        mesh=mesh,
        in_specs=(split,) * 2 + (P(),) * 5 + (split,) * 4 + (P(),) * 3,
        out_specs=(split,) * 6 + (P(),) * 6,
        check_vma=False,
    )
```

```python
from functools import partial

import jax
import jax.numpy as jnp
from jax import lax
from jax.experimental import pallas as pl
from jax.experimental.pallas import tpu as pltpu
from jax.sharding import Mesh
from jax.sharding import PartitionSpec as P


D = 1024
H = 16
HD = 64
BLOCK = 128
NVAR = 4
EPSILON = 1e-05
THETA = 10000.0

DEVICES = ("bz", "by", "hx", "core")
CHIPS = ("bz", "by", "hx")
PLANE = ("by", "hx", "core")

SEGMENT_LANE = 64
VARIATE_LANE = 76
OWN_VARIATE_LANE = 88
MASK = -512.0
QUERY_TILE = 1024
KEY_TILE = 512
PROJECT_BLOCKS = 4

bf16 = jnp.bfloat16
f32 = jnp.float32


def dot(left, right, dims):
    return lax.dot_general(left, right, (dims, ((), ())), preferred_element_type=f32)


def norm_rows(values, gain):
    factor = lax.rsqrt(jnp.mean(values * values, axis=-1, keepdims=True) + EPSILON)
    return values * factor * gain


def norm_back(values, gain, grad):
    factor = lax.rsqrt(jnp.mean(values * values, axis=-1, keepdims=True) + EPSILON)
    scaled = grad * gain
    inner = jnp.mean(scaled * values, axis=-1, keepdims=True)
    grad_values = factor * (scaled - values * (factor * factor) * inner)
    return grad_values, grad * values * factor


def swap(shard, axis):
    return lax.ppermute(shard, axis, [(0, 1), (1, 0)])


def plane_gather(shard):
    mine = jnp.concatenate(quarters(shard), axis=0)
    return mine, swap(mine, "core")


def chip_gather(shard, rider, late):
    depth = lax.axis_size("bz")
    chips = depth * 4
    z, y, x = lax.axis_index("bz"), lax.axis_index("by"), lax.axis_index("hx")
    at = jnp.arange(chips, dtype=jnp.int32)
    if depth > 4:
        pieces = lax.all_gather(shard, CHIPS, axis=0)
        return list(pieces), at, (swap(rider, "hx"), swap(rider, "by")), late
    column = z_shifts([shard] * (depth - 1))
    across_x, across_y = [swap(shard, "hx")], [swap(shard, "by")]
    across_x += [swap(piece, "hx") for piece in column]
    across_y += [swap(piece, "by") for piece in column]
    across_x, across_y, late = lax.optimization_barrier((across_x, across_y, late))
    corner = [swap(across_x[i], "by") if i > 1 else swap(across_y[i], "hx") for i in range(depth)]
    riders = swap(rider, "hx"), swap(rider, "by")
    pieces = [shard, across_x[0], across_y[0], corner[0]]
    pieces += column + across_x[1:] + across_y[1:] + corner[1:]
    back = (z - at // 4) % depth
    flips = ((at % 2) ^ x) + 2 * (((at // 2) % 2) ^ y)
    where = jnp.where(back == 0, flips, 4 + flips * (depth - 1) + back - 1).astype(jnp.int32)
    return pieces, where, riders, late


def sum_everywhere(values):
    for axis in ("core", "hx", "by"):
        values = values + swap(values, axis)
    depth = lax.axis_size("bz")
    if depth > 4:
        step = 1
        while step < depth:
            values = values + lax.ppermute(values, "bz", [(i, i ^ step) for i in range(depth)])
            step *= 2
        return values
    shifted = z_shifts([values] * (depth - 1))
    shifted = [values] + shifted
    while len(shifted) > 1:
        half = len(shifted) // 2
        shifted = [shifted[i] + shifted[half + i] for i in range(half)]
    return shifted[0]


def z_shifts(values):
    depth = lax.axis_size("bz")
    return [
        lax.ppermute(value, "bz", [(i, (i + by + 1) % depth) for i in range(depth)])
        for by, value in enumerate(values)
    ]


def sum_along_z(parts):
    depth = lax.axis_size("bz")
    if depth > 4:
        parts = parts.reshape(-1, parts.shape[2]).astype(bf16)
        return lax.psum_scatter(parts, "bz", scatter_dimension=0, tiled=True).astype(f32)
    z = lax.axis_index("bz").astype(jnp.uint32)
    parts = [pick(parts, (z + jnp.uint32(by)) & jnp.uint32(depth - 1), 0) for by in range(depth)]
    arrived = z_shifts([part.astype(bf16) for part in parts[1:]])
    return sum([part.astype(f32) for part in arrived], parts[0])


def quarters(shard):
    half = shard.shape[0] // 2
    across_x = swap(shard, "hx")
    across_y = swap(shard, "by")
    return [shard, across_x, across_y, swap(across_y[:half], "hx"), swap(across_x[half:], "by")]


def plane_scatter(mine, other):
    rows = mine.shape[0] // 4
    half = rows // 2
    mine = mine.astype(f32) + swap(other, "core").astype(f32)
    corner = mine[3 * rows :].astype(bf16)
    for_y = swap(corner[:half], "hx").astype(f32)
    for_x = swap(corner[half:], "by").astype(f32)
    to_x = mine[rows : 2 * rows]
    to_y = mine[2 * rows : 3 * rows]
    to_x = jnp.concatenate([to_x[:half], to_x[half:] + for_x], axis=0).astype(bf16)
    to_y = jnp.concatenate([to_y[:half] + for_y, to_y[half:]], axis=0).astype(bf16)
    from_x = swap(to_x, "hx")
    from_y = swap(to_y, "by")
    return mine[:rows], from_x, from_y


def plane_members():
    here = (lax.axis_index("by") * 2 + lax.axis_index("hx")) * 2 + lax.axis_index("core")
    return here ^ jnp.array([0, 2, 4, 6, 1, 3, 5, 7], jnp.int32)


def pick(array, index, axis):
    return lax.dynamic_index_in_dim(array, index.astype(jnp.uint32), axis, keepdims=False)


def lanes(shape):
    return lax.broadcasted_iota(jnp.int32, shape, len(shape) - 1)


def half_mean(values, lane):
    low = jnp.sum(jnp.where(lane < HD, values, 0.0), axis=-1, keepdims=True)
    high = jnp.sum(jnp.where(lane < HD, 0.0, values), axis=-1, keepdims=True)
    return jnp.where(lane < HD, low, high) * (1.0 / HD)


def swap_halves(values, lane):
    return jnp.where(
        (lane & (HD - 1)) < HD // 2, pltpu.roll(values, 96, 1), pltpu.roll(values, 32, 1)
    )


def mask_matrix(segments, bias_ref):
    shape = (128, 128)
    row = lax.broadcasted_iota(jnp.int32, shape, 0)
    lane = lax.broadcasted_iota(jnp.int32, shape, 1)
    segment = row - SEGMENT_LANE
    here = lane - SEGMENT_LANE
    apart = (segment >= 0) & (segment < segments) & (here >= 0) & (here < segments)
    matrix = jnp.where(apart & (here != segment), MASK, 0.0)
    variate = row - VARIATE_LANE
    known = (variate >= 0) & (variate < NVAR)
    copy = (lane - VARIATE_LANE) // NVAR
    same = (lane - VARIATE_LANE) % NVAR == variate
    bias = jnp.where(same, bias_ref[1], bias_ref[0])
    high = bias.astype(bf16).astype(f32)
    mid = (bias - high).astype(bf16).astype(f32)
    value = jnp.where(copy == 0, high, jnp.where(copy == 1, mid, bias - high - mid))
    biased = known & (lane >= VARIATE_LANE) & (lane < VARIATE_LANE + 3 * NVAR)
    matrix = jnp.where(biased, value, matrix)
    return jnp.where(known & (lane == OWN_VARIATE_LANE + variate), 1.0, matrix).astype(bf16)


def project_kernel(where_ref, bias_ref, *refs, chips, segments):
    piece_refs, refs = refs[:chips], refs[chips:]
    gain_ref, weight_ref, cosine_ref, sine_ref, gains_ref, hot_ref = refs[:6]
    normed_ref, raw_ref, query_ref, kv_ref, out_ref, x_ref, mask_ref, arrived = refs[6:]
    step = pl.program_id(0)

    @pl.when(step == 0)
    def _():
        copies = [
            pltpu.make_async_copy(piece_refs[i], x_ref.at[i], arrived.at[i]) for i in range(chips)
        ]
        for copy in copies:
            copy.start()
        mask_ref[...] = mask_matrix(segments, bias_ref)
        for copy in copies:
            copy.wait()

    places = [where_ref[step * PROJECT_BLOCKS + i] for i in range(PROJECT_BLOCKS)]
    for i, place in enumerate(places):
        out_ref[i] = x_ref[place, BLOCK:]
    x = jnp.concatenate([x_ref[place, :BLOCK] for place in places], axis=0).astype(f32)
    normed = norm_rows(x, gain_ref[...]).astype(bf16)
    normed_ref[...] = normed
    project = dot(normed, weight_ref[...], ((1,), (0,)))
    both = project[:, : 2 * HD]
    value = project[:, 2 * HD :]
    raw_ref[...] = both
    lane = lanes(both.shape)
    scaled = both * lax.rsqrt(half_mean(both * both, lane) + EPSILON) * gains_ref[...]
    turned = scaled * cosine_ref[...] + swap_halves(scaled, lane) * sine_ref[...]
    turned = turned.astype(bf16).astype(f32)
    hot = hot_ref[...]
    query_ref[...] = jnp.where(lane < HD, turned, hot.astype(f32)).astype(bf16)
    key = pltpu.roll(turned * HD ** (-0.5), HD, 1)
    ones = jnp.where((lane >= HD) & (lane < HD + 3), 1.0, 0.0)
    kv_ref[:, :128] = jnp.where(lane < HD, key, dot(hot, mask_ref[...], ((1,), (0,)))).astype(bf16)
    kv_ref[:, 128:] = jnp.where(lane < HD, value, ones).astype(bf16)


def project(where, bias, pieces, gain, weight, cosine, sine, gains, hot, segments):
    blocks = len(pieces)
    rows = blocks * BLOCK
    step_rows = PROJECT_BLOCKS * BLOCK
    out_rows = pieces[0].shape[0] - BLOCK
    row_spec = lambda width: pl.BlockSpec((step_rows, width), lambda j, *unused: (j, 0))
    whole = lambda array: pl.BlockSpec(array.shape, lambda j, *unused: (0, 0))
    anywhere = pl.BlockSpec(memory_space=pl.ANY)
    tables = [whole(gain), whole(weight), row_spec(128), row_spec(128), whole(gains)]
    return pl.pallas_call(
        partial(project_kernel, chips=blocks, segments=segments),
        grid_spec=pltpu.PrefetchScalarGridSpec(
            num_scalar_prefetch=2,
            grid=(blocks // PROJECT_BLOCKS,),
            in_specs=[anywhere] * blocks + tables + [row_spec(128)],
            out_specs=[
                row_spec(D),
                row_spec(128),
                row_spec(128),
                row_spec(256),
                pl.BlockSpec((PROJECT_BLOCKS, out_rows, D), lambda j, *unused: (j, 0, 0)),
            ],
            scratch_shapes=[
                pltpu.VMEM((blocks, BLOCK + out_rows, D), bf16),
                pltpu.VMEM((128, 128), bf16),
                pltpu.SemaphoreType.DMA((blocks,)),
            ],
        ),
        out_shape=[
            jax.ShapeDtypeStruct((rows, D), bf16),
            jax.ShapeDtypeStruct((rows, 128), f32),
            jax.ShapeDtypeStruct((rows, 128), bf16),
            jax.ShapeDtypeStruct((rows, 256), bf16),
            jax.ShapeDtypeStruct((blocks, out_rows, D), bf16),
        ],
        name="project",
    )(where, bias, *pieces, gain, weight, cosine, sine, gains, hot)


def sort_keys(place_ref, own_ref, other_ref, keys_ref):
    blocks = own_ref.shape[0] // BLOCK
    for half, source_ref in ((0, own_ref), (1, other_ref)):

        def put(j, unused, half=half, source_ref=source_ref):
            source = pl.multiple_of(j * BLOCK, BLOCK)
            target = pl.multiple_of(place_ref[half * blocks + j] * BLOCK, BLOCK)
            keys_ref[pl.ds(target, BLOCK), :] = source_ref[pl.ds(source, BLOCK), :]
            return unused

        lax.fori_loop(0, blocks, put, 0, unroll=4)


def block_start(order_ref, index):
    return pl.multiple_of(order_ref[index] * BLOCK, BLOCK)


def attend_kernel(
    order_ref,
    place_ref,
    low_ref,
    high_ref,
    query_ref,
    own_ref,
    other_ref,
    kept_ref,
    attended_ref,
    keys_ref,
):
    tile = pl.program_id(0)
    count = QUERY_TILE // BLOCK

    @pl.when(tile == 0)
    def _():
        sort_keys(place_ref, own_ref, other_ref, keys_ref)
        if order_ref.shape[0] * BLOCK != query_ref.shape[0]:
            kept_ref[...] = jnp.zeros_like(kept_ref)
            attended_ref[...] = jnp.zeros_like(attended_ref)

    starts = [block_start(order_ref, tile * count + i) for i in range(count)]
    query = jnp.concatenate([query_ref[pl.ds(start, BLOCK), :] for start in starts], axis=0)

    def chunk(index, accumulated):
        window = pl.ds(pl.multiple_of(index * KEY_TILE, KEY_TILE), KEY_TILE)
        expo = jnp.exp(dot(query, keys_ref[window, :128], ((1,), (1,))))
        return accumulated + dot(expo.astype(bf16), keys_ref[window, 128:], ((1,), (0,)))

    accumulated = lax.fori_loop(
        low_ref[tile], high_ref[tile], chunk, jnp.zeros((QUERY_TILE, 128), f32)
    )
    totals = accumulated[:, HD : HD + 1]
    lane = lanes(accumulated.shape)
    kept = jnp.where(lane < HD, accumulated / totals, totals)
    for i, start in enumerate(starts):
        piece = kept[i * BLOCK : (i + 1) * BLOCK]
        kept_ref[pl.ds(start, BLOCK), :] = piece
        attended_ref[order_ref[tile * count + i]] = piece.T[:HD].astype(bf16)


def fixed(array):
    return pl.BlockSpec(
        array.shape, lambda *unused: (0,) * len(array.shape), pipeline_mode=pl.Buffered(1)
    )


def attend(order, place, low, high, query, own, other):
    rows = query.shape[0]
    operands = (query, own, other)
    outs = (
        jax.ShapeDtypeStruct((rows, 128), f32),
        jax.ShapeDtypeStruct((rows // BLOCK, HD, BLOCK), bf16),
    )
    return pl.pallas_call(
        attend_kernel,
        grid_spec=pltpu.PrefetchScalarGridSpec(
            num_scalar_prefetch=4,
            grid=(low.shape[0],),
            in_specs=[fixed(array) for array in operands],
            out_specs=[fixed(array) for array in outs],
            scratch_shapes=[pltpu.VMEM((2 * rows, 256), bf16)],
        ),
        out_shape=list(outs),
        name="attend",
    )(order, place, low, high, *operands)


def attend_back_kernel(
    order_ref,
    place_ref,
    source_ref,
    low_ref,
    high_ref,
    query_ref,
    own_ref,
    other_ref,
    kept_ref,
    grad_ref,
    query_grad_ref,
    own_grad_ref,
    other_grad_ref,
    bias_ref,
    keys_ref,
    sorted_ref,
    wide_ref,
    sums_ref,
    every_ref,
    same_ref,
):
    step = pl.program_id(0)
    own_rows = own_ref.shape[0]
    taken = order_ref.shape[0]

    @pl.when(step == 0)
    def _():
        sort_keys(place_ref, own_ref, other_ref, keys_ref)
        every_ref[...] = jnp.zeros_like(every_ref)
        same_ref[...] = jnp.zeros_like(same_ref)
        sums_ref[...] = jnp.zeros_like(sums_ref)
        if taken * BLOCK != own_rows:
            query_grad_ref[...] = jnp.zeros_like(query_grad_ref)
        lane = lanes((BLOCK, 128))

        def put(i, unused):
            source = pl.ds(block_start(order_ref, i), BLOCK)
            target = pl.ds(pl.multiple_of(i * BLOCK, BLOCK), BLOCK)
            sorted_ref[target, :] = query_ref[source, :]
            kept = kept_ref[source, :]
            grad = grad_ref[order_ref[i]].astype(f32)
            grad = jnp.concatenate([grad, jnp.zeros_like(grad)], axis=0).T
            inverse = 1.0 / kept[:, HD : HD + 1]
            center = jnp.sum(grad * kept, axis=1, keepdims=True) * inverse
            center_high = center.astype(bf16).astype(f32)
            center_rest = center - center_high
            center_mid = center_rest.astype(bf16).astype(f32)
            center_low = center_rest - center_mid
            wide = jnp.where(lane == HD, -center_high, 0.0)
            wide = jnp.where(lane == HD + 1, -center_mid, wide)
            wide = jnp.where(lane == HD + 2, -center_low, wide)
            wide_ref[target, :] = jnp.where(lane < HD, grad * inverse, wide).astype(bf16)
            return unused

        lax.fori_loop(0, taken, put, 0, unroll=4)

    window = pl.ds(pl.multiple_of(step * KEY_TILE, KEY_TILE), KEY_TILE)
    key = keys_ref[window, :128]
    value = keys_ref[window, 128:]

    def tile(index, grads):
        rows = pl.ds(pl.multiple_of(index * QUERY_TILE, QUERY_TILE), QUERY_TILE)
        query = sorted_ref[rows, :]
        wide = wide_ref[rows, :]
        expo = jnp.exp(dot(key, query, ((1,), (1,))))
        score_low = (expo * dot(value, wide, ((1,), (1,)))).astype(bf16)
        sums_ref[rows, :] += dot(score_low, key, ((0,), (0,)))
        return (
            grads[0] + dot(score_low, query, ((1,), (0,))),
            grads[1] + dot(expo.astype(bf16), wide, ((1,), (0,))),
        )

    empty = jnp.zeros((KEY_TILE, 128), f32)
    key_grad, value_grad = lax.fori_loop(low_ref[step], high_ref[step], tile, (empty, empty))
    lane = lanes(key_grad.shape)
    joined = jnp.where(lane < HD, value_grad, pltpu.roll(key_grad, HD, 1) * HD ** (-0.5))
    joined = joined.astype(bf16)
    for i in range(KEY_TILE // BLOCK):
        source = source_ref[step * (KEY_TILE // BLOCK) + i] * BLOCK
        piece = joined[i * BLOCK : (i + 1) * BLOCK]

        @pl.when(source < own_rows)
        def _(source=source, piece=piece):
            own_grad_ref[pl.ds(pl.multiple_of(source, BLOCK), BLOCK), :] = piece

        @pl.when(source >= own_rows)
        def _(source=source, piece=piece):
            other_grad_ref[pl.ds(pl.multiple_of(source - own_rows, BLOCK), BLOCK), :] = piece

    every = jnp.where((lane >= VARIATE_LANE) & (lane < VARIATE_LANE + NVAR), key_grad, 0.0)
    shift = 128 + VARIATE_LANE - OWN_VARIATE_LANE
    same = every * pltpu.roll(key.astype(f32), shift, 1)
    every_ref[...] += jnp.sum(every.reshape(-1, 8, 128), axis=0)
    same_ref[...] += jnp.sum(same.reshape(-1, 8, 128), axis=0)

    @pl.when(step == pl.num_programs(0) - 1)
    def _():
        def put(i, unused):
            target = pl.ds(block_start(order_ref, i), BLOCK)
            rows = pl.ds(pl.multiple_of(i * BLOCK, BLOCK), BLOCK)
            query_grad_ref[target, :] = sums_ref[rows, :].astype(bf16)
            return unused

        lax.fori_loop(0, taken, put, 0, unroll=4)
        every = jnp.sum(every_ref[...], keepdims=True)
        same = jnp.sum(same_ref[...], keepdims=True)
        bias_lane = lanes((8, 128))
        bias_ref[...] = jnp.where(
            bias_lane == 0, every - same, jnp.where(bias_lane == 1, same, 0.0)
        )


def attend_back(order, place, source, low, high, query, own, other, kept, grad):
    rows = query.shape[0]
    taken = order.shape[0] * BLOCK
    operands = (query, own, other, kept, grad)
    outs = tuple(jax.ShapeDtypeStruct((rows, 128), bf16) for _ in range(3)) + (
        jax.ShapeDtypeStruct((8, 128), f32),
    )
    return pl.pallas_call(
        attend_back_kernel,
        grid_spec=pltpu.PrefetchScalarGridSpec(
            num_scalar_prefetch=5,
            grid=(low.shape[0],),
            in_specs=[fixed(array) for array in operands],
            out_specs=[fixed(array) for array in outs],
            scratch_shapes=[
                pltpu.VMEM((2 * rows, 256), bf16),
                pltpu.VMEM((taken, 128), bf16),
                pltpu.VMEM((taken, 128), bf16),
                pltpu.VMEM((taken, 128), f32),
                pltpu.VMEM((8, 128), f32),
                pltpu.VMEM((8, 128), f32),
            ],
        ),
        out_shape=list(outs),
        name="attend_back",
    )(order, place, source, low, high, *operands)


def project_back_kernel(
    query_grad_ref,
    own_ref,
    other_ref,
    raw_ref,
    cosine_ref,
    sine_ref,
    gains_ref,
    normed_ref,
    forward_ref,
    grad_ref,
    weight_grad_ref,
    gain_grad_ref,
    attn_grad_ref,
    weight_ref,
    gain_ref,
):
    step = pl.program_id(0)

    @pl.when(step == 0)
    def _():
        weight_ref[...] = jnp.zeros_like(weight_ref)
        gain_ref[...] = jnp.zeros_like(gain_ref)

    kv_grad = own_ref[...].astype(f32) + other_ref[...].astype(f32)
    kv_grad = kv_grad.astype(bf16).astype(f32)
    lane = lanes(kv_grad.shape)
    turned = jnp.where(lane < HD, query_grad_ref[...].astype(f32), kv_grad)
    grad = turned * cosine_ref[...] - swap_halves(turned, lane) * sine_ref[...]
    raw = raw_ref[...]
    factor = lax.rsqrt(half_mean(raw * raw, lane) + EPSILON)
    scaled = grad * gains_ref[...]
    inner = half_mean(scaled * raw, lane)
    both = factor * (scaled - raw * (factor * factor) * inner)
    gain_ref[...] += jnp.sum(grad * raw * factor, axis=0, keepdims=True)
    full = jnp.concatenate([both, jnp.where(lane < HD, kv_grad, 0.0)], axis=1)
    for i in range(grad_ref.shape[0]):
        grad_ref[i] = full[i * BLOCK : (i + 1) * BLOCK].T[: 3 * HD].astype(bf16)
    weight_ref[...] += dot(normed_ref[...], full.astype(bf16), ((0,), (0,)))

    @pl.when(step == pl.num_programs(0) - 1)
    def _():
        weight_grad_ref[...] = weight_ref[:, : 3 * HD].astype(bf16)
        gain_grad_ref[...] = jnp.broadcast_to(gain_ref[...], gain_grad_ref.shape)
        forward = forward_ref[...].astype(f32)
        attn = jnp.sum(weight_ref[...] * forward, axis=1, keepdims=True)
        attn_grad_ref[...] = jnp.broadcast_to(attn, attn_grad_ref.shape)


def project_back(query_grad, own, other, raw, cosine, sine, gains, normed, forward):
    rows = query_grad.shape[0]
    step_rows = 4 * BLOCK
    row_spec = lambda width: pl.BlockSpec((step_rows, width), lambda j: (j, 0))
    whole = lambda shape: pl.BlockSpec(shape, lambda j: (0, 0))
    return pl.pallas_call(
        project_back_kernel,
        grid=(rows // step_rows,),
        in_specs=[row_spec(128)] * 6 + [whole(gains.shape), row_spec(D), whole(forward.shape)],
        out_specs=[
            pl.BlockSpec((step_rows // BLOCK, 3 * HD, BLOCK), lambda j: (j, 0, 0)),
            whole((D, 3 * HD)),
            whole((8, 128)),
            whole((D, 128)),
        ],
        out_shape=[
            jax.ShapeDtypeStruct((rows // BLOCK, 3 * HD, BLOCK), bf16),
            jax.ShapeDtypeStruct((D, 3 * HD), bf16),
            jax.ShapeDtypeStruct((8, 128), f32),
            jax.ShapeDtypeStruct((D, 128), f32),
        ],
        scratch_shapes=[pltpu.VMEM((D, 4 * HD), f32), pltpu.VMEM((1, 128), f32)],
        name="project_back",
    )(query_grad, own, other, raw, cosine, sine, gains, normed, forward)


def feed_kernel(
    second_mine_ref,
    second_other_ref,
    grad_mine_ref,
    grad_other_ref,
    weight_ref,
    ffn_mine_ref,
    ffn_other_ref,
    back_mine_ref,
    back_other_ref,
    expand_out_ref,
    down_out_ref,
    expand_ref,
    down_ref,
    expand_grad_ref,
    down_grad_ref,
):
    step = pl.program_id(0)
    half = pl.num_programs(0) // 2
    depth, both_rows, width = weight_ref.shape
    down_rows = down_ref.shape[0] // depth
    expand_rows = both_rows - down_rows

    @pl.when(step == 0)
    def _():
        for z in range(depth):
            expand_ref[z * expand_rows : (z + 1) * expand_rows] = weight_ref[z, :expand_rows]
            down_ref[z * down_rows : (z + 1) * down_rows] = weight_ref[z, expand_rows:]
        expand_grad_ref[...] = jnp.zeros_like(expand_grad_ref)
        down_grad_ref[...] = jnp.zeros_like(down_grad_ref)

    second = jnp.where(step < half, second_mine_ref[...], second_other_ref[...])
    grad = jnp.where(step < half, grad_mine_ref[...], grad_other_ref[...])
    expand = dot(second, expand_ref[...], ((1,), (0,)))
    gate = expand[:, : width // 2]
    up = expand[:, width // 2 :]
    sigmoid = 1.0 / (1.0 + jnp.exp(-gate))
    silu = gate * sigmoid
    hidden = (silu * up).astype(bf16)
    grad_hidden = dot(grad, down_ref[...], ((1,), (1,)))
    grad_gate = grad_hidden * up * (sigmoid * (1.0 + gate * (1.0 - sigmoid)))
    rows = jnp.concatenate([grad_gate, grad_hidden * silu], axis=1).astype(bf16)
    ffn = dot(hidden, down_ref[...], ((1,), (0,))).astype(bf16)
    back = dot(rows, expand_ref[...], ((1,), (1,))).astype(bf16)
    expand_grad_ref[...] += dot(second, rows, ((0,), (0,)))
    down_grad_ref[...] += dot(hidden, grad, ((0,), (0,)))

    @pl.when(step < half)
    def _():
        ffn_mine_ref[...] = ffn
        back_mine_ref[...] = back

    @pl.when(step >= half)
    def _():
        ffn_other_ref[...] = ffn
        back_other_ref[...] = back

    @pl.when(step == pl.num_programs(0) - 1)
    def _():
        expand_out_ref[...] = expand_grad_ref[...].astype(bf16)
        down_out_ref[...] = down_grad_ref[...].astype(bf16)


def feed(second, grad, weight, down_rows):
    rows = second[0].shape[0]
    tile = 256
    steps = rows // tile
    depth, both_rows, width = weight.shape
    mine = pl.BlockSpec((tile, D), lambda i: (jnp.minimum(i, steps - 1), 0))
    other = pl.BlockSpec((tile, D), lambda i: (jnp.maximum(i - steps, 0), 0))
    whole = pl.BlockSpec(weight.shape, lambda i: (0, 0, 0), pipeline_mode=pl.Buffered(1))
    token_rows = jax.ShapeDtypeStruct((rows, D), bf16)
    expand_out = jax.ShapeDtypeStruct((depth * (both_rows - down_rows), width), bf16)
    down_out = jax.ShapeDtypeStruct((depth * down_rows, D), bf16)
    return pl.pallas_call(
        feed_kernel,
        grid=(2 * steps,),
        in_specs=[mine, other, mine, other, whole],
        out_specs=[mine, other, mine, other, fixed(expand_out), fixed(down_out)],
        out_shape=[token_rows] * 4 + [expand_out, down_out],
        scratch_shapes=[
            pltpu.VMEM((depth * (both_rows - down_rows), width), bf16),
            pltpu.VMEM((depth * down_rows, D), bf16),
            pltpu.VMEM((depth * (both_rows - down_rows), width), f32),
            pltpu.VMEM((depth * down_rows, D), f32),
        ],
        name="feed",
    )(*second, *grad, weight)


def out_kernel(parts_ref, x_ref, weight_ref, gain_ref, middle_ref, second_ref, squares_ref):
    branch = dot(parts_ref[...], weight_ref[...], ((0,), (0,)))
    x = x_ref[...].astype(f32)
    middle = x + branch
    middle_ref[...] = middle
    second_ref[...] = norm_rows(middle, gain_ref[...]).astype(bf16)
    row = lax.broadcasted_iota(jnp.int32, squares_ref.shape, 0)
    x_sum = jnp.sum(x * x, keepdims=True)
    branch_sum = jnp.sum(branch * branch, keepdims=True)
    squares_ref[...] = jnp.where(row == 0, x_sum, branch_sum)


def out_project(parts, x, weight, gain):
    rows = x.shape[0]
    return pl.pallas_call(
        out_kernel,
        out_shape=[
            jax.ShapeDtypeStruct((rows, D), f32),
            jax.ShapeDtypeStruct((rows, D), bf16),
            jax.ShapeDtypeStruct((8, 128), f32),
        ],
        name="out_project",
    )(parts, x, weight, gain)


def middle_back_kernel(
    own_ref,
    from_x_ref,
    from_y_ref,
    middle_ref,
    cotangent_ref,
    gain_ref,
    weight_ref,
    grad_middle_ref,
    branch_ref,
    parts_ref,
    gain_grad_ref,
):
    grad_second = own_ref[...] + from_x_ref[...].astype(f32) + from_y_ref[...].astype(f32)
    grad_middle, gain_rows = norm_back(middle_ref[...], gain_ref[...], grad_second)
    grad_middle = cotangent_ref[...].astype(f32) + grad_middle
    grad_middle_ref[...] = grad_middle
    branch = grad_middle.astype(bf16)
    branch_ref[...] = branch
    parts_ref[...] = dot(weight_ref[...], branch, ((1,), (1,))).astype(bf16)
    gain_grad_ref[...] = jnp.broadcast_to(
        jnp.sum(gain_rows, axis=0, keepdims=True), gain_grad_ref.shape
    )


def middle_back(own, from_x, from_y, middle, cotangent, gain, weight):
    rows = middle.shape[0]
    return pl.pallas_call(
        middle_back_kernel,
        out_shape=[
            jax.ShapeDtypeStruct((rows, D), f32),
            jax.ShapeDtypeStruct((rows, D), bf16),
            jax.ShapeDtypeStruct((D, rows), bf16),
            jax.ShapeDtypeStruct((8, D), f32),
        ],
        name="middle_back",
    )(own, from_x, from_y, middle, cotangent, gain, weight)


def out_grad_kernel(
    members_ref,
    merged_ref,
    branch_ref,
    ffn_mine_ref,
    ffn_other_ref,
    mine_ref,
    other_ref,
    grad_ref,
    depth,
):
    shard = mine_ref.shape[0] // 4
    rows = shard // depth
    grad_ref[...] = dot(merged_ref[...], branch_ref[...], ((1,), (0,)))
    mine_ref[:, :D] = ffn_mine_ref[...]
    other_ref[:, :D] = ffn_other_ref[...]
    for place in range(8):
        target_ref = mine_ref if place < 4 else other_ref
        for z in range(depth):
            source = pl.multiple_of((z * 8 + members_ref[place]) * rows, rows)
            target = (place % 4) * shard + z * rows
            target_ref[target : target + rows, D:] = grad_ref[pl.ds(source, rows), :].astype(bf16)


def out_grad(members, merged, branch, ffn_mine, ffn_other, depth):
    joined = jax.ShapeDtypeStruct((ffn_mine.shape[0], 2 * D), bf16)
    operands = (merged, branch, ffn_mine, ffn_other)
    return pl.pallas_call(
        partial(out_grad_kernel, depth=depth),
        grid_spec=pltpu.PrefetchScalarGridSpec(
            num_scalar_prefetch=1,
            grid=(1,),
            in_specs=[fixed(array) for array in operands],
            out_specs=[fixed(joined), fixed(joined)],
            scratch_shapes=[pltpu.VMEM((D, D), f32)],
        ),
        out_shape=[joined, joined],
        name="out_grad",
    )(members, *operands)


def input_back_kernel(
    joined_ref, weight_ref, x_ref, gain_ref, middle_ref, grad_ref, qkv_ref, wide_ref
):
    heads = joined_ref.shape[0]
    rows = qkv_ref.shape[0]
    for head in range(heads):
        wide_ref[head * 3 * HD : (head + 1) * 3 * HD] = joined_ref[head, : 3 * HD]
    for pair in range(heads // 2):
        left = joined_ref[2 * pair, 3 * HD :].astype(f32)
        right = joined_ref[2 * pair + 1, 3 * HD :].astype(f32)
        at = pair * 2 * HD
        low = jnp.concatenate([left[:, :HD], right[:, :HD]], axis=1)
        high = jnp.concatenate([left[:, HD:], right[:, HD:]], axis=1)
        qkv_ref[:, at : at + 2 * HD] = low[:rows]
        qkv_ref[:, D + at : D + at + 2 * HD] = high[:rows]
        qkv_ref[: rows // 2, 2 * D + at : 2 * D + at + 2 * HD] = low[rows:]
        qkv_ref[rows // 2 :, 2 * D + at : 2 * D + at + 2 * HD] = high[rows:]
    grad_normed = dot(wide_ref[...], weight_ref[...], ((0,), (1,)))
    grad, _ = norm_back(x_ref[...].astype(f32), gain_ref[...], grad_normed)
    grad_ref[...] = middle_ref[...] + grad


def input_back(joined, weight, x, gain, middle):
    rows = x.shape[0]
    return pl.pallas_call(
        input_back_kernel,
        out_shape=[
            jax.ShapeDtypeStruct((rows, D), f32),
            jax.ShapeDtypeStruct(((joined.shape[1] - 3 * HD) * 2 // 3, 3 * D), f32),
        ],
        scratch_shapes=[pltpu.VMEM((3 * D, rows), bf16)],
        name="input_back",
    )(joined, weight, x, gain, middle)


def widen_kernel(parts_ref, grad_ref):
    sources, _, width = parts_ref.shape
    for source in range(sources):
        for at in range(width // 128):
            to = (at * sources + source) * 128
            grad_ref[:, to : to + 128] = parts_ref[source, :, at * 128 : (at + 1) * 128].astype(f32)


def widen(parts, depth, hidden_rows):
    sources, rows, width = parts.shape
    if hidden_rows != 128:
        parts = parts.reshape(sources, rows, 2, depth, hidden_rows)
        return parts.transpose(1, 2, 3, 0, 4).reshape(rows, -1).astype(f32)
    return pl.pallas_call(
        widen_kernel, out_shape=jax.ShapeDtypeStruct((rows, sources * width), f32), name="widen"
    )(parts)


def token_meta(seq_lengths, block_order):
    blocks = block_order.shape[0]
    packed_at = jnp.repeat(block_order, BLOCK) * BLOCK + jnp.tile(
        jnp.arange(BLOCK, dtype=jnp.int32), blocks
    )
    ends = jnp.cumsum(seq_lengths)
    after = packed_at[:, None] >= ends[None, :]
    segment = jnp.sum(after.astype(jnp.int32), axis=1)
    begin = jnp.max(jnp.where(after, ends[None, :], jnp.zeros_like(ends)[None, :]), axis=1)
    return (segment, packed_at - begin, ends)


def own_rows(array, core):
    pairs = array.reshape(-1, 2, BLOCK)
    return pick(pairs, core, 1).reshape(-1)


def one_hot_rows(segment, variate):
    lane = jnp.arange(128, dtype=jnp.int32)[None, :]
    hot = lane == SEGMENT_LANE + segment[:, None]
    for copy in range(3):
        hot = hot | (lane == VARIATE_LANE + copy * NVAR + variate[:, None])
    return hot.astype(bf16)


def over_sharers(parts, sharers):
    if sharers == 1:
        return parts
    parts = parts.reshape((H, sharers) + parts.shape[1:]).astype(f32)
    return jnp.sum(parts, axis=1).astype(bf16)


def body(
    inputs,
    cotangent,
    attn_gain,
    ffn_gain,
    query_gain,
    key_gain,
    variate_bias,
    qkv_weight,
    out_weight,
    expand_weight,
    down_weight,
    seq_lengths,
    variate_ids,
    block_order,
):
    depth = lax.axis_size("bz")
    chips = depth * 4
    sharers = chips // H
    core = lax.axis_index("core")
    chip = (lax.axis_index("bz") * 2 + lax.axis_index("by")) * 2 + lax.axis_index("hx")
    head = chip // sharers
    share = chip % sharers
    rows = qkv_weight.shape[0]
    hidden_rows = down_weight.shape[0]
    segments = seq_lengths.shape[0] + 1
    tokens = variate_ids.shape[0]

    by_head = qkv_weight.reshape(rows, 3, H, HD)
    to_heads = jnp.repeat(
        by_head.transpose(2, 0, 1, 3).reshape(H, rows, 3 * HD), 2 * sharers, axis=0
    )
    own_qkv = lax.all_to_all(to_heads, DEVICES, 0, 0, tiled=True)
    own_qkv = jnp.pad(own_qkv.reshape(D, 3 * HD), ((0, 0), (0, HD)))
    to_plane = (
        expand_weight.reshape(rows, 2, depth, 8, hidden_rows)
        .transpose(3, 0, 1, 2, 4)
        .reshape(8, rows, 2 * depth * hidden_rows)
    )
    expand_part = lax.all_to_all(to_plane, PLANE, 0, 0, tiled=True)
    expand_part = expand_part.reshape(8 * rows, -1)

    segment, position, ends = token_meta(seq_lengths, block_order)
    own_segment = own_rows(segment, core)
    own_variate = own_rows(variate_ids, core)
    own_position = own_rows(position, core)
    bias = pick(variate_bias, head, 1)
    hot = one_hot_rows(own_segment, own_variate)
    freqs = THETA ** (-jnp.arange(HD // 2, dtype=f32) / (HD // 2))
    angles = own_position.astype(f32)[:, None] * freqs[None, :]
    cosine = jnp.tile(jnp.cos(angles), (1, 4))
    sine = jnp.sin(angles)
    sine = jnp.tile(jnp.concatenate([-sine, sine], axis=1), (1, 2))
    pairs = block_order.reshape(chips, 2)
    own_place = pick(pairs, core, 1)
    other_place = pick(pairs, 1 - core, 1)
    place = jnp.concatenate([own_place, other_place])
    rank = jnp.sum((own_place[None, :] < own_place[:, None]).astype(jnp.int32), axis=1)
    taken = chips // sharers
    wanted = share * taken + jnp.arange(taken, dtype=jnp.int32)
    chosen = (rank[None, :] == wanted[:, None]).astype(jnp.int32)
    order = jnp.sum(chosen * jnp.arange(chips, dtype=jnp.int32)[None, :], axis=1)
    sorted_place = jnp.sum(chosen * own_place[None, :], axis=1).reshape(-1, QUERY_TILE // BLOCK)
    first_token = sorted_place[:, 0] * BLOCK
    last_token = sorted_place[:, -1] * BLOCK + BLOCK - 1
    begins = jnp.max(jnp.where(ends[None, :] <= first_token[:, None], ends[None, :], 0), axis=1)
    finish = jnp.min(jnp.where(ends[None, :] > last_token[:, None], ends[None, :], tokens), axis=1)
    low = begins // KEY_TILE
    high = (finish + KEY_TILE - 1) // KEY_TILE
    slots = jnp.arange(2 * chips, dtype=jnp.int32)
    source = jnp.sum(
        jnp.where(place[None, :] == slots[:, None], slots[None, :], 0), axis=1, dtype=jnp.int32
    )
    chunks = jnp.arange(tokens // KEY_TILE, dtype=jnp.int32)[:, None]
    low_tile = jnp.sum((high[None, :] <= chunks).astype(jnp.int32), axis=1)
    high_tile = jnp.sum((low[None, :] <= chunks).astype(jnp.int32), axis=1)
    gains = jnp.concatenate([query_gain, key_gain])[None, :]

    late = (hot, cosine, sine, place, order, low, high, source, low_tile, high_tile)
    pieces, where, riders, late = chip_gather(
        jnp.concatenate([inputs, out_weight], axis=0), cotangent, late
    )
    hot, cosine, sine, place, order, low, high, source, low_tile, high_tile = late

    feed_part = jnp.concatenate([expand_part, down_weight], axis=0)
    feed_own = lax.all_gather(feed_part[None], "bz", axis=0, tiled=True)

    normed_low, raw, query, own_kv, out_mine = project(
        where, bias, pieces, attn_gain[None], own_qkv, cosine, sine, gains, hot, segments
    )
    own_kv, riders = lax.optimization_barrier((own_kv, riders))
    other_kv = swap(own_kv, "core")
    rider_corner = swap(riders[0], "by")
    kept, attended = attend(order, place, low, high, query, own_kv, other_kv)
    attended, rider_corner = lax.optimization_barrier((attended, rider_corner))
    cotangent_mine = jnp.concatenate([cotangent, *riders, rider_corner], axis=0)
    cotangent_other = swap(cotangent_mine, "core")
    out_other = swap(out_mine, "core")
    out_full = jnp.stack(
        [jnp.where(core == 0, out_mine, out_other), jnp.where(core == 0, out_other, out_mine)],
        axis=1,
    ).reshape(D, D)
    merged = lax.all_to_all(attended, CHIPS, 0, 0, tiled=True)
    merged, cotangent_other = lax.optimization_barrier((merged, cotangent_other))
    cotangent_plane = (cotangent_mine, cotangent_other)
    merged = over_sharers(merged, sharers).reshape(D, BLOCK)
    middle, second, squares = out_project(merged, inputs, out_full, ffn_gain[None])
    second_plane = plane_gather(second)

    ffn_mine, ffn_other, back_mine, back_other, expand_grad, down_grad = feed(
        second_plane, cotangent_plane, feed_own, hidden_rows
    )
    expand_grad = lax.psum_scatter(expand_grad, "bz", scatter_dimension=0, tiled=True)
    down_grad = lax.psum_scatter(down_grad, "bz", scatter_dimension=0, tiled=True)

    qkv_full = lax.all_gather(
        by_head.transpose(0, 2, 1, 3).reshape(rows, 3 * D), DEVICES, axis=0, tiled=True
    )
    grad_middle, branch_grad, to_chips, grad_ffn = middle_back(
        *plane_scatter(back_mine, back_other), middle, cotangent, ffn_gain[None], out_full
    )
    grad_attended = lax.all_to_all(
        jnp.repeat(to_chips.reshape(H, HD, BLOCK), sharers, axis=0), CHIPS, 0, 0, tiled=True
    )

    joined_mine, joined_other = out_grad(
        plane_members(), merged, branch_grad, ffn_mine, ffn_other, depth
    )
    joined_other = swap(joined_other, "core")
    joined = (joined_mine.astype(f32) + joined_other.astype(f32)).astype(bf16)
    joined = joined.reshape(4, BLOCK, 2 * D)
    to_x = jnp.concatenate([joined[1], joined[3]], axis=0)
    grad_attended, to_x = lax.optimization_barrier((grad_attended, to_x))
    from_x = swap(to_x, "hx")

    query_grad, own_grad, other_grad, bias_grad = attend_back(
        order, place, source, low_tile, high_tile, query, own_kv, other_kv, kept, grad_attended
    )
    query_grad, from_x = lax.optimization_barrier((query_grad, from_x))
    from_y = swap((joined[2].astype(f32) + from_x[BLOCK:].astype(f32)).astype(bf16), "by")
    expand_grad = lax.all_to_all(
        expand_grad.reshape(8, rows, -1), PLANE, 0, 0, tiled=True
    )
    grad_project, grad_qkv_part, gain_grad, attn_grad = project_back(
        query_grad,
        own_grad,
        swap(other_grad, "core"),
        raw,
        cosine,
        sine,
        gains,
        normed_low,
        own_qkv,
    )
    joined = joined[0].astype(f32) + from_x[:BLOCK].astype(f32) + from_y.astype(f32)
    ffn_branch = joined[:, :D]
    outputs = (middle + ffn_branch).astype(bf16)
    grad_out = sum_along_z(joined[:, D:].reshape(depth, rows, D))
    grad_qkv_part, expand_grad = lax.optimization_barrier((grad_qkv_part, expand_grad))
    grad_qkv_part = grad_qkv_part.reshape(chips, 2, rows, 3 * HD)
    grad_qkv_own = pick(grad_qkv_part, core, 1)
    grad_qkv_other = pick(grad_qkv_part, 1 - core, 1)
    grad_qkv_own = grad_qkv_own.astype(f32) + swap(grad_qkv_other, "core").astype(f32)
    values = grad_qkv_own[:, :, 2 * HD :]
    values = jnp.concatenate([values[:, : rows // 2], values[:, rows // 2 :]], axis=2)
    joined = jnp.concatenate(
        [grad_project, grad_qkv_own[:, :, : 2 * HD].astype(bf16), values.astype(bf16)], axis=1
    )
    joined = lax.all_to_all(joined, CHIPS, 0, 0, tiled=True)

    bias_part = jnp.where(
        jnp.arange(H)[None, :] == head, bias_grad[0, :2][:, None], jnp.zeros((2, H), f32)
    )
    packed = jnp.concatenate(
        [
            attn_grad[:, 0] / attn_gain,
            grad_ffn[0],
            gain_grad[0],
            bias_part.reshape(-1),
            squares[:2, 0],
            jnp.sum(ffn_branch * ffn_branch)[None],
            jnp.zeros((93,), f32),
        ]
    )
    summed = sum_everywhere(packed.reshape(-1, 128))
    grad_down = down_grad.astype(f32)
    grad_expand = widen(expand_grad, depth, hidden_rows)
    joined, grad_down, grad_expand = lax.optimization_barrier((joined, grad_down, grad_expand))
    grad_inputs, grad_qkv = input_back(
        over_sharers(joined, sharers), qkv_full, inputs, attn_gain[None], grad_middle
    )
    summed = summed.reshape(-1)
    at = 2 * D + 2 * HD
    root_means = jnp.sqrt(summed[at + 2 * H : at + 2 * H + 3] / (tokens * D))
    return (
        outputs,
        grad_inputs,
        grad_qkv,
        grad_out,
        grad_expand,
        grad_down,
        summed[:D],
        summed[D : 2 * D],
        summed[2 * D : 2 * D + HD],
        summed[2 * D + HD : at],
        summed[at : at + 2 * H].reshape(2, H),
        root_means,
    )


def solution(mesh):
    grid = mesh.devices if mesh.axis_names == ("head", "blk") else mesh.devices.T
    heads, blks = grid.shape
    mesh = Mesh(grid.reshape(heads // 2, 2, blks // 2, 2), ("hx", "core", "bz", "by"))
    split = P(DEVICES, None)

    return jax.shard_map(
        body,
        mesh=mesh,
        in_specs=(split,) * 2 + (P(),) * 5 + (split,) * 4 + (P(),) * 3,
        out_specs=(split,) * 6 + (P(),) * 6,
        check_vma=False,
    )
```

```python
from functools import partial

import jax
import jax.numpy as jnp
from jax import lax
from jax.experimental import pallas as pl
from jax.experimental.pallas import tpu as pltpu
from jax.sharding import Mesh
from jax.sharding import PartitionSpec as P


D = 1024
H = 16
HD = 64
BLOCK = 128
NVAR = 4
EPSILON = 1e-05
THETA = 10000.0

DEVICES = ("bz", "by", "hx", "core")
CHIPS = ("bz", "by", "hx")
PLANE = ("by", "hx", "core")

SEGMENT_LANE = 64
VARIATE_LANE = 76
OWN_VARIATE_LANE = 88
MASK = -512.0
QUERY_TILE = 512
KEY_TILE = 512
PROJECT_BLOCKS = 4

bf16 = jnp.bfloat16
f32 = jnp.float32


def dot(left, right, dims):
    return lax.dot_general(left, right, (dims, ((), ())), preferred_element_type=f32)


def norm_rows(values, gain):
    factor = lax.rsqrt(jnp.mean(values * values, axis=-1, keepdims=True) + EPSILON)
    return values * factor * gain


def norm_back(values, gain, grad):
    factor = lax.rsqrt(jnp.mean(values * values, axis=-1, keepdims=True) + EPSILON)
    scaled = grad * gain
    inner = jnp.mean(scaled * values, axis=-1, keepdims=True)
    grad_values = factor * (scaled - values * (factor * factor) * inner)
    return grad_values, grad * values * factor


def swap(shard, axis):
    return lax.ppermute(shard, axis, [(0, 1), (1, 0)])


def plane_gather(shard):
    mine = jnp.concatenate(quarters(shard), axis=0)
    return mine, swap(mine, "core")


def chip_gather(shard, rider, late):
    depth = lax.axis_size("bz")
    chips = depth * 4
    z, y, x = lax.axis_index("bz"), lax.axis_index("by"), lax.axis_index("hx")
    at = jnp.arange(chips, dtype=jnp.int32)
    if depth > 4:
        pieces = lax.all_gather(shard, CHIPS, axis=0)
        return list(pieces), at, (swap(rider, "hx"), swap(rider, "by")), late
    column = z_shifts([shard] * (depth - 1))
    across_x, across_y = [swap(shard, "hx")], [swap(shard, "by")]
    across_x += [swap(piece, "hx") for piece in column]
    across_y += [swap(piece, "by") for piece in column]
    across_x, across_y, late = lax.optimization_barrier((across_x, across_y, late))
    corner = [swap(across_x[i], "by") if i > 1 else swap(across_y[i], "hx") for i in range(depth)]
    riders = swap(rider, "hx"), swap(rider, "by")
    pieces = [shard, across_x[0], across_y[0], corner[0]]
    pieces += column + across_x[1:] + across_y[1:] + corner[1:]
    back = (z - at // 4) % depth
    flips = ((at % 2) ^ x) + 2 * (((at // 2) % 2) ^ y)
    where = jnp.where(back == 0, flips, 4 + flips * (depth - 1) + back - 1).astype(jnp.int32)
    return pieces, where, riders, late


def sum_everywhere(values):
    for axis in ("core", "hx", "by"):
        values = values + swap(values, axis)
    depth = lax.axis_size("bz")
    if depth > 4:
        step = 1
        while step < depth:
            values = values + lax.ppermute(values, "bz", [(i, i ^ step) for i in range(depth)])
            step *= 2
        return values
    shifted = z_shifts([values] * (depth - 1))
    shifted = [values] + shifted
    while len(shifted) > 1:
        half = len(shifted) // 2
        shifted = [shifted[i] + shifted[half + i] for i in range(half)]
    return shifted[0]


def z_shifts(values):
    depth = lax.axis_size("bz")
    return [
        lax.ppermute(value, "bz", [(i, (i + by + 1) % depth) for i in range(depth)])
        for by, value in enumerate(values)
    ]


def sum_along_z(parts):
    depth = lax.axis_size("bz")
    if depth > 4:
        parts = parts.reshape(-1, parts.shape[2]).astype(bf16)
        return lax.psum_scatter(parts, "bz", scatter_dimension=0, tiled=True).astype(f32)
    z = lax.axis_index("bz").astype(jnp.uint32)
    parts = [pick(parts, (z + jnp.uint32(by)) & jnp.uint32(depth - 1), 0) for by in range(depth)]
    arrived = z_shifts([part.astype(bf16) for part in parts[1:]])
    return sum([part.astype(f32) for part in arrived], parts[0])


def quarters(shard):
    half = shard.shape[0] // 2
    across_x = swap(shard, "hx")
    across_y = swap(shard, "by")
    return [shard, across_x, across_y, swap(across_y[:half], "hx"), swap(across_x[half:], "by")]


def plane_scatter(mine, other):
    rows = mine.shape[0] // 4
    half = rows // 2
    mine = mine.astype(f32) + swap(other, "core").astype(f32)
    corner = mine[3 * rows :].astype(bf16)
    for_y = swap(corner[:half], "hx").astype(f32)
    for_x = swap(corner[half:], "by").astype(f32)
    to_x = mine[rows : 2 * rows]
    to_y = mine[2 * rows : 3 * rows]
    to_x = jnp.concatenate([to_x[:half], to_x[half:] + for_x], axis=0).astype(bf16)
    to_y = jnp.concatenate([to_y[:half] + for_y, to_y[half:]], axis=0).astype(bf16)
    from_x = swap(to_x, "hx")
    from_y = swap(to_y, "by")
    return mine[:rows], from_x, from_y


def plane_members():
    here = (lax.axis_index("by") * 2 + lax.axis_index("hx")) * 2 + lax.axis_index("core")
    return here ^ jnp.array([0, 2, 4, 6, 1, 3, 5, 7], jnp.int32)


def pick(array, index, axis):
    return lax.dynamic_index_in_dim(array, index.astype(jnp.uint32), axis, keepdims=False)


def lanes(shape):
    return lax.broadcasted_iota(jnp.int32, shape, len(shape) - 1)


def half_mean(values, lane):
    low = jnp.sum(jnp.where(lane < HD, values, 0.0), axis=-1, keepdims=True)
    high = jnp.sum(jnp.where(lane < HD, 0.0, values), axis=-1, keepdims=True)
    return jnp.where(lane < HD, low, high) * (1.0 / HD)


def swap_halves(values, lane):
    return jnp.where(
        (lane & (HD - 1)) < HD // 2, pltpu.roll(values, 96, 1), pltpu.roll(values, 32, 1)
    )


def mask_matrix(segments, bias_ref):
    shape = (128, 128)
    row = lax.broadcasted_iota(jnp.int32, shape, 0)
    lane = lax.broadcasted_iota(jnp.int32, shape, 1)
    segment = row - SEGMENT_LANE
    here = lane - SEGMENT_LANE
    apart = (segment >= 0) & (segment < segments) & (here >= 0) & (here < segments)
    matrix = jnp.where(apart & (here != segment), MASK, 0.0)
    variate = row - VARIATE_LANE
    known = (variate >= 0) & (variate < NVAR)
    copy = (lane - VARIATE_LANE) // NVAR
    same = (lane - VARIATE_LANE) % NVAR == variate
    bias = jnp.where(same, bias_ref[1], bias_ref[0])
    high = bias.astype(bf16).astype(f32)
    mid = (bias - high).astype(bf16).astype(f32)
    value = jnp.where(copy == 0, high, jnp.where(copy == 1, mid, bias - high - mid))
    biased = known & (lane >= VARIATE_LANE) & (lane < VARIATE_LANE + 3 * NVAR)
    matrix = jnp.where(biased, value, matrix)
    return jnp.where(known & (lane == OWN_VARIATE_LANE + variate), 1.0, matrix).astype(bf16)


def project_kernel(where_ref, bias_ref, *refs, chips, segments):
    piece_refs, refs = refs[:chips], refs[chips:]
    gain_ref, weight_ref, cosine_ref, sine_ref, gains_ref, hot_ref = refs[:6]
    normed_ref, raw_ref, query_ref, kv_ref, out_ref, x_ref, mask_ref, arrived = refs[6:]
    step = pl.program_id(0)

    @pl.when(step == 0)
    def _():
        copies = [
            pltpu.make_async_copy(piece_refs[i], x_ref.at[i], arrived.at[i]) for i in range(chips)
        ]
        for copy in copies:
            copy.start()
        mask_ref[...] = mask_matrix(segments, bias_ref)
        for copy in copies:
            copy.wait()

    places = [where_ref[step * PROJECT_BLOCKS + i] for i in range(PROJECT_BLOCKS)]
    for i, place in enumerate(places):
        out_ref[i] = x_ref[place, BLOCK:]
    x = jnp.concatenate([x_ref[place, :BLOCK] for place in places], axis=0).astype(f32)
    normed = norm_rows(x, gain_ref[...]).astype(bf16)
    normed_ref[...] = normed
    project = dot(normed, weight_ref[...], ((1,), (0,)))
    both = project[:, : 2 * HD]
    value = project[:, 2 * HD :]
    raw_ref[...] = both
    lane = lanes(both.shape)
    scaled = both * lax.rsqrt(half_mean(both * both, lane) + EPSILON) * gains_ref[...]
    turned = scaled * cosine_ref[...] + swap_halves(scaled, lane) * sine_ref[...]
    turned = turned.astype(bf16).astype(f32)
    hot = hot_ref[...]
    query_ref[...] = jnp.where(lane < HD, turned, hot.astype(f32)).astype(bf16)
    key = pltpu.roll(turned * HD ** (-0.5), HD, 1)
    ones = jnp.where((lane >= HD) & (lane < HD + 3), 1.0, 0.0)
    kv_ref[:, :128] = jnp.where(lane < HD, key, dot(hot, mask_ref[...], ((1,), (0,)))).astype(bf16)
    kv_ref[:, 128:] = jnp.where(lane < HD, value, ones).astype(bf16)


def project(where, bias, pieces, gain, weight, cosine, sine, gains, hot, segments):
    blocks = len(pieces)
    rows = blocks * BLOCK
    step_rows = PROJECT_BLOCKS * BLOCK
    out_rows = pieces[0].shape[0] - BLOCK
    row_spec = lambda width: pl.BlockSpec((step_rows, width), lambda j, *unused: (j, 0))
    whole = lambda array: pl.BlockSpec(array.shape, lambda j, *unused: (0, 0))
    anywhere = pl.BlockSpec(memory_space=pl.ANY)
    tables = [whole(gain), whole(weight), row_spec(128), row_spec(128), whole(gains)]
    return pl.pallas_call(
        partial(project_kernel, chips=blocks, segments=segments),
        grid_spec=pltpu.PrefetchScalarGridSpec(
            num_scalar_prefetch=2,
            grid=(blocks // PROJECT_BLOCKS,),
            in_specs=[anywhere] * blocks + tables + [row_spec(128)],
            out_specs=[
                row_spec(D),
                row_spec(128),
                row_spec(128),
                row_spec(256),
                pl.BlockSpec((PROJECT_BLOCKS, out_rows, D), lambda j, *unused: (j, 0, 0)),
            ],
            scratch_shapes=[
                pltpu.VMEM((blocks, BLOCK + out_rows, D), bf16),
                pltpu.VMEM((128, 128), bf16),
                pltpu.SemaphoreType.DMA((blocks,)),
            ],
        ),
        out_shape=[
            jax.ShapeDtypeStruct((rows, D), bf16),
            jax.ShapeDtypeStruct((rows, 128), f32),
            jax.ShapeDtypeStruct((rows, 128), bf16),
            jax.ShapeDtypeStruct((rows, 256), bf16),
            jax.ShapeDtypeStruct((blocks, out_rows, D), bf16),
        ],
        name="project",
    )(where, bias, *pieces, gain, weight, cosine, sine, gains, hot)


def sort_keys(place_ref, own_ref, other_ref, keys_ref):
    blocks = own_ref.shape[0] // BLOCK
    for half, source_ref in ((0, own_ref), (1, other_ref)):

        def put(j, unused, half=half, source_ref=source_ref):
            source = pl.multiple_of(j * BLOCK, BLOCK)
            target = pl.multiple_of(place_ref[half * blocks + j] * BLOCK, BLOCK)
            keys_ref[pl.ds(target, BLOCK), :] = source_ref[pl.ds(source, BLOCK), :]
            return unused

        lax.fori_loop(0, blocks, put, 0, unroll=8)


def block_start(order_ref, index):
    return pl.multiple_of(order_ref[index] * BLOCK, BLOCK)


def attend_kernel(
    order_ref,
    place_ref,
    low_ref,
    high_ref,
    query_ref,
    own_ref,
    other_ref,
    kept_ref,
    attended_ref,
    keys_ref,
):
    tile = pl.program_id(0)
    count = QUERY_TILE // BLOCK

    @pl.when(tile == 0)
    def _():
        sort_keys(place_ref, own_ref, other_ref, keys_ref)
        if order_ref.shape[0] * BLOCK != query_ref.shape[0]:
            kept_ref[...] = jnp.zeros_like(kept_ref)
            attended_ref[...] = jnp.zeros_like(attended_ref)

    starts = [block_start(order_ref, tile * count + i) for i in range(count)]
    query = jnp.concatenate([query_ref[pl.ds(start, BLOCK), :] for start in starts], axis=0)

    def chunk(index, accumulated):
        window = pl.ds(pl.multiple_of(index * KEY_TILE, KEY_TILE), KEY_TILE)
        expo = jnp.exp(dot(query, keys_ref[window, :128], ((1,), (1,))))
        return accumulated + dot(expo.astype(bf16), keys_ref[window, 128:], ((1,), (0,)))

    accumulated = lax.fori_loop(
        low_ref[tile], high_ref[tile], chunk, jnp.zeros((QUERY_TILE, 128), f32)
    )
    totals = accumulated[:, HD : HD + 1]
    lane = lanes(accumulated.shape)
    kept = jnp.where(lane < HD, accumulated / totals, totals)
    for i, start in enumerate(starts):
        piece = kept[i * BLOCK : (i + 1) * BLOCK]
        kept_ref[pl.ds(start, BLOCK), :] = piece
        attended_ref[order_ref[tile * count + i]] = piece.T[:HD].astype(bf16)


def fixed(array):
    return pl.BlockSpec(
        array.shape, lambda *unused: (0,) * len(array.shape), pipeline_mode=pl.Buffered(1)
    )


def attend(order, place, low, high, query, own, other):
    rows = query.shape[0]
    operands = (query, own, other)
    outs = (
        jax.ShapeDtypeStruct((rows, 128), f32),
        jax.ShapeDtypeStruct((rows // BLOCK, HD, BLOCK), bf16),
    )
    return pl.pallas_call(
        attend_kernel,
        grid_spec=pltpu.PrefetchScalarGridSpec(
            num_scalar_prefetch=4,
            grid=(low.shape[0],),
            in_specs=[fixed(array) for array in operands],
            out_specs=[fixed(array) for array in outs],
            scratch_shapes=[pltpu.VMEM((2 * rows, 256), bf16)],
        ),
        out_shape=list(outs),
        name="attend",
    )(order, place, low, high, *operands)


def attend_back_kernel(
    order_ref,
    place_ref,
    source_ref,
    low_ref,
    high_ref,
    query_ref,
    own_ref,
    other_ref,
    kept_ref,
    grad_ref,
    query_grad_ref,
    own_grad_ref,
    other_grad_ref,
    bias_ref,
    keys_ref,
    sorted_ref,
    wide_ref,
    sums_ref,
    every_ref,
    same_ref,
):
    step = pl.program_id(0)
    own_rows = own_ref.shape[0]
    taken = order_ref.shape[0]

    @pl.when(step == 0)
    def _():
        sort_keys(place_ref, own_ref, other_ref, keys_ref)
        every_ref[...] = jnp.zeros_like(every_ref)
        same_ref[...] = jnp.zeros_like(same_ref)
        sums_ref[...] = jnp.zeros_like(sums_ref)
        if taken * BLOCK != own_rows:
            query_grad_ref[...] = jnp.zeros_like(query_grad_ref)
        lane = lanes((BLOCK, 128))

        def put(i, unused):
            source = pl.ds(block_start(order_ref, i), BLOCK)
            target = pl.ds(pl.multiple_of(i * BLOCK, BLOCK), BLOCK)
            sorted_ref[target, :] = query_ref[source, :]
            kept = kept_ref[source, :]
            grad = grad_ref[order_ref[i]].astype(f32)
            grad = jnp.concatenate([grad, jnp.zeros_like(grad)], axis=0).T
            inverse = 1.0 / kept[:, HD : HD + 1]
            center = jnp.sum(grad * kept, axis=1, keepdims=True) * inverse
            center_high = center.astype(bf16).astype(f32)
            center_rest = center - center_high
            center_mid = center_rest.astype(bf16).astype(f32)
            center_low = center_rest - center_mid
            wide = jnp.where(lane == HD, -center_high, 0.0)
            wide = jnp.where(lane == HD + 1, -center_mid, wide)
            wide = jnp.where(lane == HD + 2, -center_low, wide)
            wide_ref[target, :] = jnp.where(lane < HD, grad * inverse, wide).astype(bf16)
            return unused

        lax.fori_loop(0, taken, put, 0, unroll=8)

    window = pl.ds(pl.multiple_of(step * KEY_TILE, KEY_TILE), KEY_TILE)
    key = keys_ref[window, :128]
    value = keys_ref[window, 128:]

    def tile(index, grads):
        rows = pl.ds(pl.multiple_of(index * QUERY_TILE, QUERY_TILE), QUERY_TILE)
        query = sorted_ref[rows, :]
        wide = wide_ref[rows, :]
        expo = jnp.exp(dot(key, query, ((1,), (1,))))
        score_low = (expo * dot(value, wide, ((1,), (1,)))).astype(bf16)
        sums_ref[rows, :] += dot(score_low, key, ((0,), (0,)))
        return (
            grads[0] + dot(score_low, query, ((1,), (0,))),
            grads[1] + dot(expo.astype(bf16), wide, ((1,), (0,))),
        )

    empty = jnp.zeros((KEY_TILE, 128), f32)
    key_grad, value_grad = lax.fori_loop(low_ref[step], high_ref[step], tile, (empty, empty))
    lane = lanes(key_grad.shape)
    joined = jnp.where(lane < HD, value_grad, pltpu.roll(key_grad, HD, 1) * HD ** (-0.5))
    joined = joined.astype(bf16)
    for i in range(KEY_TILE // BLOCK):
        source = source_ref[step * (KEY_TILE // BLOCK) + i] * BLOCK
        piece = joined[i * BLOCK : (i + 1) * BLOCK]

        @pl.when(source < own_rows)
        def _(source=source, piece=piece):
            own_grad_ref[pl.ds(pl.multiple_of(source, BLOCK), BLOCK), :] = piece

        @pl.when(source >= own_rows)
        def _(source=source, piece=piece):
            other_grad_ref[pl.ds(pl.multiple_of(source - own_rows, BLOCK), BLOCK), :] = piece

    every = jnp.where((lane >= VARIATE_LANE) & (lane < VARIATE_LANE + NVAR), key_grad, 0.0)
    shift = 128 + VARIATE_LANE - OWN_VARIATE_LANE
    same = every * pltpu.roll(key.astype(f32), shift, 1)
    every_ref[...] += jnp.sum(every.reshape(-1, 8, 128), axis=0)
    same_ref[...] += jnp.sum(same.reshape(-1, 8, 128), axis=0)

    @pl.when(step == pl.num_programs(0) - 1)
    def _():
        def put(i, unused):
            target = pl.ds(block_start(order_ref, i), BLOCK)
            rows = pl.ds(pl.multiple_of(i * BLOCK, BLOCK), BLOCK)
            query_grad_ref[target, :] = sums_ref[rows, :].astype(bf16)
            return unused

        lax.fori_loop(0, taken, put, 0, unroll=8)
        every = jnp.sum(every_ref[...], keepdims=True)
        same = jnp.sum(same_ref[...], keepdims=True)
        bias_lane = lanes((8, 128))
        bias_ref[...] = jnp.where(
            bias_lane == 0, every - same, jnp.where(bias_lane == 1, same, 0.0)
        )


def attend_back(order, place, source, low, high, query, own, other, kept, grad):
    rows = query.shape[0]
    taken = order.shape[0] * BLOCK
    operands = (query, own, other, kept, grad)
    outs = tuple(jax.ShapeDtypeStruct((rows, 128), bf16) for _ in range(3)) + (
        jax.ShapeDtypeStruct((8, 128), f32),
    )
    return pl.pallas_call(
        attend_back_kernel,
        grid_spec=pltpu.PrefetchScalarGridSpec(
            num_scalar_prefetch=5,
            grid=(low.shape[0],),
            in_specs=[fixed(array) for array in operands],
            out_specs=[fixed(array) for array in outs],
            scratch_shapes=[
                pltpu.VMEM((2 * rows, 256), bf16),
                pltpu.VMEM((taken, 128), bf16),
                pltpu.VMEM((taken, 128), bf16),
                pltpu.VMEM((taken, 128), f32),
                pltpu.VMEM((8, 128), f32),
                pltpu.VMEM((8, 128), f32),
            ],
        ),
        out_shape=list(outs),
        name="attend_back",
    )(order, place, source, low, high, *operands)


def project_back_kernel(
    query_grad_ref,
    own_ref,
    other_ref,
    raw_ref,
    cosine_ref,
    sine_ref,
    gains_ref,
    normed_ref,
    forward_ref,
    grad_ref,
    weight_grad_ref,
    gain_grad_ref,
    attn_grad_ref,
    weight_ref,
    gain_ref,
):
    step = pl.program_id(0)

    @pl.when(step == 0)
    def _():
        weight_ref[...] = jnp.zeros_like(weight_ref)
        gain_ref[...] = jnp.zeros_like(gain_ref)

    kv_grad = own_ref[...].astype(f32) + other_ref[...].astype(f32)
    kv_grad = kv_grad.astype(bf16).astype(f32)
    lane = lanes(kv_grad.shape)
    turned = jnp.where(lane < HD, query_grad_ref[...].astype(f32), kv_grad)
    grad = turned * cosine_ref[...] - swap_halves(turned, lane) * sine_ref[...]
    raw = raw_ref[...]
    factor = lax.rsqrt(half_mean(raw * raw, lane) + EPSILON)
    scaled = grad * gains_ref[...]
    inner = half_mean(scaled * raw, lane)
    both = factor * (scaled - raw * (factor * factor) * inner)
    gain_ref[...] += jnp.sum(grad * raw * factor, axis=0, keepdims=True)
    full = jnp.concatenate([both, jnp.where(lane < HD, kv_grad, 0.0)], axis=1)
    for i in range(grad_ref.shape[0]):
        grad_ref[i] = full[i * BLOCK : (i + 1) * BLOCK].T[: 3 * HD].astype(bf16)
    weight_ref[...] += dot(normed_ref[...], full.astype(bf16), ((0,), (0,)))

    @pl.when(step == pl.num_programs(0) - 1)
    def _():
        weight_grad_ref[...] = weight_ref[:, : 3 * HD].astype(bf16)
        gain_grad_ref[...] = jnp.broadcast_to(gain_ref[...], gain_grad_ref.shape)
        forward = forward_ref[...].astype(f32)
        attn = jnp.sum(weight_ref[...] * forward, axis=1, keepdims=True)
        attn_grad_ref[...] = jnp.broadcast_to(attn, attn_grad_ref.shape)


def project_back(query_grad, own, other, raw, cosine, sine, gains, normed, forward):
    rows = query_grad.shape[0]
    step_rows = 4 * BLOCK
    row_spec = lambda width: pl.BlockSpec((step_rows, width), lambda j: (j, 0))
    whole = lambda shape: pl.BlockSpec(shape, lambda j: (0, 0))
    return pl.pallas_call(
        project_back_kernel,
        grid=(rows // step_rows,),
        in_specs=[row_spec(128)] * 6 + [whole(gains.shape), row_spec(D), whole(forward.shape)],
        out_specs=[
            pl.BlockSpec((step_rows // BLOCK, 3 * HD, BLOCK), lambda j: (j, 0, 0)),
            whole((D, 3 * HD)),
            whole((8, 128)),
            whole((D, 128)),
        ],
        out_shape=[
            jax.ShapeDtypeStruct((rows // BLOCK, 3 * HD, BLOCK), bf16),
            jax.ShapeDtypeStruct((D, 3 * HD), bf16),
            jax.ShapeDtypeStruct((8, 128), f32),
            jax.ShapeDtypeStruct((D, 128), f32),
        ],
        scratch_shapes=[pltpu.VMEM((D, 4 * HD), f32), pltpu.VMEM((1, 128), f32)],
        name="project_back",
    )(query_grad, own, other, raw, cosine, sine, gains, normed, forward)


def feed_kernel(
    second_mine_ref,
    second_other_ref,
    grad_mine_ref,
    grad_other_ref,
    weight_ref,
    ffn_mine_ref,
    ffn_other_ref,
    back_mine_ref,
    back_other_ref,
    expand_out_ref,
    down_out_ref,
    expand_ref,
    down_ref,
    expand_grad_ref,
    down_grad_ref,
):
    step = pl.program_id(0)
    half = pl.num_programs(0) // 2
    depth, both_rows, width = weight_ref.shape
    down_rows = down_ref.shape[0] // depth
    expand_rows = both_rows - down_rows

    @pl.when(step == 0)
    def _():
        for z in range(depth):
            expand_ref[z * expand_rows : (z + 1) * expand_rows] = weight_ref[z, :expand_rows]
            down_ref[z * down_rows : (z + 1) * down_rows] = weight_ref[z, expand_rows:]
        expand_grad_ref[...] = jnp.zeros_like(expand_grad_ref)
        down_grad_ref[...] = jnp.zeros_like(down_grad_ref)

    second = jnp.where(step < half, second_mine_ref[...], second_other_ref[...])
    grad = jnp.where(step < half, grad_mine_ref[...], grad_other_ref[...])
    expand = dot(second, expand_ref[...], ((1,), (0,)))
    gate = expand[:, : width // 2]
    up = expand[:, width // 2 :]
    sigmoid = 1.0 / (1.0 + jnp.exp(-gate))
    silu = gate * sigmoid
    hidden = (silu * up).astype(bf16)
    grad_hidden = dot(grad, down_ref[...], ((1,), (1,)))
    grad_gate = grad_hidden * up * (sigmoid * (1.0 + gate * (1.0 - sigmoid)))
    rows = jnp.concatenate([grad_gate, grad_hidden * silu], axis=1).astype(bf16)
    ffn = dot(hidden, down_ref[...], ((1,), (0,))).astype(bf16)
    back = dot(rows, expand_ref[...], ((1,), (1,))).astype(bf16)
    expand_grad_ref[...] += dot(second, rows, ((0,), (0,)))
    down_grad_ref[...] += dot(hidden, grad, ((0,), (0,)))

    @pl.when(step < half)
    def _():
        ffn_mine_ref[...] = ffn
        back_mine_ref[...] = back

    @pl.when(step >= half)
    def _():
        ffn_other_ref[...] = ffn
        back_other_ref[...] = back

    @pl.when(step == pl.num_programs(0) - 1)
    def _():
        expand_out_ref[...] = expand_grad_ref[...].astype(bf16)
        down_out_ref[...] = down_grad_ref[...].astype(bf16)


def feed(second, grad, weight, down_rows):
    rows = second[0].shape[0]
    tile = 256
    steps = rows // tile
    depth, both_rows, width = weight.shape
    mine = pl.BlockSpec((tile, D), lambda i: (jnp.minimum(i, steps - 1), 0))
    other = pl.BlockSpec((tile, D), lambda i: (jnp.maximum(i - steps, 0), 0))
    whole = pl.BlockSpec(weight.shape, lambda i: (0, 0, 0), pipeline_mode=pl.Buffered(1))
    token_rows = jax.ShapeDtypeStruct((rows, D), bf16)
    expand_out = jax.ShapeDtypeStruct((depth * (both_rows - down_rows), width), bf16)
    down_out = jax.ShapeDtypeStruct((depth * down_rows, D), bf16)
    return pl.pallas_call(
        feed_kernel,
        grid=(2 * steps,),
        in_specs=[mine, other, mine, other, whole],
        out_specs=[mine, other, mine, other, fixed(expand_out), fixed(down_out)],
        out_shape=[token_rows] * 4 + [expand_out, down_out],
        scratch_shapes=[
            pltpu.VMEM((depth * (both_rows - down_rows), width), bf16),
            pltpu.VMEM((depth * down_rows, D), bf16),
            pltpu.VMEM((depth * (both_rows - down_rows), width), f32),
            pltpu.VMEM((depth * down_rows, D), f32),
        ],
        name="feed",
    )(*second, *grad, weight)


def out_kernel(parts_ref, x_ref, weight_ref, gain_ref, middle_ref, second_ref, squares_ref):
    branch = dot(parts_ref[...], weight_ref[...], ((0,), (0,)))
    x = x_ref[...].astype(f32)
    middle = x + branch
    middle_ref[...] = middle
    second_ref[...] = norm_rows(middle, gain_ref[...]).astype(bf16)
    row = lax.broadcasted_iota(jnp.int32, squares_ref.shape, 0)
    x_sum = jnp.sum(x * x, keepdims=True)
    branch_sum = jnp.sum(branch * branch, keepdims=True)
    squares_ref[...] = jnp.where(row == 0, x_sum, branch_sum)


def out_project(parts, x, weight, gain):
    rows = x.shape[0]
    return pl.pallas_call(
        out_kernel,
        out_shape=[
            jax.ShapeDtypeStruct((rows, D), f32),
            jax.ShapeDtypeStruct((rows, D), bf16),
            jax.ShapeDtypeStruct((8, 128), f32),
        ],
        name="out_project",
    )(parts, x, weight, gain)


def middle_back_kernel(
    own_ref,
    from_x_ref,
    from_y_ref,
    middle_ref,
    cotangent_ref,
    gain_ref,
    weight_ref,
    grad_middle_ref,
    branch_ref,
    parts_ref,
    gain_grad_ref,
):
    grad_second = own_ref[...] + from_x_ref[...].astype(f32) + from_y_ref[...].astype(f32)
    grad_middle, gain_rows = norm_back(middle_ref[...], gain_ref[...], grad_second)
    grad_middle = cotangent_ref[...].astype(f32) + grad_middle
    grad_middle_ref[...] = grad_middle
    branch = grad_middle.astype(bf16)
    branch_ref[...] = branch
    parts_ref[...] = dot(weight_ref[...], branch, ((1,), (1,))).astype(bf16)
    gain_grad_ref[...] = jnp.broadcast_to(
        jnp.sum(gain_rows, axis=0, keepdims=True), gain_grad_ref.shape
    )


def middle_back(own, from_x, from_y, middle, cotangent, gain, weight):
    rows = middle.shape[0]
    return pl.pallas_call(
        middle_back_kernel,
        out_shape=[
            jax.ShapeDtypeStruct((rows, D), f32),
            jax.ShapeDtypeStruct((rows, D), bf16),
            jax.ShapeDtypeStruct((D, rows), bf16),
            jax.ShapeDtypeStruct((8, D), f32),
        ],
        name="middle_back",
    )(own, from_x, from_y, middle, cotangent, gain, weight)


def out_grad_kernel(
    members_ref,
    merged_ref,
    branch_ref,
    ffn_mine_ref,
    ffn_other_ref,
    mine_ref,
    other_ref,
    grad_ref,
    depth,
):
    shard = mine_ref.shape[0] // 4
    rows = shard // depth
    grad_ref[...] = dot(merged_ref[...], branch_ref[...], ((1,), (0,)))
    mine_ref[:, :D] = ffn_mine_ref[...]
    other_ref[:, :D] = ffn_other_ref[...]
    for place in range(8):
        target_ref = mine_ref if place < 4 else other_ref
        for z in range(depth):
            source = pl.multiple_of((z * 8 + members_ref[place]) * rows, rows)
            target = (place % 4) * shard + z * rows
            target_ref[target : target + rows, D:] = grad_ref[pl.ds(source, rows), :].astype(bf16)


def out_grad(members, merged, branch, ffn_mine, ffn_other, depth):
    joined = jax.ShapeDtypeStruct((ffn_mine.shape[0], 2 * D), bf16)
    operands = (merged, branch, ffn_mine, ffn_other)
    return pl.pallas_call(
        partial(out_grad_kernel, depth=depth),
        grid_spec=pltpu.PrefetchScalarGridSpec(
            num_scalar_prefetch=1,
            grid=(1,),
            in_specs=[fixed(array) for array in operands],
            out_specs=[fixed(joined), fixed(joined)],
            scratch_shapes=[pltpu.VMEM((D, D), f32)],
        ),
        out_shape=[joined, joined],
        name="out_grad",
    )(members, *operands)


def input_back_kernel(
    joined_ref, weight_ref, x_ref, gain_ref, middle_ref, grad_ref, qkv_ref, wide_ref
):
    heads = joined_ref.shape[0]
    rows = qkv_ref.shape[0]
    for head in range(heads):
        wide_ref[head * 3 * HD : (head + 1) * 3 * HD] = joined_ref[head, : 3 * HD]
    for pair in range(heads // 2):
        left = joined_ref[2 * pair, 3 * HD :].astype(f32)
        right = joined_ref[2 * pair + 1, 3 * HD :].astype(f32)
        at = pair * 2 * HD
        low = jnp.concatenate([left[:, :HD], right[:, :HD]], axis=1)
        high = jnp.concatenate([left[:, HD:], right[:, HD:]], axis=1)
        qkv_ref[:, at : at + 2 * HD] = low[:rows]
        qkv_ref[:, D + at : D + at + 2 * HD] = high[:rows]
        qkv_ref[: rows // 2, 2 * D + at : 2 * D + at + 2 * HD] = low[rows:]
        qkv_ref[rows // 2 :, 2 * D + at : 2 * D + at + 2 * HD] = high[rows:]
    grad_normed = dot(wide_ref[...], weight_ref[...], ((0,), (1,)))
    grad, _ = norm_back(x_ref[...].astype(f32), gain_ref[...], grad_normed)
    grad_ref[...] = middle_ref[...] + grad


def input_back(joined, weight, x, gain, middle):
    rows = x.shape[0]
    return pl.pallas_call(
        input_back_kernel,
        out_shape=[
            jax.ShapeDtypeStruct((rows, D), f32),
            jax.ShapeDtypeStruct(((joined.shape[1] - 3 * HD) * 2 // 3, 3 * D), f32),
        ],
        scratch_shapes=[pltpu.VMEM((3 * D, rows), bf16)],
        name="input_back",
    )(joined, weight, x, gain, middle)


def widen_kernel(parts_ref, grad_ref):
    sources, _, width = parts_ref.shape
    for source in range(sources):
        for at in range(width // 128):
            to = (at * sources + source) * 128
            grad_ref[:, to : to + 128] = parts_ref[source, :, at * 128 : (at + 1) * 128].astype(f32)


def widen(parts, depth, hidden_rows):
    sources, rows, width = parts.shape
    if hidden_rows != 128:
        parts = parts.reshape(sources, rows, 2, depth, hidden_rows)
        return parts.transpose(1, 2, 3, 0, 4).reshape(rows, -1).astype(f32)
    return pl.pallas_call(
        widen_kernel, out_shape=jax.ShapeDtypeStruct((rows, sources * width), f32), name="widen"
    )(parts)


def token_meta(seq_lengths, block_order):
    blocks = block_order.shape[0]
    packed_at = jnp.repeat(block_order, BLOCK) * BLOCK + jnp.tile(
        jnp.arange(BLOCK, dtype=jnp.int32), blocks
    )
    ends = jnp.cumsum(seq_lengths)
    after = packed_at[:, None] >= ends[None, :]
    segment = jnp.sum(after.astype(jnp.int32), axis=1)
    begin = jnp.max(jnp.where(after, ends[None, :], jnp.zeros_like(ends)[None, :]), axis=1)
    return (segment, packed_at - begin, ends)


def own_rows(array, core):
    pairs = array.reshape(-1, 2, BLOCK)
    return pick(pairs, core, 1).reshape(-1)


def one_hot_rows(segment, variate):
    lane = jnp.arange(128, dtype=jnp.int32)[None, :]
    hot = lane == SEGMENT_LANE + segment[:, None]
    for copy in range(3):
        hot = hot | (lane == VARIATE_LANE + copy * NVAR + variate[:, None])
    return hot.astype(bf16)


def over_sharers(parts, sharers):
    if sharers == 1:
        return parts
    parts = parts.reshape((H, sharers) + parts.shape[1:]).astype(f32)
    return jnp.sum(parts, axis=1).astype(bf16)


def body(
    inputs,
    cotangent,
    attn_gain,
    ffn_gain,
    query_gain,
    key_gain,
    variate_bias,
    qkv_weight,
    out_weight,
    expand_weight,
    down_weight,
    seq_lengths,
    variate_ids,
    block_order,
):
    depth = lax.axis_size("bz")
    chips = depth * 4
    sharers = chips // H
    core = lax.axis_index("core")
    chip = (lax.axis_index("bz") * 2 + lax.axis_index("by")) * 2 + lax.axis_index("hx")
    head = chip // sharers
    share = chip % sharers
    rows = qkv_weight.shape[0]
    hidden_rows = down_weight.shape[0]
    segments = seq_lengths.shape[0] + 1
    tokens = variate_ids.shape[0]

    by_head = qkv_weight.reshape(rows, 3, H, HD)
    to_heads = jnp.repeat(
        by_head.transpose(2, 0, 1, 3).reshape(H, rows, 3 * HD), 2 * sharers, axis=0
    )
    own_qkv = lax.all_to_all(to_heads, DEVICES, 0, 0, tiled=True)
    own_qkv = jnp.pad(own_qkv.reshape(D, 3 * HD), ((0, 0), (0, HD)))
    to_plane = (
        expand_weight.reshape(rows, 2, depth, 8, hidden_rows)
        .transpose(3, 0, 1, 2, 4)
        .reshape(8, rows, 2 * depth * hidden_rows)
    )
    expand_part = lax.all_to_all(to_plane, PLANE, 0, 0, tiled=True)
    expand_part = expand_part.reshape(8 * rows, -1)

    segment, position, ends = token_meta(seq_lengths, block_order)
    own_segment = own_rows(segment, core)
    own_variate = own_rows(variate_ids, core)
    own_position = own_rows(position, core)
    bias = pick(variate_bias, head, 1)
    hot = one_hot_rows(own_segment, own_variate)
    freqs = THETA ** (-jnp.arange(HD // 2, dtype=f32) / (HD // 2))
    angles = own_position.astype(f32)[:, None] * freqs[None, :]
    cosine = jnp.tile(jnp.cos(angles), (1, 4))
    sine = jnp.sin(angles)
    sine = jnp.tile(jnp.concatenate([-sine, sine], axis=1), (1, 2))
    pairs = block_order.reshape(chips, 2)
    own_place = pick(pairs, core, 1)
    other_place = pick(pairs, 1 - core, 1)
    place = jnp.concatenate([own_place, other_place])
    rank = jnp.sum((own_place[None, :] < own_place[:, None]).astype(jnp.int32), axis=1)
    taken = chips // sharers
    wanted = share * taken + jnp.arange(taken, dtype=jnp.int32)
    chosen = (rank[None, :] == wanted[:, None]).astype(jnp.int32)
    order = jnp.sum(chosen * jnp.arange(chips, dtype=jnp.int32)[None, :], axis=1)
    sorted_place = jnp.sum(chosen * own_place[None, :], axis=1).reshape(-1, QUERY_TILE // BLOCK)
    first_token = sorted_place[:, 0] * BLOCK
    last_token = sorted_place[:, -1] * BLOCK + BLOCK - 1
    begins = jnp.max(jnp.where(ends[None, :] <= first_token[:, None], ends[None, :], 0), axis=1)
    finish = jnp.min(jnp.where(ends[None, :] > last_token[:, None], ends[None, :], tokens), axis=1)
    low = begins // KEY_TILE
    high = (finish + KEY_TILE - 1) // KEY_TILE
    slots = jnp.arange(2 * chips, dtype=jnp.int32)
    source = jnp.sum(
        jnp.where(place[None, :] == slots[:, None], slots[None, :], 0), axis=1, dtype=jnp.int32
    )
    chunks = jnp.arange(tokens // KEY_TILE, dtype=jnp.int32)[:, None]
    low_tile = jnp.sum((high[None, :] <= chunks).astype(jnp.int32), axis=1)
    high_tile = jnp.sum((low[None, :] <= chunks).astype(jnp.int32), axis=1)
    gains = jnp.concatenate([query_gain, key_gain])[None, :]

    late = (hot, cosine, sine, place, order, low, high, source, low_tile, high_tile)
    pieces, where, riders, late = chip_gather(
        jnp.concatenate([inputs, out_weight], axis=0), cotangent, late
    )
    hot, cosine, sine, place, order, low, high, source, low_tile, high_tile = late

    feed_part = jnp.concatenate([expand_part, down_weight], axis=0)
    feed_own = lax.all_gather(feed_part[None], "bz", axis=0, tiled=True)

    normed_low, raw, query, own_kv, out_mine = project(
        where, bias, pieces, attn_gain[None], own_qkv, cosine, sine, gains, hot, segments
    )
    own_kv, riders = lax.optimization_barrier((own_kv, riders))
    other_kv = swap(own_kv, "core")
    rider_corner = swap(riders[0], "by")
    kept, attended = attend(order, place, low, high, query, own_kv, other_kv)
    attended, rider_corner = lax.optimization_barrier((attended, rider_corner))
    cotangent_mine = jnp.concatenate([cotangent, *riders, rider_corner], axis=0)
    cotangent_other = swap(cotangent_mine, "core")
    out_other = swap(out_mine, "core")
    out_full = jnp.stack(
        [jnp.where(core == 0, out_mine, out_other), jnp.where(core == 0, out_other, out_mine)],
        axis=1,
    ).reshape(D, D)
    merged = lax.all_to_all(attended, CHIPS, 0, 0, tiled=True)
    merged, cotangent_other = lax.optimization_barrier((merged, cotangent_other))
    cotangent_plane = (cotangent_mine, cotangent_other)
    merged = over_sharers(merged, sharers).reshape(D, BLOCK)
    middle, second, squares = out_project(merged, inputs, out_full, ffn_gain[None])
    second_plane = plane_gather(second)

    ffn_mine, ffn_other, back_mine, back_other, expand_grad, down_grad = feed(
        second_plane, cotangent_plane, feed_own, hidden_rows
    )
    expand_grad = lax.psum_scatter(expand_grad, "bz", scatter_dimension=0, tiled=True)
    down_grad = lax.psum_scatter(down_grad, "bz", scatter_dimension=0, tiled=True)

    qkv_full = lax.all_gather(
        by_head.transpose(0, 2, 1, 3).reshape(rows, 3 * D), DEVICES, axis=0, tiled=True
    )
    grad_middle, branch_grad, to_chips, grad_ffn = middle_back(
        *plane_scatter(back_mine, back_other), middle, cotangent, ffn_gain[None], out_full
    )
    grad_attended = lax.all_to_all(
        jnp.repeat(to_chips.reshape(H, HD, BLOCK), sharers, axis=0), CHIPS, 0, 0, tiled=True
    )

    joined_mine, joined_other = out_grad(
        plane_members(), merged, branch_grad, ffn_mine, ffn_other, depth
    )
    joined_other = swap(joined_other, "core")
    joined = (joined_mine.astype(f32) + joined_other.astype(f32)).astype(bf16)
    joined = joined.reshape(4, BLOCK, 2 * D)
    to_x = jnp.concatenate([joined[1], joined[3]], axis=0)
    grad_attended, to_x = lax.optimization_barrier((grad_attended, to_x))
    from_x = swap(to_x, "hx")

    query_grad, own_grad, other_grad, bias_grad = attend_back(
        order, place, source, low_tile, high_tile, query, own_kv, other_kv, kept, grad_attended
    )
    query_grad, from_x = lax.optimization_barrier((query_grad, from_x))
    from_y = swap((joined[2].astype(f32) + from_x[BLOCK:].astype(f32)).astype(bf16), "by")
    expand_grad = lax.all_to_all(
        expand_grad.reshape(8, rows, -1), PLANE, 0, 0, tiled=True
    )
    grad_project, grad_qkv_part, gain_grad, attn_grad = project_back(
        query_grad,
        own_grad,
        swap(other_grad, "core"),
        raw,
        cosine,
        sine,
        gains,
        normed_low,
        own_qkv,
    )
    joined = joined[0].astype(f32) + from_x[:BLOCK].astype(f32) + from_y.astype(f32)
    ffn_branch = joined[:, :D]
    outputs = (middle + ffn_branch).astype(bf16)
    grad_out = sum_along_z(joined[:, D:].reshape(depth, rows, D))
    grad_qkv_part, expand_grad = lax.optimization_barrier((grad_qkv_part, expand_grad))
    grad_qkv_part = grad_qkv_part.reshape(chips, 2, rows, 3 * HD)
    grad_qkv_own = pick(grad_qkv_part, core, 1)
    grad_qkv_other = pick(grad_qkv_part, 1 - core, 1)
    grad_qkv_own = grad_qkv_own.astype(f32) + swap(grad_qkv_other, "core").astype(f32)
    values = grad_qkv_own[:, :, 2 * HD :]
    values = jnp.concatenate([values[:, : rows // 2], values[:, rows // 2 :]], axis=2)
    joined = jnp.concatenate(
        [grad_project, grad_qkv_own[:, :, : 2 * HD].astype(bf16), values.astype(bf16)], axis=1
    )
    joined = lax.all_to_all(joined, CHIPS, 0, 0, tiled=True)

    bias_part = jnp.where(
        jnp.arange(H)[None, :] == head, bias_grad[0, :2][:, None], jnp.zeros((2, H), f32)
    )
    packed = jnp.concatenate(
        [
            attn_grad[:, 0] / attn_gain,
            grad_ffn[0],
            gain_grad[0],
            bias_part.reshape(-1),
            squares[:2, 0],
            jnp.sum(ffn_branch * ffn_branch)[None],
            jnp.zeros((93,), f32),
        ]
    )
    summed = sum_everywhere(packed.reshape(-1, 128))
    grad_down = down_grad.astype(f32)
    grad_expand = widen(expand_grad, depth, hidden_rows)
    joined, grad_down, grad_expand = lax.optimization_barrier((joined, grad_down, grad_expand))
    grad_inputs, grad_qkv = input_back(
        over_sharers(joined, sharers), qkv_full, inputs, attn_gain[None], grad_middle
    )
    summed = summed.reshape(-1)
    at = 2 * D + 2 * HD
    root_means = jnp.sqrt(summed[at + 2 * H : at + 2 * H + 3] / (tokens * D))
    return (
        outputs,
        grad_inputs,
        grad_qkv,
        grad_out,
        grad_expand,
        grad_down,
        summed[:D],
        summed[D : 2 * D],
        summed[2 * D : 2 * D + HD],
        summed[2 * D + HD : at],
        summed[at : at + 2 * H].reshape(2, H),
        root_means,
    )


def solution(mesh):
    grid = mesh.devices if mesh.axis_names == ("head", "blk") else mesh.devices.T
    heads, blks = grid.shape
    mesh = Mesh(grid.reshape(heads // 2, 2, blks // 2, 2), ("hx", "core", "bz", "by"))
    split = P(DEVICES, None)

    return jax.shard_map(
        body,
        mesh=mesh,
        in_specs=(split,) * 2 + (P(),) * 5 + (split,) * 4 + (P(),) * 3,
        out_specs=(split,) * 6 + (P(),) * 6,
        check_vma=False,
    )
```
